128 devices in a mesh: cfg: 2 (over z_lo), seq: 8 (over x, core), blk: 8 (over z_hi, y).
Axes of the slice: x: 4, y: 4, z: 4 (z_hi: 2, z_lo: 2; z = z_hi * 2 + z_lo), core: 2. Of those that a mesh axis runs over, the one named last changes fastest.
Arguments:
- hidden: bfloat16 [2, 3072, 5120], P('cfg', 'seq', 'blk'), may hold values from -2.5 to 2.5
- modulation: float32 [3, 5120], replicated, may hold values from -4 to 4
- in_projection: bfloat16 [5120, 3, 3072], P(('cfg', 'seq'), None, 'blk'), may hold values from -0.078125 to 0.078125
- out_projection: bfloat16 [3072, 5120], P('blk', ('cfg', 'seq')), may hold values from -0.15625 to 0.15625
- lengths: int32 [5], replicated, may hold values from 1 to 1536, 3072 in all
- positions: int32 [3, 3072], P(None, 'seq'), may hold values from 0 to 63
- guidance: float32 [1], replicated, may hold values from 2 to 5
Outputs:
- guided: float32 [8, 2, 192, 5120], P('seq', 'cfg', None, 'blk')
The draws below stay inside these ranges and needn't reach their ends.
Inputs may be any that keep to these rules, and one draw needn't show every extreme that they name: The clip lengths sum to 3072 and the longest is exactly 1536.
All inputs are finite; a program needn't handle non-finite values.
Results may differ from the reference program's by a relative error of at most 0.012.
The reference program's roundings to bfloat16 on the way count: a program that leaves them out, or rounds other values in their place, can miss the bound.
Values may be sent and summed in bfloat16 or wider, within the bound.
A program may use at most 128 MiB of HBM per device.

```python
import math
import jax
import jax.numpy as jnp
import numpy as np
from jax import lax

D = 5120
HEAD_DIM = 128
HEADS = 24
INNER = 3072
TOK_DEV = 384
TOKENS = 3072
CLIPS = 5
N_SEQ = 8


def draw_hidden(key, part):
    key_cols, key_rows, key_base = jax.random.split(key, 3)
    col_scale = jnp.exp(jax.random.uniform(key_cols, (1, 1, D), jnp.float32, math.log(0.25), math.log(2.5)))
    row_scale = jnp.exp(jax.random.uniform(key_rows, (2, TOKENS, 1), jnp.float32, math.log(0.3), math.log(1.0)))
    base = jnp.clip(jax.random.normal(key_base, (2, TOKENS, D), jnp.float32), -4.0, 4.0)
    return (0.25 * base * col_scale * row_scale).astype(jnp.bfloat16)


def set_ends(drawn, key, smallest, top_value):
    longest = drawn.shape.index(max(drawn.shape))
    spots = []
    for shift in (0, 1):
        where = [jax.random.randint(jax.random.fold_in(key, axis), (), 0, length) for axis, length in enumerate(drawn.shape)]
        where[longest] = (where[longest] + shift) % drawn.shape[longest]
        spots.append(tuple(where))
    return drawn.at[spots[0]].set(smallest).at[spots[1]].set(top_value)


def spiked(result, own_key, source, target, blocks, factor):
    def block_of(axis_at):
        return (jnp.arange(result.shape[axis_at]) // (result.shape[axis_at] // blocks)).reshape((-1,) + (1,) * (result.ndim - 1 - axis_at))

    first = jax.random.permutation(own_key, blocks)[block_of(target)]
    other_side = (block_of(target) + blocks // 2) % blocks
    return jnp.where((block_of(source) == first) | (block_of(source) == other_side), factor * result, result)


def levels(key, extent, shards, low, high):
    factor_of, own = 1.0, jax.random.fold_in(key, 6)
    for position, parts in shards:
        draws = jnp.exp(jax.random.uniform(jax.random.fold_in(own, position), (parts,), jnp.float32, low / len(shards), high / len(shards)))
        factor_of = factor_of * jnp.repeat(draws, extent[position] // parts).reshape([-1 if axis == position else 1 for axis in range(len(extent))])
    return factor_of


def split_up(count, total, most, slope):
    portions = [(1 << 20) // math.isqrt(standing ** slope) + 1 for standing in range(2, count + 1)]
    rest, counts = total - most - (count - 1), [1] * (count - 1)
    while rest > 0:
        free = [i for i in range(count - 1) if counts[i] < most]
        pool, remaining = sum([portions[i] for i in free]), rest
        for i in free:
            more = min(most - counts[i], max(1, remaining * portions[i] // pool), rest)
            counts[i] = counts[i] + more
            rest = rest - more
    return np.array([most] + counts)


def ragged(rng, number_of, total, most, lean):
    if number_of == 2:
        one = jax.random.randint(rng, (), max(1, total - most), min(most, total - 1) + 1)
        return jnp.stack([one, total - one])
    sizes = jnp.asarray(split_up(number_of, total, most, lean), jnp.int32)
    pairs = (number_of - 1) // 2
    giver, sink = sizes[1:1 + 2 * pairs:2], sizes[2:2 + 2 * pairs:2]
    slack = jnp.minimum(giver - 1, most - sink)
    passed = jax.random.randint(jax.random.fold_in(rng, 1), (pairs,), 0, 1 << 20) % (slack + 1)
    sizes = sizes.at[1:1 + 2 * pairs:2].set(giver - passed).at[2:2 + 2 * pairs:2].set(sink + passed)
    return sizes[jax.random.permutation(jax.random.fold_in(rng, 2), number_of)]


def bell_draw(stream_key, dims, scale, limit, pieces=(), kind=jnp.bfloat16):
    drawn = scale * jax.random.normal(stream_key, dims, jnp.float32)
    if pieces:
        drawn = drawn * levels(stream_key, dims, pieces, -0.22, 0.18)
    return jnp.clip(drawn, -limit, limit).astype(kind)


def heavy_noise(key, extent, width, bound, cuts, heavy, kind=jnp.bfloat16):
    entries = width * jax.random.normal(key, extent, jnp.float32)
    if cuts:
        entries = entries * levels(key, extent, cuts, -0.22, 0.18)
    return jnp.clip(spiked(entries, jax.random.fold_in(key, 3), *heavy), -bound, bound).astype(kind)


def setup_inputs(seed: int = 0) -> dict:
    key_of = jax.random.split(jax.random.key(seed), 8)
    hidden = draw_hidden(jax.random.fold_in(key_of[7], 71), 0)
    modulation = bell_draw(key_of[1], (3, D), 1.0, 4.0, (), jnp.float32)
    in_projection = bell_draw(key_of[2], (D, 3, INNER), D ** -0.5, 0.078125, ((0, 16), (2, 8)))
    out_projection = heavy_noise(key_of[3], (INNER, D), INNER ** -0.5, 0.15625, ((0, 8), (1, 16)), (0, 1, 16, 2.0))
    lengths = ragged(key_of[4], CLIPS, TOKENS, TOKENS // 2, 2).astype(jnp.int32)
    positions = set_ends(jax.random.randint(key_of[5], (3, TOKENS), 0, 64), jax.random.fold_in(key_of[5], 1), 0, 63).astype(jnp.int32)
    guidance = jnp.clip(jax.random.uniform(key_of[6], (1,), jnp.float32, 2.0, 5.0), 2.0, 5.0)
    return {"hidden": hidden, "modulation": modulation, "in_projection": in_projection, "out_projection": out_projection, "lengths": lengths, "positions": positions, "guidance": guidance}


def rotary_angles(head_width):
    third = head_width // 6
    first_dim = head_width - 4 * third
    other_dim = 2 * third
    pair_index = np.arange(head_width) // 2
    first_pairs = first_dim // 2
    other_pairs = other_dim // 2
    in_first = pair_index < first_pairs
    in_second = (pair_index >= first_pairs) & (pair_index < first_pairs + other_pairs)
    in_third = pair_index >= first_pairs + other_pairs
    row_first = np.where(in_first, 10000.0 ** (-2.0 * pair_index / first_dim), 0.0)
    row_second = np.where(in_second, 10000.0 ** (-2.0 * (pair_index - first_pairs) / other_dim), 0.0)
    row_third = np.where(in_third, 10000.0 ** (-2.0 * (pair_index - first_pairs - other_pairs) / other_dim), 0.0)
    return np.stack([row_first, row_second, row_third]).astype(np.float32)

def turn_matrix(head_width):
    row_index = np.arange(head_width)[:, None]
    col_index = np.arange(head_width)[None, :]
    upper = np.where((col_index == row_index + 1) & (row_index % 2 == 0), 1.0, 0.0)
    lower = np.where((col_index == row_index - 1) & (row_index % 2 == 1), -1.0, 0.0)
    return (upper + lower).astype(np.float32)

def layer_norm(inputs):
    row_mean = lax.optimization_barrier(jnp.mean(inputs, -1, keepdims=True))
    centered = inputs - row_mean
    variance = lax.optimization_barrier(jnp.mean(centered * centered, -1, keepdims=True))
    return centered * lax.rsqrt(variance + 1e-06)

def rms_norm(inputs):
    return inputs * lax.rsqrt(lax.optimization_barrier(jnp.mean(inputs * inputs, -1, keepdims=True)) + 1e-06)

def rotate(inputs, cosine, sine, turning):
    turned = jnp.einsum('thd,de->the', inputs, turning, precision=lax.Precision.HIGHEST)
    return inputs * cosine + turned * sine

def clip_index(clip_ends, first_row, count):
    token_index = first_row + jnp.arange(count, dtype=jnp.int32)
    return lax.optimization_barrier(jnp.sum((token_index[:, None] >= clip_ends[None, :]).astype(jnp.int32), 1))

def half_output(states, modulation, in_projection, out_projection, clip_ends, cosine, sine, turning):
    inputs = states.astype(jnp.float32)
    modulated = (layer_norm(inputs) * (1.0 + modulation[1]) + modulation[0]).astype(jnp.bfloat16)
    mixed = jnp.dot(modulated, in_projection.reshape(D, 3 * INNER), preferred_element_type=jnp.float32)
    mixed = mixed.reshape(TOKENS, 3, HEADS, HEAD_DIM)
    queries = rotate(rms_norm(mixed[:, 0]), cosine, sine, turning).astype(jnp.bfloat16)
    key_rows = rotate(rms_norm(mixed[:, 1]), cosine, sine, turning).astype(jnp.bfloat16)
    value_rows = mixed[:, 2].astype(jnp.bfloat16)
    token_clip = clip_index(clip_ends, 0, TOKENS)
    same_clip = token_clip[:, None] == token_clip[None, :]
    score_scale = HEAD_DIM ** (-0.5)

    def one_head(operands):
        query_head, key_head, value_head = operands
        scores = jnp.dot(query_head, key_head.T, preferred_element_type=jnp.float32) * score_scale
        weights = jnp.where(same_clip, jnp.exp(scores), 0.0)
        total = lax.optimization_barrier(jnp.sum(weights, -1, keepdims=True))
        numerator = jnp.dot(weights.astype(jnp.bfloat16), value_head, preferred_element_type=jnp.float32)
        return (numerator / total).astype(jnp.bfloat16)
    attended = lax.map(one_head, (queries.transpose(1, 0, 2), key_rows.transpose(1, 0, 2), value_rows.transpose(1, 0, 2)))
    attended = attended.transpose(1, 0, 2).reshape(TOKENS, INNER)
    projected = jnp.dot(attended, out_projection, preferred_element_type=jnp.float32)
    return inputs + modulation[2] * projected

def reference(hidden, modulation, in_projection, out_projection, lengths, positions, guidance):
    clip_ends = jnp.cumsum(lengths).astype(jnp.int32)
    angle_table = jnp.asarray(rotary_angles(HEAD_DIM))
    turning = jnp.asarray(turn_matrix(HEAD_DIM))
    angles = jnp.einsum('at,ae->te', positions.astype(jnp.float32), angle_table, precision=lax.Precision.HIGHEST)
    cosine = jnp.cos(angles)[:, None, :]
    sine = jnp.sin(angles)[:, None, :]
    cond_out = half_output(hidden[0], modulation, in_projection, out_projection, clip_ends, cosine, sine, turning)
    uncond_out = half_output(hidden[1], modulation, in_projection, out_projection, clip_ends, cosine, sine, turning)
    guided = uncond_out + guidance[0] * (cond_out - uncond_out)
    return guided.reshape(N_SEQ, 2, TOK_DEV // 2, D)
```

```python
import jax
import jax.numpy as jnp
import numpy as np
from jax import lax
from jax.sharding import Mesh, PartitionSpec as P

HEAD_DIM = 128
SEQ = ("x", "core")
BLK = ("zhi", "y")
SWAP = [(0, 1), (1, 0)]


def rotary_angles(head_width):
    third = head_width // 6
    first_dim = head_width - 4 * third
    other_dim = 2 * third
    pair_index = np.arange(head_width) // 2
    first_pairs = first_dim // 2
    other_pairs = other_dim // 2
    in_first = pair_index < first_pairs
    in_second = (pair_index >= first_pairs) & (pair_index < first_pairs + other_pairs)
    in_third = pair_index >= first_pairs + other_pairs
    row_first = np.where(in_first, 10000.0 ** (-2.0 * pair_index / first_dim), 0.0)
    row_second = np.where(
        in_second, 10000.0 ** (-2.0 * (pair_index - first_pairs) / other_dim), 0.0
    )
    row_third = np.where(
        in_third, 10000.0 ** (-2.0 * (pair_index - first_pairs - other_pairs) / other_dim), 0.0
    )
    return np.stack([row_first, row_second, row_third]).astype(np.float32)


def turn_matrix(head_width):
    row_index = np.arange(head_width)[:, None]
    col_index = np.arange(head_width)[None, :]
    upper = np.where((col_index == row_index + 1) & (row_index % 2 == 0), 1.0, 0.0)
    lower = np.where((col_index == row_index - 1) & (row_index % 2 == 1), -1.0, 0.0)
    return (upper + lower).astype(np.float32)


def layer_norm(inputs):
    row_mean = jnp.mean(inputs, -1, keepdims=True)
    centered = inputs - row_mean
    variance = jnp.mean(centered * centered, -1, keepdims=True)
    return centered * lax.rsqrt(variance + 1e-06)


def rms_norm(inputs):
    return inputs * lax.rsqrt(jnp.mean(inputs * inputs, -1, keepdims=True) + 1e-06)


def rotate(inputs, cosine, sine, turning):
    turned = jnp.einsum("thd,de->the", inputs, turning, precision=lax.Precision.HIGHEST)
    return inputs * cosine + turned * sine


def clip_of(clip_ends, token_index):
    return jnp.sum((token_index[:, None] >= clip_ends[None, :]).astype(jnp.int32), 1)


def local(hidden, modulation, in_projection, out_projection, lengths, positions, guidance):
    cfg = lax.axis_index("cfg")
    core = lax.axis_index("core")
    seq = lax.axis_index("x") * 2 + core
    states = hidden[0]
    tok_count = states.shape[0]
    half_rows = tok_count // 2
    n_blk = lax.axis_size(BLK)
    inner_width = in_projection.shape[2]
    head_count = inner_width // HEAD_DIM

    sent_rows = lax.dynamic_slice_in_dim(states, (1 - cfg) * half_rows, half_rows, 0)
    other_rows = lax.ppermute(sent_rows, "cfg", SWAP)
    mine_rows = lax.dynamic_slice_in_dim(states, cfg * half_rows, half_rows, 0)
    is_cond = cfg == 0
    cond_rows = jnp.where(is_cond, mine_rows, other_rows).astype(jnp.float32)
    uncond_rows = jnp.where(is_cond, other_rows, mine_rows).astype(jnp.float32)
    scale = guidance[0]
    hidden_part = uncond_rows + scale * (cond_rows - uncond_rows)

    full_states = lax.all_gather(states, BLK, axis=1, tiled=True)
    modulated = (
        layer_norm(full_states.astype(jnp.float32)) * (1.0 + modulation[1]) + modulation[0]
    ).astype(jnp.bfloat16)

    w_mine = lax.all_gather(in_projection, ("cfg", "x"), axis=0, tiled=True)
    w_other = lax.ppermute(w_mine, "core", SWAP)
    rows = in_projection.shape[0]
    n_pairs = w_mine.shape[0] // rows
    mod4 = modulated.reshape(tok_count, n_pairs, 2, rows)
    mod_mine = lax.dynamic_index_in_dim(mod4, core, axis=2, keepdims=False)
    mod_other = lax.dynamic_index_in_dim(mod4, 1 - core, axis=2, keepdims=False)
    mixed = jnp.einsum(
        "tjd,jdqe->tqe",
        mod_mine,
        w_mine.reshape(n_pairs, rows, 3, inner_width),
        preferred_element_type=jnp.float32,
    ) + jnp.einsum(
        "tjd,jdqe->tqe",
        mod_other,
        w_other.reshape(n_pairs, rows, 3, inner_width),
        preferred_element_type=jnp.float32,
    )
    mixed = mixed.reshape(tok_count, 3, head_count, HEAD_DIM)

    angle_table = jnp.asarray(rotary_angles(HEAD_DIM))
    turning = jnp.asarray(turn_matrix(HEAD_DIM))
    angles = jnp.einsum(
        "at,ae->te", positions.astype(jnp.float32), angle_table, precision=lax.Precision.HIGHEST
    )
    cosine = jnp.cos(angles)[:, None, :]
    sine = jnp.sin(angles)[:, None, :]
    queries = rotate(rms_norm(mixed[:, 0]), cosine, sine, turning).astype(jnp.bfloat16)
    key_rows = rotate(rms_norm(mixed[:, 1]), cosine, sine, turning).astype(jnp.bfloat16)
    value_rows = mixed[:, 2].astype(jnp.bfloat16)

    kv = jnp.stack([key_rows, value_rows], axis=1)
    kv_mine = lax.all_gather(kv, "x", axis=0, tiled=True)
    kv_other = lax.ppermute(kv_mine, "core", SWAP)
    kv_all = jnp.concatenate([kv_mine, kv_other], axis=0)
    key_piece = kv_all[:, 0]
    value_piece = kv_all[:, 1]
    row_count = key_piece.shape[0]
    n_x = kv_mine.shape[0] // tok_count

    clip_ends = jnp.cumsum(lengths)
    query_clip = clip_of(clip_ends, seq * tok_count + jnp.arange(tok_count, dtype=jnp.int32))
    key_row = jnp.arange(row_count, dtype=jnp.int32)
    key_block = key_row // tok_count
    key_core = jnp.where(key_block < n_x, core, 1 - core)
    key_token = ((key_block % n_x) * 2 + key_core) * tok_count + key_row % tok_count
    key_clip_all = clip_of(clip_ends, key_token)

    score_scale = HEAD_DIM ** (-0.5)
    start_state = (
        jnp.zeros((tok_count, head_count, HEAD_DIM), jnp.float32),
        jnp.zeros((head_count, tok_count), jnp.float32),
    )
    key_block_size = 512 if row_count % 512 == 0 else row_count

    def key_step(block_index, running):
        numerator, denominator = running
        key_slab = lax.dynamic_slice_in_dim(key_piece, block_index * key_block_size, key_block_size, 0)
        value_slab = lax.dynamic_slice_in_dim(value_piece, block_index * key_block_size, key_block_size, 0)
        key_clip = lax.dynamic_slice_in_dim(key_clip_all, block_index * key_block_size, key_block_size, 0)
        scores = (
            jnp.einsum("qhd,khd->hqk", queries, key_slab, preferred_element_type=jnp.float32)
            * score_scale
        )
        same_clip = query_clip[:, None] == key_clip[None, :]
        weights = jnp.where(same_clip[None], jnp.exp(scores), 0.0)
        numerator = numerator + jnp.einsum(
            "hqk,khd->qhd",
            weights.astype(jnp.bfloat16),
            value_slab,
            preferred_element_type=jnp.float32,
        )
        denominator = denominator + jnp.sum(weights, -1)
        return (numerator, denominator)

    numerator, denominator = lax.fori_loop(0, row_count // key_block_size, key_step, start_state)
    attended = (
        (numerator / jnp.transpose(denominator)[:, :, None])
        .astype(jnp.bfloat16)
        .reshape(tok_count, inner_width)
    )

    wo_mine = lax.all_gather(out_projection, ("cfg", "x"), axis=1, tiled=True)
    wo_other = lax.ppermute(wo_mine, "core", SWAP)
    cols = out_projection.shape[1]
    wo_mine = wo_mine.reshape(inner_width, n_blk, cols)
    wo_other = wo_other.reshape(inner_width, n_blk, cols)
    first_core = core == 0
    wo_full = jnp.stack(
        [jnp.where(first_core, wo_mine, wo_other), jnp.where(first_core, wo_other, wo_mine)], axis=2
    ).reshape(inner_width, n_blk, 2 * cols)

    weight = jnp.where(is_cond, scale, 1.0 - scale)
    gate = modulation[2].reshape(n_blk, 2 * cols) * weight
    partial = jnp.einsum(
        "rte,ebn->rbtn",
        attended.reshape(2, half_rows, inner_width),
        wo_full,
        preferred_element_type=jnp.float32,
    ) * gate[None, :, None, :]
    projected = lax.psum_scatter(
        partial.reshape(2 * n_blk, half_rows, 2 * cols),
        ("cfg",) + BLK,
        scatter_dimension=0,
        tiled=True,
    )
    guided = hidden_part + projected[0]
    return guided.reshape(1, 1, half_rows, 2 * cols)


def solution(mesh):
    devices = mesh.devices.reshape(2, 4, 2, 2, 4)
    own = Mesh(devices, ("cfg", "x", "core", "zhi", "y"))
    return jax.shard_map(
        local,
        mesh=own,
        in_specs=(
            P("cfg", SEQ, BLK),
            P(),
            P(("cfg",) + SEQ, None, BLK),
            P(BLK, ("cfg",) + SEQ),
            P(),
            P(None, SEQ),
            P(),
        ),
        out_specs=P(SEQ, "cfg", None, BLK),
        check_vma=False,
    )
```

```python
import jax
import jax.numpy as jnp
import numpy as np
from jax import lax
from jax.sharding import Mesh, PartitionSpec as P

HEAD_DIM = 128
SEQ = ("x", "core")
BLK = ("zhi", "y")
SWAP = [(0, 1), (1, 0)]


def rotary_angles(head_width):
    third = head_width // 6
    first_dim = head_width - 4 * third
    other_dim = 2 * third
    pair_index = np.arange(head_width) // 2
    first_pairs = first_dim // 2
    other_pairs = other_dim // 2
    in_first = pair_index < first_pairs
    in_second = (pair_index >= first_pairs) & (pair_index < first_pairs + other_pairs)
    in_third = pair_index >= first_pairs + other_pairs
    row_first = np.where(in_first, 10000.0 ** (-2.0 * pair_index / first_dim), 0.0)
    row_second = np.where(
        in_second, 10000.0 ** (-2.0 * (pair_index - first_pairs) / other_dim), 0.0
    )
    row_third = np.where(
        in_third, 10000.0 ** (-2.0 * (pair_index - first_pairs - other_pairs) / other_dim), 0.0
    )
    return np.stack([row_first, row_second, row_third]).astype(np.float32)


def turn_matrix(head_width):
    row_index = np.arange(head_width)[:, None]
    col_index = np.arange(head_width)[None, :]
    upper = np.where((col_index == row_index + 1) & (row_index % 2 == 0), 1.0, 0.0)
    lower = np.where((col_index == row_index - 1) & (row_index % 2 == 1), -1.0, 0.0)
    return (upper + lower).astype(np.float32)


def layer_norm(inputs):
    row_mean = jnp.mean(inputs, -1, keepdims=True)
    centered = inputs - row_mean
    variance = jnp.mean(centered * centered, -1, keepdims=True)
    return centered * lax.rsqrt(variance + 1e-06)


def rms_norm(inputs):
    return inputs * lax.rsqrt(jnp.mean(inputs * inputs, -1, keepdims=True) + 1e-06)


def rotate(inputs, cosine, sine, turning):
    turned = jnp.einsum("thd,de->the", inputs, turning, precision=lax.Precision.HIGHEST)
    return inputs * cosine + turned * sine


def clip_of(clip_ends, token_index):
    return jnp.sum((token_index[:, None] >= clip_ends[None, :]).astype(jnp.int32), 1)


def local(hidden, modulation, in_projection, out_projection, lengths, positions, guidance):
    cfg = lax.axis_index("cfg")
    core = lax.axis_index("core")
    seq = lax.axis_index("x") * 2 + core
    blk = lax.axis_index("zhi") * lax.axis_size("y") + lax.axis_index("y")
    states = hidden[0]
    tok_count = states.shape[0]
    feat_width = states.shape[1]
    half_rows = tok_count // 2
    n_blk = lax.axis_size(BLK)
    inner_width = in_projection.shape[2]
    head_count = inner_width // HEAD_DIM

    sent_rows = lax.dynamic_slice_in_dim(states, (1 - cfg) * half_rows, half_rows, 0)
    other_rows = lax.ppermute(sent_rows, "cfg", SWAP)
    mine_rows = lax.dynamic_slice_in_dim(states, cfg * half_rows, half_rows, 0)
    is_cond = cfg == 0
    cond_rows = jnp.where(is_cond, mine_rows, other_rows).astype(jnp.float32)
    uncond_rows = jnp.where(is_cond, other_rows, mine_rows).astype(jnp.float32)
    scale = guidance[0]
    hidden_part = uncond_rows + scale * (cond_rows - uncond_rows)

    spread = jnp.broadcast_to(states[None], (n_blk,) + states.shape)
    full_states = lax.all_to_all(spread, BLK, 0, 0, tiled=False)
    full_states, hidden_part = lax.optimization_barrier((full_states, hidden_part))
    inputs = full_states.astype(jnp.float32)
    row_mean = jnp.mean(inputs, (0, 2), keepdims=True)
    centered = inputs - row_mean
    variance = jnp.mean(centered * centered, (0, 2), keepdims=True)
    normed = centered * lax.rsqrt(variance + 1e-06)
    mod_shift = modulation[0].reshape(n_blk, 1, feat_width)
    mod_scale = modulation[1].reshape(n_blk, 1, feat_width)
    modulated = (normed * (1.0 + mod_scale) + mod_shift).astype(jnp.bfloat16)

    piece = lax.all_gather(in_projection, ("cfg",) + SEQ, axis=0, tiled=True)
    mixed = jnp.einsum(
        "itf,ifqe->tqe",
        modulated,
        piece.reshape(n_blk, feat_width, 3, inner_width),
        preferred_element_type=jnp.float32,
    )
    mixed = mixed.reshape(tok_count, 3, head_count, HEAD_DIM)

    angle_table = jnp.asarray(rotary_angles(HEAD_DIM))
    turning = jnp.asarray(turn_matrix(HEAD_DIM))
    angles = jnp.einsum(
        "at,ae->te", positions.astype(jnp.float32), angle_table, precision=lax.Precision.HIGHEST
    )
    cosine = jnp.cos(angles)[:, None, :]
    sine = jnp.sin(angles)[:, None, :]
    queries = rotate(rms_norm(mixed[:, 0]), cosine, sine, turning).astype(jnp.bfloat16)
    key_rows = rotate(rms_norm(mixed[:, 1]), cosine, sine, turning).astype(jnp.bfloat16)
    value_rows = mixed[:, 2].astype(jnp.bfloat16)

    kv = jnp.stack([key_rows, value_rows], axis=1)
    kv_mine = lax.all_gather(kv, "x", axis=0, tiled=True)
    kv_other = lax.ppermute(kv_mine, "core", SWAP)
    kv_all = jnp.concatenate([kv_mine, kv_other], axis=0)
    key_piece = kv_all[:, 0]
    value_piece = kv_all[:, 1]
    row_count = key_piece.shape[0]
    n_x = kv_mine.shape[0] // tok_count

    clip_ends = jnp.cumsum(lengths)
    query_clip = clip_of(clip_ends, seq * tok_count + jnp.arange(tok_count, dtype=jnp.int32))
    key_row = jnp.arange(row_count, dtype=jnp.int32)
    key_block = key_row // tok_count
    key_core = jnp.where(key_block < n_x, core, 1 - core)
    key_token = ((key_block % n_x) * 2 + key_core) * tok_count + key_row % tok_count
    key_clip_all = clip_of(clip_ends, key_token)

    score_scale = HEAD_DIM ** (-0.5)
    start_state = (
        jnp.zeros((tok_count, head_count, HEAD_DIM), jnp.float32),
        jnp.zeros((head_count, tok_count), jnp.float32),
    )
    key_block_size = 512 if row_count % 512 == 0 else row_count

    def key_step(block_index, running):
        numerator, denominator = running
        key_slab = lax.dynamic_slice_in_dim(key_piece, block_index * key_block_size, key_block_size, 0)
        value_slab = lax.dynamic_slice_in_dim(value_piece, block_index * key_block_size, key_block_size, 0)
        key_clip = lax.dynamic_slice_in_dim(key_clip_all, block_index * key_block_size, key_block_size, 0)
        scores = (
            jnp.einsum("qhd,khd->hqk", queries, key_slab, preferred_element_type=jnp.float32)
            * score_scale
        )
        same_clip = query_clip[:, None] == key_clip[None, :]
        weights = jnp.where(same_clip[None], jnp.exp(scores), 0.0)
        numerator = numerator + jnp.einsum(
            "hqk,khd->qhd",
            weights.astype(jnp.bfloat16),
            value_slab,
            preferred_element_type=jnp.float32,
        )
        denominator = denominator + jnp.sum(weights, -1)
        return (numerator, denominator)

    numerator, denominator = lax.fori_loop(0, row_count // key_block_size, key_step, start_state)
    attended = (
        (numerator / jnp.transpose(denominator)[:, :, None])
        .astype(jnp.bfloat16)
        .reshape(tok_count, inner_width)
    )

    out_piece = lax.all_gather(out_projection, ("cfg",) + SEQ, axis=1, tiled=True)
    partial = jnp.einsum(
        "rte,ebn->rbtn",
        attended.reshape(2, half_rows, inner_width),
        out_piece.reshape(inner_width, n_blk, feat_width),
        preferred_element_type=jnp.float32,
    ).astype(jnp.bfloat16)
    arrived = lax.all_to_all(
        partial.reshape(2 * n_blk, half_rows, feat_width), ("cfg",) + BLK, 0, 0, tiled=False
    ).astype(jnp.float32)
    cond_sum = jnp.sum(arrived[:n_blk], 0)
    uncond_sum = jnp.sum(arrived[n_blk:], 0)
    gate = lax.dynamic_slice_in_dim(modulation[2], blk * feat_width, feat_width, 0)
    projected = gate * (uncond_sum + scale * (cond_sum - uncond_sum))
    guided = hidden_part + projected
    return guided.reshape(1, 1, half_rows, feat_width)


def solution(mesh):
    devices = mesh.devices.reshape(2, 4, 2, 2, 4)
    own = Mesh(devices, ("cfg", "x", "core", "zhi", "y"))
    return jax.shard_map(
        local,
        mesh=own,
        in_specs=(
            P("cfg", SEQ, BLK),
            P(),
            P(("cfg",) + SEQ, None, BLK),
            P(BLK, ("cfg",) + SEQ),
            P(),
            P(None, SEQ),
            P(),
        ),
        out_specs=P(SEQ, "cfg", None, BLK),
        check_vma=False,
    )
```

```python
import jax
import jax.numpy as jnp
import numpy as np
from jax import lax
from jax.experimental.layout import Layout, with_layout_constraint
from jax.sharding import Mesh, PartitionSpec as P

HEAD_DIM = 128
SEQ = ("x", "core")
BLK = ("zhi", "y")
SWAP = [(0, 1), (1, 0)]


def rotary_angles(head_width):
    third = head_width // 6
    first_dim = head_width - 4 * third
    other_dim = 2 * third
    pair_index = np.arange(head_width) // 2
    first_pairs = first_dim // 2
    other_pairs = other_dim // 2
    in_first = pair_index < first_pairs
    in_second = (pair_index >= first_pairs) & (pair_index < first_pairs + other_pairs)
    in_third = pair_index >= first_pairs + other_pairs
    row_first = np.where(in_first, 10000.0 ** (-2.0 * pair_index / first_dim), 0.0)
    row_second = np.where(
        in_second, 10000.0 ** (-2.0 * (pair_index - first_pairs) / other_dim), 0.0
    )
    row_third = np.where(
        in_third, 10000.0 ** (-2.0 * (pair_index - first_pairs - other_pairs) / other_dim), 0.0
    )
    return np.stack([row_first, row_second, row_third]).astype(np.float32)


def turn_matrix(head_width):
    row_index = np.arange(head_width)[:, None]
    col_index = np.arange(head_width)[None, :]
    upper = np.where((col_index == row_index + 1) & (row_index % 2 == 0), 1.0, 0.0)
    lower = np.where((col_index == row_index - 1) & (row_index % 2 == 1), -1.0, 0.0)
    return (upper + lower).astype(np.float32)


def layer_norm(inputs):
    row_mean = jnp.mean(inputs, -1, keepdims=True)
    centered = inputs - row_mean
    variance = jnp.mean(centered * centered, -1, keepdims=True)
    return centered * lax.rsqrt(variance + 1e-06)


def rms_norm(inputs):
    return inputs * lax.rsqrt(jnp.mean(inputs * inputs, -1, keepdims=True) + 1e-06)


def rotate(inputs, cosine, sine, turning):
    turned = jnp.einsum("thd,de->the", inputs, turning, precision=lax.Precision.HIGHEST)
    return inputs * cosine + turned * sine


def clip_of(clip_ends, token_index):
    return jnp.sum((token_index[:, None] >= clip_ends[None, :]).astype(jnp.int32), 1)


def local(hidden, modulation, in_projection, out_projection, lengths, positions, guidance):
    cfg = lax.axis_index("cfg")
    core = lax.axis_index("core")
    seq = lax.axis_index("x") * 2 + core
    blk = lax.axis_index("zhi") * lax.axis_size("y") + lax.axis_index("y")
    states = hidden[0]
    tok_count = states.shape[0]
    feat_width = states.shape[1]
    half_rows = tok_count // 2
    n_blk = lax.axis_size(BLK)
    inner_width = in_projection.shape[2]
    head_count = inner_width // HEAD_DIM

    sent_rows = lax.dynamic_slice_in_dim(states, (1 - cfg) * half_rows, half_rows, 0)
    other_rows = lax.ppermute(sent_rows, "cfg", SWAP)
    mine_rows = lax.dynamic_slice_in_dim(states, cfg * half_rows, half_rows, 0)
    is_cond = cfg == 0
    cond_rows = jnp.where(is_cond, mine_rows, other_rows).astype(jnp.float32)
    uncond_rows = jnp.where(is_cond, other_rows, mine_rows).astype(jnp.float32)
    scale = guidance[0]
    hidden_part = uncond_rows + scale * (cond_rows - uncond_rows)

    spread = jnp.broadcast_to(states[None], (n_blk,) + states.shape)
    full_states = lax.all_to_all(spread, BLK, 0, 0, tiled=False)
    full_states, hidden_part = lax.optimization_barrier((full_states, hidden_part))
    inputs = full_states.astype(jnp.float32)
    row_mean = jnp.mean(inputs, (0, 2), keepdims=True)
    centered = inputs - row_mean
    variance = jnp.mean(centered * centered, (0, 2), keepdims=True)
    normed = centered * lax.rsqrt(variance + 1e-06)
    mod_shift = modulation[0].reshape(n_blk, 1, feat_width)
    mod_scale = modulation[1].reshape(n_blk, 1, feat_width)
    modulated = (normed * (1.0 + mod_scale) + mod_shift).astype(jnp.bfloat16)

    piece = lax.all_gather(in_projection, ("cfg",) + SEQ, axis=0, tiled=True)
    mixed = jnp.einsum(
        "itf,ifqe->tqe",
        modulated,
        piece.reshape(n_blk, feat_width, 3, inner_width),
        preferred_element_type=jnp.float32,
    )
    mixed = with_layout_constraint(mixed, Layout((0, 1, 2)))
    mixed = mixed.reshape(tok_count, 3, head_count, HEAD_DIM)

    angle_table = jnp.asarray(rotary_angles(HEAD_DIM))
    turning = jnp.asarray(turn_matrix(HEAD_DIM))
    angles = jnp.einsum(
        "at,ae->te", positions.astype(jnp.float32), angle_table, precision=lax.Precision.HIGHEST
    )
    cosine = jnp.cos(angles)[:, None, :]
    sine = jnp.sin(angles)[:, None, :]
    queries = rotate(rms_norm(mixed[:, 0]), cosine, sine, turning).astype(jnp.bfloat16)
    key_rows = rotate(rms_norm(mixed[:, 1]), cosine, sine, turning).astype(jnp.bfloat16)
    value_rows = mixed[:, 2].astype(jnp.bfloat16)

    kv = jnp.stack([key_rows, value_rows], axis=1)
    kv_mine = lax.all_gather(kv, "x", axis=0, tiled=True)
    kv_other = lax.ppermute(kv_mine, "core", SWAP)
    kv_all = jnp.concatenate([kv_mine, kv_other], axis=0)
    key_piece = kv_all[:, 0]
    value_piece = kv_all[:, 1]
    row_count = key_piece.shape[0]
    n_x = kv_mine.shape[0] // tok_count

    clip_ends = jnp.cumsum(lengths)
    query_clip = clip_of(clip_ends, seq * tok_count + jnp.arange(tok_count, dtype=jnp.int32))
    key_row = jnp.arange(row_count, dtype=jnp.int32)
    key_block = key_row // tok_count
    key_core = jnp.where(key_block < n_x, core, 1 - core)
    key_token = ((key_block % n_x) * 2 + key_core) * tok_count + key_row % tok_count
    key_clip_all = clip_of(clip_ends, key_token)

    score_scale = HEAD_DIM ** (-0.5)
    start_state = (
        jnp.zeros((tok_count, head_count, HEAD_DIM), jnp.float32),
        jnp.zeros((head_count, tok_count), jnp.float32),
    )
    key_block_size = 512 if row_count % 512 == 0 else row_count

    def key_step(block_index, running):
        numerator, denominator = running
        key_slab = lax.dynamic_slice_in_dim(key_piece, block_index * key_block_size, key_block_size, 0)
        value_slab = lax.dynamic_slice_in_dim(value_piece, block_index * key_block_size, key_block_size, 0)
        key_clip = lax.dynamic_slice_in_dim(key_clip_all, block_index * key_block_size, key_block_size, 0)
        scores = (
            jnp.einsum("qhd,khd->hqk", queries, key_slab, preferred_element_type=jnp.float32)
            * score_scale
        )
        same_clip = query_clip[:, None] == key_clip[None, :]
        weights = jnp.where(same_clip[None], jnp.exp(scores), 0.0)
        numerator = numerator + jnp.einsum(
            "hqk,khd->qhd",
            weights.astype(jnp.bfloat16),
            value_slab,
            preferred_element_type=jnp.float32,
        )
        denominator = denominator + jnp.sum(weights, -1)
        return (numerator, denominator)

    numerator, denominator = lax.fori_loop(0, row_count // key_block_size, key_step, start_state)
    attended = (
        (numerator / jnp.transpose(denominator)[:, :, None])
        .astype(jnp.bfloat16)
        .reshape(tok_count, inner_width)
    )

    sent_att = lax.dynamic_slice_in_dim(attended, (1 - cfg) * half_rows, half_rows, 0)
    other_att = lax.ppermute(sent_att, "cfg", SWAP)
    mine_att = lax.dynamic_slice_in_dim(attended, cfg * half_rows, half_rows, 0)
    cond_att = jnp.where(is_cond, mine_att, other_att)
    uncond_att = jnp.where(is_cond, other_att, mine_att)
    out_piece = lax.all_gather(out_projection, ("cfg",) + SEQ, axis=1, tiled=True).reshape(
        inner_width, n_blk, feat_width
    )
    cond_part = jnp.einsum("te,ebn->btn", cond_att, out_piece, preferred_element_type=jnp.float32)
    uncond_part = jnp.einsum("te,ebn->btn", uncond_att, out_piece, preferred_element_type=jnp.float32)
    partial = (uncond_part + scale * (cond_part - uncond_part)).astype(jnp.bfloat16)
    arrived = lax.all_to_all(partial, BLK, 0, 0, tiled=False).astype(jnp.float32)
    gate = lax.dynamic_slice_in_dim(modulation[2], blk * feat_width, feat_width, 0)
    projected = gate * jnp.sum(arrived, 0)
    guided = hidden_part + projected
    return guided.reshape(1, 1, half_rows, feat_width)


def solution(mesh):
    devices = mesh.devices.reshape(2, 4, 2, 2, 4)
    own = Mesh(devices, ("cfg", "x", "core", "zhi", "y"))
    return jax.shard_map(
        local,
        mesh=own,
        in_specs=(
            P("cfg", SEQ, BLK),
            P(),
            P(("cfg",) + SEQ, None, BLK),
            P(BLK, ("cfg",) + SEQ),
            P(),
            P(None, SEQ),
            P(),
        ),
        out_specs=P(SEQ, "cfg", None, BLK),
        check_vma=False,
    )
```

```python
import jax
import jax.numpy as jnp
import numpy as np
from jax import lax
from jax.experimental.layout import Layout, with_layout_constraint
from jax.sharding import Mesh, PartitionSpec as P

HEAD_DIM = 128
SEQ = ("x", "core")
BLK = ("zhi", "y")
SWAP = [(0, 1), (1, 0)]


def rotary_angles(head_width):
    third = head_width // 6
    first_dim = head_width - 4 * third
    other_dim = 2 * third
    pair_index = np.arange(head_width) // 2
    first_pairs = first_dim // 2
    other_pairs = other_dim // 2
    in_first = pair_index < first_pairs
    in_second = (pair_index >= first_pairs) & (pair_index < first_pairs + other_pairs)
    in_third = pair_index >= first_pairs + other_pairs
    row_first = np.where(in_first, 10000.0 ** (-2.0 * pair_index / first_dim), 0.0)
    row_second = np.where(
        in_second, 10000.0 ** (-2.0 * (pair_index - first_pairs) / other_dim), 0.0
    )
    row_third = np.where(
        in_third, 10000.0 ** (-2.0 * (pair_index - first_pairs - other_pairs) / other_dim), 0.0
    )
    return np.stack([row_first, row_second, row_third]).astype(np.float32)


def turn_matrix(head_width):
    row_index = np.arange(head_width)[:, None]
    col_index = np.arange(head_width)[None, :]
    upper = np.where((col_index == row_index + 1) & (row_index % 2 == 0), 1.0, 0.0)
    lower = np.where((col_index == row_index - 1) & (row_index % 2 == 1), -1.0, 0.0)
    return (upper + lower).astype(np.float32)


def layer_norm(inputs):
    row_mean = jnp.mean(inputs, -1, keepdims=True)
    centered = inputs - row_mean
    variance = jnp.mean(centered * centered, -1, keepdims=True)
    return centered * lax.rsqrt(variance + 1e-06)


def rms_norm(inputs):
    return inputs * lax.rsqrt(jnp.mean(inputs * inputs, -1, keepdims=True) + 1e-06)


def rotate(inputs, cosine, sine, turning):
    turned = jnp.einsum("thd,de->the", inputs, turning, precision=lax.Precision.HIGHEST)
    return inputs * cosine + turned * sine


def clip_of(clip_ends, token_index):
    return jnp.sum((token_index[:, None] >= clip_ends[None, :]).astype(jnp.int32), 1)


def local(hidden, modulation, in_projection, out_projection, lengths, positions, guidance):
    cfg = lax.axis_index("cfg")
    core = lax.axis_index("core")
    seq = lax.axis_index("x") * 2 + core
    blk = lax.axis_index("zhi") * lax.axis_size("y") + lax.axis_index("y")
    states = hidden[0]
    tok_count = states.shape[0]
    feat_width = states.shape[1]
    half_rows = tok_count // 2
    n_blk = lax.axis_size(BLK)
    inner_width = in_projection.shape[2]
    head_count = inner_width // HEAD_DIM

    sent_rows = lax.dynamic_slice_in_dim(states, (1 - cfg) * half_rows, half_rows, 0)
    other_rows = lax.ppermute(sent_rows, "cfg", SWAP)
    mine_rows = lax.dynamic_slice_in_dim(states, cfg * half_rows, half_rows, 0)
    is_cond = cfg == 0
    cond_rows = jnp.where(is_cond, mine_rows, other_rows).astype(jnp.float32)
    uncond_rows = jnp.where(is_cond, other_rows, mine_rows).astype(jnp.float32)
    scale = guidance[0]
    hidden_part = uncond_rows + scale * (cond_rows - uncond_rows)

    spread = jnp.broadcast_to(states[None], (n_blk,) + states.shape)
    full_states = lax.all_to_all(spread, BLK, 0, 0, tiled=False)
    full_states, hidden_part = lax.optimization_barrier((full_states, hidden_part))
    inputs = full_states.astype(jnp.float32)
    row_mean = jnp.mean(inputs, (0, 2), keepdims=True)
    centered = inputs - row_mean
    variance = jnp.mean(centered * centered, (0, 2), keepdims=True)
    normed = centered * lax.rsqrt(variance + 1e-06)
    mod_shift = modulation[0].reshape(n_blk, 1, feat_width)
    mod_scale = modulation[1].reshape(n_blk, 1, feat_width)
    modulated = (normed * (1.0 + mod_scale) + mod_shift).astype(jnp.bfloat16)

    shard_other = lax.ppermute(in_projection, "cfg", SWAP)
    stacked = jnp.stack(
        [
            jnp.where(is_cond, in_projection, shard_other),
            jnp.where(is_cond, shard_other, in_projection),
        ]
    )
    piece = lax.all_gather(stacked, SEQ, axis=0, tiled=False)
    n_seq = piece.shape[0]
    rows = in_projection.shape[0]
    per_blk = feat_width // rows
    mod_perm = modulated.reshape(2, n_blk // 2, tok_count, per_blk, rows).transpose(2, 1, 3, 0, 4)
    mod_perm = mod_perm.reshape(tok_count, n_seq, 2, rows)
    mixed = jnp.einsum(
        "tabi,abiqe->tqe",
        mod_perm,
        piece,
        preferred_element_type=jnp.float32,
    )
    mixed = with_layout_constraint(mixed, Layout((0, 1, 2)))
    mixed = mixed.reshape(tok_count, 3, head_count, HEAD_DIM)

    angle_table = jnp.asarray(rotary_angles(HEAD_DIM))
    turning = jnp.asarray(turn_matrix(HEAD_DIM))
    angles = jnp.einsum(
        "at,ae->te", positions.astype(jnp.float32), angle_table, precision=lax.Precision.HIGHEST
    )
    cosine = jnp.cos(angles)[:, None, :]
    sine = jnp.sin(angles)[:, None, :]
    queries = rotate(rms_norm(mixed[:, 0]), cosine, sine, turning).astype(jnp.bfloat16)
    key_rows = rotate(rms_norm(mixed[:, 1]), cosine, sine, turning).astype(jnp.bfloat16)
    value_rows = mixed[:, 2].astype(jnp.bfloat16)

    kv = jnp.stack([key_rows, value_rows], axis=1)
    kv_mine = lax.all_gather(kv, "x", axis=0, tiled=True)
    kv_other = lax.ppermute(kv_mine, "core", SWAP)
    kv_all = jnp.concatenate([kv_mine, kv_other], axis=0)
    key_piece = kv_all[:, 0]
    value_piece = kv_all[:, 1]
    row_count = key_piece.shape[0]
    n_x = kv_mine.shape[0] // tok_count

    clip_ends = jnp.cumsum(lengths)
    query_clip = clip_of(clip_ends, seq * tok_count + jnp.arange(tok_count, dtype=jnp.int32))
    key_row = jnp.arange(row_count, dtype=jnp.int32)
    key_block = key_row // tok_count
    key_core = jnp.where(key_block < n_x, core, 1 - core)
    key_token = ((key_block % n_x) * 2 + key_core) * tok_count + key_row % tok_count
    key_clip_all = clip_of(clip_ends, key_token)

    score_scale = HEAD_DIM ** (-0.5)
    start_state = (
        jnp.zeros((tok_count, head_count, HEAD_DIM), jnp.float32),
        jnp.zeros((head_count, tok_count), jnp.float32),
    )
    key_block_size = 512 if row_count % 512 == 0 else row_count

    def key_step(block_index, running):
        numerator, denominator = running
        key_slab = lax.dynamic_slice_in_dim(key_piece, block_index * key_block_size, key_block_size, 0)
        value_slab = lax.dynamic_slice_in_dim(value_piece, block_index * key_block_size, key_block_size, 0)
        key_clip = lax.dynamic_slice_in_dim(key_clip_all, block_index * key_block_size, key_block_size, 0)
        scores = (
            jnp.einsum("qhd,khd->hqk", queries, key_slab, preferred_element_type=jnp.float32)
            * score_scale
        )
        same_clip = query_clip[:, None] == key_clip[None, :]
        weights = jnp.where(same_clip[None], jnp.exp(scores), 0.0)
        numerator = numerator + jnp.einsum(
            "hqk,khd->qhd",
            weights.astype(jnp.bfloat16),
            value_slab,
            preferred_element_type=jnp.float32,
        )
        denominator = denominator + jnp.sum(weights, -1)
        return (numerator, denominator)

    numerator, denominator = lax.fori_loop(0, row_count // key_block_size, key_step, start_state)
    attended = (
        (numerator / jnp.transpose(denominator)[:, :, None])
        .astype(jnp.bfloat16)
        .reshape(tok_count, inner_width)
    )

    sent_att = lax.dynamic_slice_in_dim(attended, (1 - cfg) * half_rows, half_rows, 0)
    other_att = lax.ppermute(sent_att, "cfg", SWAP)
    mine_att = lax.dynamic_slice_in_dim(attended, cfg * half_rows, half_rows, 0)
    cond_att = jnp.where(is_cond, mine_att, other_att)
    uncond_att = jnp.where(is_cond, other_att, mine_att)
    out_piece = lax.all_gather(out_projection, ("cfg",) + SEQ, axis=1, tiled=True).reshape(
        inner_width, n_blk, feat_width
    )
    cond_part = jnp.einsum("te,ebn->btn", cond_att, out_piece, preferred_element_type=jnp.float32)
    uncond_part = jnp.einsum("te,ebn->btn", uncond_att, out_piece, preferred_element_type=jnp.float32)
    partial = (uncond_part + scale * (cond_part - uncond_part)).astype(jnp.bfloat16)
    arrived = lax.all_to_all(partial, BLK, 0, 0, tiled=False).astype(jnp.float32)
    gate = lax.dynamic_slice_in_dim(modulation[2], blk * feat_width, feat_width, 0)
    projected = gate * jnp.sum(arrived, 0)
    guided = hidden_part + projected
    return guided.reshape(1, 1, half_rows, feat_width)


def solution(mesh):
    devices = mesh.devices.reshape(2, 4, 2, 2, 4)
    own = Mesh(devices, ("cfg", "x", "core", "zhi", "y"))
    return jax.shard_map(
        local,
        mesh=own,
        in_specs=(
            P("cfg", SEQ, BLK),
            P(),
            P(("cfg",) + SEQ, None, BLK),
            P(BLK, ("cfg",) + SEQ),
            P(),
            P(None, SEQ),
            P(),
        ),
        out_specs=P(SEQ, "cfg", None, BLK),
        check_vma=False,
    )
```

```python
import jax
import jax.numpy as jnp
import numpy as np
from jax import lax
from jax.experimental.layout import Layout, with_layout_constraint
from jax.sharding import Mesh, PartitionSpec as P

HEAD_DIM = 128
SEQ = ("x", "core")
BLK = ("zhi", "y")
SWAP = [(0, 1), (1, 0)]


def rotary_angles(head_width):
    third = head_width // 6
    first_dim = head_width - 4 * third
    other_dim = 2 * third
    pair_index = np.arange(head_width) // 2
    first_pairs = first_dim // 2
    other_pairs = other_dim // 2
    in_first = pair_index < first_pairs
    in_second = (pair_index >= first_pairs) & (pair_index < first_pairs + other_pairs)
    in_third = pair_index >= first_pairs + other_pairs
    row_first = np.where(in_first, 10000.0 ** (-2.0 * pair_index / first_dim), 0.0)
    row_second = np.where(
        in_second, 10000.0 ** (-2.0 * (pair_index - first_pairs) / other_dim), 0.0
    )
    row_third = np.where(
        in_third, 10000.0 ** (-2.0 * (pair_index - first_pairs - other_pairs) / other_dim), 0.0
    )
    return np.stack([row_first, row_second, row_third]).astype(np.float32)


def turn_matrix(head_width):
    row_index = np.arange(head_width)[:, None]
    col_index = np.arange(head_width)[None, :]
    upper = np.where((col_index == row_index + 1) & (row_index % 2 == 0), 1.0, 0.0)
    lower = np.where((col_index == row_index - 1) & (row_index % 2 == 1), -1.0, 0.0)
    return (upper + lower).astype(np.float32)


def layer_norm(inputs):
    row_mean = jnp.mean(inputs, -1, keepdims=True)
    centered = inputs - row_mean
    variance = jnp.mean(centered * centered, -1, keepdims=True)
    return centered * lax.rsqrt(variance + 1e-06)


def rms_norm(inputs):
    return inputs * lax.rsqrt(jnp.mean(inputs * inputs, -1, keepdims=True) + 1e-06)


def rotate(inputs, cosine, sine, turning):
    turned = jnp.einsum("thd,de->the", inputs, turning, precision=lax.Precision.HIGHEST)
    return inputs * cosine + turned * sine


def clip_of(clip_ends, token_index):
    return jnp.sum((token_index[:, None] >= clip_ends[None, :]).astype(jnp.int32), 1)


def local(hidden, modulation, in_projection, out_projection, lengths, positions, guidance):
    cfg = lax.axis_index("cfg")
    core = lax.axis_index("core")
    seq = lax.axis_index("x") * 2 + core
    blk = lax.axis_index("zhi") * lax.axis_size("y") + lax.axis_index("y")
    states = hidden[0]
    tok_count = states.shape[0]
    feat_width = states.shape[1]
    half_rows = tok_count // 2
    n_blk = lax.axis_size(BLK)
    inner_width = in_projection.shape[2]
    head_count = inner_width // HEAD_DIM

    sent_rows = lax.dynamic_slice_in_dim(states, (1 - cfg) * half_rows, half_rows, 0)
    other_rows = lax.ppermute(sent_rows, "cfg", SWAP)
    mine_rows = lax.dynamic_slice_in_dim(states, cfg * half_rows, half_rows, 0)
    is_cond = cfg == 0
    cond_rows = jnp.where(is_cond, mine_rows, other_rows).astype(jnp.float32)
    uncond_rows = jnp.where(is_cond, other_rows, mine_rows).astype(jnp.float32)
    scale = guidance[0]
    hidden_part = uncond_rows + scale * (cond_rows - uncond_rows)

    spread = jnp.broadcast_to(states[None], (n_blk,) + states.shape)
    full_states = lax.all_to_all(spread, BLK, 0, 0, tiled=False)
    full_states, hidden_part = lax.optimization_barrier((full_states, hidden_part))
    inputs = full_states.astype(jnp.float32)
    row_mean = jnp.mean(inputs, (0, 2), keepdims=True)
    centered = inputs - row_mean
    variance = jnp.mean(centered * centered, (0, 2), keepdims=True)
    normed = centered * lax.rsqrt(variance + 1e-06)
    mod_shift = modulation[0].reshape(n_blk, 1, feat_width)
    mod_scale = modulation[1].reshape(n_blk, 1, feat_width)
    modulated = (normed * (1.0 + mod_scale) + mod_shift).astype(jnp.bfloat16)

    piece_own = lax.all_gather(in_projection, SEQ, axis=0, tiled=False)
    shard_other = lax.ppermute(in_projection, "cfg", SWAP)
    piece_other = lax.all_gather(shard_other, SEQ, axis=0, tiled=False)
    n_seq = piece_own.shape[0]
    rows = in_projection.shape[0]
    per_blk = feat_width // rows
    mod_perm = modulated.reshape(2, n_blk // 2, tok_count, per_blk, rows).transpose(0, 2, 1, 3, 4)
    mod_perm = mod_perm.reshape(2, tok_count, n_seq, rows)
    mod_own = lax.dynamic_index_in_dim(mod_perm, cfg, axis=0, keepdims=False)
    mod_other = lax.dynamic_index_in_dim(mod_perm, 1 - cfg, axis=0, keepdims=False)
    mixed = jnp.einsum(
        "tai,aiqe->tqe", mod_own, piece_own, preferred_element_type=jnp.float32
    ) + jnp.einsum("tai,aiqe->tqe", mod_other, piece_other, preferred_element_type=jnp.float32)
    mixed = with_layout_constraint(mixed, Layout((0, 1, 2)))
    mixed = mixed.reshape(tok_count, 3, head_count, HEAD_DIM)

    angle_table = jnp.asarray(rotary_angles(HEAD_DIM))
    turning = jnp.asarray(turn_matrix(HEAD_DIM))
    angles = jnp.einsum(
        "at,ae->te", positions.astype(jnp.float32), angle_table, precision=lax.Precision.HIGHEST
    )
    cosine = jnp.cos(angles)[:, None, :]
    sine = jnp.sin(angles)[:, None, :]
    queries = rotate(rms_norm(mixed[:, 0]), cosine, sine, turning).astype(jnp.bfloat16)
    key_rows = rotate(rms_norm(mixed[:, 1]), cosine, sine, turning).astype(jnp.bfloat16)
    value_rows = mixed[:, 2].astype(jnp.bfloat16)

    kv = jnp.stack([key_rows, value_rows], axis=1)
    kv_mine = lax.all_gather(kv, "x", axis=0, tiled=True)
    kv_other = lax.ppermute(kv_mine, "core", SWAP)
    kv_all = jnp.concatenate([kv_mine, kv_other], axis=0)
    key_piece = kv_all[:, 0]
    value_piece = kv_all[:, 1]
    row_count = key_piece.shape[0]
    n_x = kv_mine.shape[0] // tok_count

    clip_ends = jnp.cumsum(lengths)
    query_clip = clip_of(clip_ends, seq * tok_count + jnp.arange(tok_count, dtype=jnp.int32))
    key_row = jnp.arange(row_count, dtype=jnp.int32)
    key_block = key_row // tok_count
    key_core = jnp.where(key_block < n_x, core, 1 - core)
    key_token = ((key_block % n_x) * 2 + key_core) * tok_count + key_row % tok_count
    key_clip_all = clip_of(clip_ends, key_token)

    score_scale = HEAD_DIM ** (-0.5)
    start_state = (
        jnp.zeros((tok_count, head_count, HEAD_DIM), jnp.float32),
        jnp.zeros((head_count, tok_count), jnp.float32),
    )
    key_block_size = 512 if row_count % 512 == 0 else row_count

    def key_step(block_index, running):
        numerator, denominator = running
        key_slab = lax.dynamic_slice_in_dim(key_piece, block_index * key_block_size, key_block_size, 0)
        value_slab = lax.dynamic_slice_in_dim(value_piece, block_index * key_block_size, key_block_size, 0)
        key_clip = lax.dynamic_slice_in_dim(key_clip_all, block_index * key_block_size, key_block_size, 0)
        scores = (
            jnp.einsum("qhd,khd->hqk", queries, key_slab, preferred_element_type=jnp.float32)
            * score_scale
        )
        same_clip = query_clip[:, None] == key_clip[None, :]
        weights = jnp.where(same_clip[None], jnp.exp(scores), 0.0)
        numerator = numerator + jnp.einsum(
            "hqk,khd->qhd",
            weights.astype(jnp.bfloat16),
            value_slab,
            preferred_element_type=jnp.float32,
        )
        denominator = denominator + jnp.sum(weights, -1)
        return (numerator, denominator)

    numerator, denominator = lax.fori_loop(0, row_count // key_block_size, key_step, start_state)
    attended = (
        (numerator / jnp.transpose(denominator)[:, :, None])
        .astype(jnp.bfloat16)
        .reshape(tok_count, inner_width)
    )

    sent_att = lax.dynamic_slice_in_dim(attended, (1 - cfg) * half_rows, half_rows, 0)
    other_att = lax.ppermute(sent_att, "cfg", SWAP)
    mine_att = lax.dynamic_slice_in_dim(attended, cfg * half_rows, half_rows, 0)
    cond_att = jnp.where(is_cond, mine_att, other_att)
    uncond_att = jnp.where(is_cond, other_att, mine_att)
    out_piece = lax.all_gather(out_projection, ("cfg",) + SEQ, axis=1, tiled=True).reshape(
        inner_width, n_blk, feat_width
    )
    cond_part = jnp.einsum("te,ebn->btn", cond_att, out_piece, preferred_element_type=jnp.float32)
    uncond_part = jnp.einsum("te,ebn->btn", uncond_att, out_piece, preferred_element_type=jnp.float32)
    partial = (uncond_part + scale * (cond_part - uncond_part)).astype(jnp.bfloat16)
    arrived = lax.all_to_all(partial, BLK, 0, 0, tiled=False).astype(jnp.float32)
    gate = lax.dynamic_slice_in_dim(modulation[2], blk * feat_width, feat_width, 0)
    projected = gate * jnp.sum(arrived, 0)
    guided = hidden_part + projected
    return guided.reshape(1, 1, half_rows, feat_width)


def solution(mesh):
    devices = mesh.devices.reshape(2, 4, 2, 2, 4)
    own = Mesh(devices, ("cfg", "x", "core", "zhi", "y"))
    return jax.shard_map(
        local,
        mesh=own,
        in_specs=(
            P("cfg", SEQ, BLK),
            P(),
            P(("cfg",) + SEQ, None, BLK),
            P(BLK, ("cfg",) + SEQ),
            P(),
            P(None, SEQ),
            P(),
        ),
        out_specs=P(SEQ, "cfg", None, BLK),
        check_vma=False,
    )
```

```python
import jax
import jax.numpy as jnp
import numpy as np
from jax import lax
from jax.experimental.layout import Layout, with_layout_constraint
from jax.sharding import Mesh, PartitionSpec as P

HEAD_DIM = 128
SEQ = ("x", "core")
BLK = ("zhi", "y")
SWAP = [(0, 1), (1, 0)]


def rotary_angles(head_width):
    third = head_width // 6
    first_dim = head_width - 4 * third
    other_dim = 2 * third
    pair_index = np.arange(head_width) // 2
    first_pairs = first_dim // 2
    other_pairs = other_dim // 2
    in_first = pair_index < first_pairs
    in_second = (pair_index >= first_pairs) & (pair_index < first_pairs + other_pairs)
    in_third = pair_index >= first_pairs + other_pairs
    row_first = np.where(in_first, 10000.0 ** (-2.0 * pair_index / first_dim), 0.0)
    row_second = np.where(
        in_second, 10000.0 ** (-2.0 * (pair_index - first_pairs) / other_dim), 0.0
    )
    row_third = np.where(
        in_third, 10000.0 ** (-2.0 * (pair_index - first_pairs - other_pairs) / other_dim), 0.0
    )
    return np.stack([row_first, row_second, row_third]).astype(np.float32)


def turn_matrix(head_width):
    row_index = np.arange(head_width)[:, None]
    col_index = np.arange(head_width)[None, :]
    upper = np.where((col_index == row_index + 1) & (row_index % 2 == 0), 1.0, 0.0)
    lower = np.where((col_index == row_index - 1) & (row_index % 2 == 1), -1.0, 0.0)
    return (upper + lower).astype(np.float32)


def layer_norm(inputs):
    row_mean = jnp.mean(inputs, -1, keepdims=True)
    centered = inputs - row_mean
    variance = jnp.mean(centered * centered, -1, keepdims=True)
    return centered * lax.rsqrt(variance + 1e-06)


def rms_norm(inputs):
    return inputs * lax.rsqrt(jnp.mean(inputs * inputs, -1, keepdims=True) + 1e-06)


def rotate(inputs, cosine, sine, turning):
    turned = jnp.einsum("thd,de->the", inputs, turning, precision=lax.Precision.HIGHEST)
    return inputs * cosine + turned * sine


def clip_of(clip_ends, token_index):
    return jnp.sum((token_index[:, None] >= clip_ends[None, :]).astype(jnp.int32), 1)


def local(hidden, modulation, in_projection, out_projection, lengths, positions, guidance):
    cfg = lax.axis_index("cfg")
    core = lax.axis_index("core")
    seq = lax.axis_index("x") * 2 + core
    blk = lax.axis_index("zhi") * lax.axis_size("y") + lax.axis_index("y")
    states = hidden[0]
    tok_count = states.shape[0]
    feat_width = states.shape[1]
    half_rows = tok_count // 2
    n_blk = lax.axis_size(BLK)
    inner_width = in_projection.shape[2]
    head_count = inner_width // HEAD_DIM

    sent_rows = lax.dynamic_slice_in_dim(states, (1 - cfg) * half_rows, half_rows, 0)
    other_rows = lax.ppermute(sent_rows, "cfg", SWAP)
    mine_rows = lax.dynamic_slice_in_dim(states, cfg * half_rows, half_rows, 0)
    is_cond = cfg == 0
    cond_rows = jnp.where(is_cond, mine_rows, other_rows).astype(jnp.float32)
    uncond_rows = jnp.where(is_cond, other_rows, mine_rows).astype(jnp.float32)
    scale = guidance[0]
    hidden_part = uncond_rows + scale * (cond_rows - uncond_rows)

    spread = jnp.broadcast_to(states[None], (n_blk,) + states.shape)
    full_states = lax.all_to_all(spread, BLK, 0, 0, tiled=False)
    full_states, hidden_part = lax.optimization_barrier((full_states, hidden_part))
    inputs = full_states.astype(jnp.float32)
    row_mean = jnp.mean(inputs, (0, 2), keepdims=True)
    centered = inputs - row_mean
    variance = jnp.mean(centered * centered, (0, 2), keepdims=True)
    normed = centered * lax.rsqrt(variance + 1e-06)
    mod_shift = modulation[0].reshape(n_blk, 1, feat_width)
    mod_scale = modulation[1].reshape(n_blk, 1, feat_width)
    modulated = (normed * (1.0 + mod_scale) + mod_shift).astype(jnp.bfloat16)

    stacked = lax.all_gather(in_projection, "cfg", axis=0, tiled=False)
    piece = lax.all_gather(stacked, SEQ, axis=0, tiled=False)
    n_seq = piece.shape[0]
    rows = in_projection.shape[0]
    per_blk = feat_width // rows
    mod_perm = modulated.reshape(2, n_blk // 2, tok_count, per_blk, rows).transpose(2, 1, 3, 0, 4)
    mod_perm = mod_perm.reshape(tok_count, n_seq, 2, rows)
    mixed = jnp.einsum(
        "tabi,abiqe->tqe",
        mod_perm,
        piece,
        preferred_element_type=jnp.float32,
    )
    mixed = with_layout_constraint(mixed, Layout((0, 1, 2)))
    mixed = mixed.reshape(tok_count, 3, head_count, HEAD_DIM)

    angle_table = jnp.asarray(rotary_angles(HEAD_DIM))
    turning = jnp.asarray(turn_matrix(HEAD_DIM))
    angles = jnp.einsum(
        "at,ae->te", positions.astype(jnp.float32), angle_table, precision=lax.Precision.HIGHEST
    )
    cosine = jnp.cos(angles)[:, None, :]
    sine = jnp.sin(angles)[:, None, :]
    queries = rotate(rms_norm(mixed[:, 0]), cosine, sine, turning).astype(jnp.bfloat16)
    key_rows = rotate(rms_norm(mixed[:, 1]), cosine, sine, turning).astype(jnp.bfloat16)
    value_rows = mixed[:, 2].astype(jnp.bfloat16)

    kv = jnp.stack([key_rows, value_rows], axis=1)
    kv_mine = lax.all_gather(kv, "x", axis=0, tiled=True)
    kv_other = lax.ppermute(kv_mine, "core", SWAP)
    kv_all = jnp.concatenate([kv_mine, kv_other], axis=0)
    key_piece = kv_all[:, 0]
    value_piece = kv_all[:, 1]
    row_count = key_piece.shape[0]
    n_x = kv_mine.shape[0] // tok_count

    clip_ends = jnp.cumsum(lengths)
    query_clip = clip_of(clip_ends, seq * tok_count + jnp.arange(tok_count, dtype=jnp.int32))
    key_row = jnp.arange(row_count, dtype=jnp.int32)
    key_block = key_row // tok_count
    key_core = jnp.where(key_block < n_x, core, 1 - core)
    key_token = ((key_block % n_x) * 2 + key_core) * tok_count + key_row % tok_count
    key_clip_all = clip_of(clip_ends, key_token)

    score_scale = HEAD_DIM ** (-0.5)
    key_block_size = 512 if row_count % 512 == 0 else row_count

    def attend(first_query):
        query_rows = lax.dynamic_slice_in_dim(queries, first_query, half_rows, 0)
        clip_rows = lax.dynamic_slice_in_dim(query_clip, first_query, half_rows, 0)
        numerator = jnp.zeros((half_rows, head_count, HEAD_DIM), jnp.float32)
        denominator = jnp.zeros((head_count, half_rows), jnp.float32)
        for start in range(0, row_count, key_block_size):
            key_slab = key_piece[start:start + key_block_size]
            value_slab = value_piece[start:start + key_block_size]
            key_clip = key_clip_all[start:start + key_block_size]
            scores = (
                jnp.einsum("qhd,khd->hqk", query_rows, key_slab, preferred_element_type=jnp.float32)
                * score_scale
            )
            same_clip = clip_rows[:, None] == key_clip[None, :]
            weights = jnp.where(same_clip[None], jnp.exp(scores), 0.0)
            numerator = numerator + jnp.einsum(
                "hqk,khd->qhd",
                weights.astype(jnp.bfloat16),
                value_slab,
                preferred_element_type=jnp.float32,
            )
            denominator = denominator + jnp.sum(weights, -1)
        return (
            (numerator / jnp.transpose(denominator)[:, :, None])
            .astype(jnp.bfloat16)
            .reshape(half_rows, inner_width)
        )

    sent_att = attend((1 - cfg) * half_rows)
    other_att = lax.ppermute(sent_att, "cfg", SWAP)
    mine_att = attend(cfg * half_rows)
    cond_att = jnp.where(is_cond, mine_att, other_att)
    uncond_att = jnp.where(is_cond, other_att, mine_att)
    out_piece = lax.all_gather(out_projection, ("cfg",) + SEQ, axis=1, tiled=True).reshape(
        inner_width, n_blk, feat_width
    )
    cond_part = jnp.einsum("te,ebn->btn", cond_att, out_piece, preferred_element_type=jnp.float32)
    uncond_part = jnp.einsum("te,ebn->btn", uncond_att, out_piece, preferred_element_type=jnp.float32)
    partial = (uncond_part + scale * (cond_part - uncond_part)).astype(jnp.bfloat16)
    arrived = lax.all_to_all(partial, BLK, 0, 0, tiled=False).astype(jnp.float32)
    gate = lax.dynamic_slice_in_dim(modulation[2], blk * feat_width, feat_width, 0)
    projected = gate * jnp.sum(arrived, 0)
    guided = hidden_part + projected
    return guided.reshape(1, 1, half_rows, feat_width)


def solution(mesh):
    devices = mesh.devices.reshape(2, 4, 2, 2, 4)
    own = Mesh(devices, ("cfg", "x", "core", "zhi", "y"))
    return jax.shard_map(
        local,
        mesh=own,
        in_specs=(
            P("cfg", SEQ, BLK),
            P(),
            P(("cfg",) + SEQ, None, BLK),
            P(BLK, ("cfg",) + SEQ),
            P(),
            P(None, SEQ),
            P(),
        ),
        out_specs=P(SEQ, "cfg", None, BLK),
        check_vma=False,
    )
```

```python
import jax
import jax.numpy as jnp
import numpy as np
from jax import lax
from jax.experimental.layout import Layout, with_layout_constraint
from jax.sharding import Mesh, PartitionSpec as P

HEAD_DIM = 128
SEQ = ("x", "core")
BLK = ("zhi", "y")
SWAP = [(0, 1), (1, 0)]


def rotary_angles(head_width):
    third = head_width // 6
    first_dim = head_width - 4 * third
    other_dim = 2 * third
    pair_index = np.arange(head_width) // 2
    first_pairs = first_dim // 2
    other_pairs = other_dim // 2
    in_first = pair_index < first_pairs
    in_second = (pair_index >= first_pairs) & (pair_index < first_pairs + other_pairs)
    in_third = pair_index >= first_pairs + other_pairs
    row_first = np.where(in_first, 10000.0 ** (-2.0 * pair_index / first_dim), 0.0)
    row_second = np.where(
        in_second, 10000.0 ** (-2.0 * (pair_index - first_pairs) / other_dim), 0.0
    )
    row_third = np.where(
        in_third, 10000.0 ** (-2.0 * (pair_index - first_pairs - other_pairs) / other_dim), 0.0
    )
    return np.stack([row_first, row_second, row_third]).astype(np.float32)


def turn_matrix(head_width):
    row_index = np.arange(head_width)[:, None]
    col_index = np.arange(head_width)[None, :]
    upper = np.where((col_index == row_index + 1) & (row_index % 2 == 0), 1.0, 0.0)
    lower = np.where((col_index == row_index - 1) & (row_index % 2 == 1), -1.0, 0.0)
    return (upper + lower).astype(np.float32)


def layer_norm(inputs):
    row_mean = jnp.mean(inputs, -1, keepdims=True)
    centered = inputs - row_mean
    variance = jnp.mean(centered * centered, -1, keepdims=True)
    return centered * lax.rsqrt(variance + 1e-06)


def rms_norm(inputs):
    return inputs * lax.rsqrt(jnp.mean(inputs * inputs, -1, keepdims=True) + 1e-06)


def rotate(inputs, cosine, sine, turning):
    turned = jnp.einsum("thd,de->the", inputs, turning, precision=lax.Precision.HIGHEST)
    return inputs * cosine + turned * sine


def clip_of(clip_ends, token_index):
    return jnp.sum((token_index[:, None] >= clip_ends[None, :]).astype(jnp.int32), 1)


def local(hidden, modulation, in_projection, out_projection, lengths, positions, guidance):
    cfg = lax.axis_index("cfg")
    core = lax.axis_index("core")
    seq = lax.axis_index("x") * 2 + core
    blk = lax.axis_index("zhi") * lax.axis_size("y") + lax.axis_index("y")
    states = hidden[0]
    tok_count = states.shape[0]
    feat_width = states.shape[1]
    half_rows = tok_count // 2
    n_blk = lax.axis_size(BLK)
    inner_width = in_projection.shape[2]
    head_count = inner_width // HEAD_DIM

    sent_rows = lax.dynamic_slice_in_dim(states, (1 - cfg) * half_rows, half_rows, 0)
    other_rows = lax.ppermute(sent_rows, "cfg", SWAP)
    mine_rows = lax.dynamic_slice_in_dim(states, cfg * half_rows, half_rows, 0)
    is_cond = cfg == 0
    cond_rows = jnp.where(is_cond, mine_rows, other_rows).astype(jnp.float32)
    uncond_rows = jnp.where(is_cond, other_rows, mine_rows).astype(jnp.float32)
    scale = guidance[0]
    hidden_part = uncond_rows + scale * (cond_rows - uncond_rows)

    spread = jnp.broadcast_to(states[None], (n_blk,) + states.shape)
    full_states = lax.all_to_all(spread, BLK, 0, 0, tiled=False)
    full_states, hidden_part = lax.optimization_barrier((full_states, hidden_part))
    inputs = full_states.astype(jnp.float32)
    row_mean = jnp.mean(inputs, (0, 2), keepdims=True)
    centered = inputs - row_mean
    variance = jnp.mean(centered * centered, (0, 2), keepdims=True)
    normed = centered * lax.rsqrt(variance + 1e-06)
    mod_shift = modulation[0].reshape(n_blk, 1, feat_width)
    mod_scale = modulation[1].reshape(n_blk, 1, feat_width)
    modulated = (normed * (1.0 + mod_scale) + mod_shift).astype(jnp.bfloat16)

    shard_other = lax.ppermute(in_projection, "cfg", SWAP)
    stacked = jnp.stack(
        [
            jnp.where(is_cond, in_projection, shard_other),
            jnp.where(is_cond, shard_other, in_projection),
        ]
    )
    piece = lax.all_gather(stacked, SEQ, axis=0, tiled=False)
    n_seq = piece.shape[0]
    rows = in_projection.shape[0]
    per_blk = feat_width // rows
    mod_perm = modulated.reshape(2, n_blk // 2, tok_count, per_blk, rows).transpose(2, 1, 3, 0, 4)
    mod_perm = mod_perm.reshape(tok_count, n_seq, 2, rows)
    mixed = jnp.einsum(
        "tabi,abiqe->tqe",
        mod_perm,
        piece,
        preferred_element_type=jnp.float32,
    )
    mixed = with_layout_constraint(mixed, Layout((0, 1, 2)))
    mixed = mixed.reshape(tok_count, 3, head_count, HEAD_DIM)

    angle_table = jnp.asarray(rotary_angles(HEAD_DIM))
    turning = jnp.asarray(turn_matrix(HEAD_DIM))
    angles = jnp.einsum(
        "at,ae->te", positions.astype(jnp.float32), angle_table, precision=lax.Precision.HIGHEST
    )
    cosine = jnp.cos(angles)[:, None, :]
    sine = jnp.sin(angles)[:, None, :]
    queries = rotate(rms_norm(mixed[:, 0]), cosine, sine, turning).astype(jnp.bfloat16)
    key_rows = rotate(rms_norm(mixed[:, 1]), cosine, sine, turning).astype(jnp.bfloat16)
    value_rows = mixed[:, 2].astype(jnp.bfloat16)

    kv = jnp.stack([key_rows, value_rows], axis=1)
    n_x = lax.axis_size("x")
    x_index = lax.axis_index("x")
    kv_mine = jnp.concatenate(
        [kv] + [lax.ppermute(kv, "x", [(i, (i + j) % n_x) for i in range(n_x)]) for j in range(1, n_x)],
        axis=0,
    )
    kv_other = lax.ppermute(kv_mine, "core", SWAP)
    kv_all = jnp.concatenate([kv_mine, kv_other], axis=0)
    key_piece = kv_all[:, 0]
    value_piece = kv_all[:, 1]
    row_count = key_piece.shape[0]

    clip_ends = jnp.cumsum(lengths)
    query_clip = clip_of(clip_ends, seq * tok_count + jnp.arange(tok_count, dtype=jnp.int32))
    key_row = jnp.arange(row_count, dtype=jnp.int32)
    key_block = key_row // tok_count
    key_core = jnp.where(key_block < n_x, core, 1 - core)
    key_x = (x_index - key_block % n_x + n_x) % n_x
    key_token = (key_x * 2 + key_core) * tok_count + key_row % tok_count
    key_clip_all = clip_of(clip_ends, key_token)

    score_scale = HEAD_DIM ** (-0.5)
    key_block_size = 512 if row_count % 512 == 0 else row_count

    def attend(first_query):
        query_rows = lax.dynamic_slice_in_dim(queries, first_query, half_rows, 0)
        clip_rows = lax.dynamic_slice_in_dim(query_clip, first_query, half_rows, 0)
        numerator = jnp.zeros((half_rows, head_count, HEAD_DIM), jnp.float32)
        denominator = jnp.zeros((head_count, half_rows), jnp.float32)
        for start in range(0, row_count, key_block_size):
            key_slab = key_piece[start:start + key_block_size]
            value_slab = value_piece[start:start + key_block_size]
            key_clip = key_clip_all[start:start + key_block_size]
            scores = (
                jnp.einsum("qhd,khd->hqk", query_rows, key_slab, preferred_element_type=jnp.float32)
                * score_scale
            )
            same_clip = clip_rows[:, None] == key_clip[None, :]
            weights = jnp.where(same_clip[None], jnp.exp(scores), 0.0)
            numerator = numerator + jnp.einsum(
                "hqk,khd->qhd",
                weights.astype(jnp.bfloat16),
                value_slab,
                preferred_element_type=jnp.float32,
            )
            denominator = denominator + jnp.sum(weights, -1)
        return (
            (numerator / jnp.transpose(denominator)[:, :, None])
            .astype(jnp.bfloat16)
            .reshape(half_rows, inner_width)
        )

    sent_att = attend((1 - cfg) * half_rows)
    other_att = lax.ppermute(sent_att, "cfg", SWAP)
    mine_att = attend(cfg * half_rows)
    cond_att = jnp.where(is_cond, mine_att, other_att)
    uncond_att = jnp.where(is_cond, other_att, mine_att)
    out_piece = lax.all_gather(out_projection, ("cfg",) + SEQ, axis=1, tiled=True).reshape(
        inner_width, n_blk, feat_width
    )
    cond_part = jnp.einsum("te,ebn->btn", cond_att, out_piece, preferred_element_type=jnp.float32)
    uncond_part = jnp.einsum("te,ebn->btn", uncond_att, out_piece, preferred_element_type=jnp.float32)
    partial = (uncond_part + scale * (cond_part - uncond_part)).astype(jnp.bfloat16)
    arrived = lax.all_to_all(partial, BLK, 0, 0, tiled=False).astype(jnp.float32)
    gate = lax.dynamic_slice_in_dim(modulation[2], blk * feat_width, feat_width, 0)
    projected = gate * jnp.sum(arrived, 0)
    guided = hidden_part + projected
    return guided.reshape(1, 1, half_rows, feat_width)


def solution(mesh):
    devices = mesh.devices.reshape(2, 4, 2, 2, 4)
    own = Mesh(devices, ("cfg", "x", "core", "zhi", "y"))
    return jax.shard_map(
        local,
        mesh=own,
        in_specs=(
            P("cfg", SEQ, BLK),
            P(),
            P(("cfg",) + SEQ, None, BLK),
            P(BLK, ("cfg",) + SEQ),
            P(),
            P(None, SEQ),
            P(),
        ),
        out_specs=P(SEQ, "cfg", None, BLK),
        check_vma=False,
    )
```

```python
import jax
import jax.numpy as jnp
import numpy as np
from jax import lax
from jax.experimental.layout import Layout, with_layout_constraint
from jax.sharding import Mesh, PartitionSpec as P

HEAD_DIM = 128
SEQ = ("x", "core")
BLK = ("zhi", "y")
SWAP = [(0, 1), (1, 0)]


def rotary_angles(head_width):
    third = head_width // 6
    first_dim = head_width - 4 * third
    other_dim = 2 * third
    pair_index = np.arange(head_width) // 2
    first_pairs = first_dim // 2
    other_pairs = other_dim // 2
    in_first = pair_index < first_pairs
    in_second = (pair_index >= first_pairs) & (pair_index < first_pairs + other_pairs)
    in_third = pair_index >= first_pairs + other_pairs
    row_first = np.where(in_first, 10000.0 ** (-2.0 * pair_index / first_dim), 0.0)
    row_second = np.where(
        in_second, 10000.0 ** (-2.0 * (pair_index - first_pairs) / other_dim), 0.0
    )
    row_third = np.where(
        in_third, 10000.0 ** (-2.0 * (pair_index - first_pairs - other_pairs) / other_dim), 0.0
    )
    return np.stack([row_first, row_second, row_third]).astype(np.float32)


def turn_matrix(head_width):
    row_index = np.arange(head_width)[:, None]
    col_index = np.arange(head_width)[None, :]
    upper = np.where((col_index == row_index + 1) & (row_index % 2 == 0), 1.0, 0.0)
    lower = np.where((col_index == row_index - 1) & (row_index % 2 == 1), -1.0, 0.0)
    return (upper + lower).astype(np.float32)


def layer_norm(inputs):
    row_mean = jnp.mean(inputs, -1, keepdims=True)
    centered = inputs - row_mean
    variance = jnp.mean(centered * centered, -1, keepdims=True)
    return centered * lax.rsqrt(variance + 1e-06)


def rms_norm(inputs):
    return inputs * lax.rsqrt(jnp.mean(inputs * inputs, -1, keepdims=True) + 1e-06)


def rotate(inputs, cosine, sine, turning):
    turned = jnp.einsum("thd,de->the", inputs, turning, precision=lax.Precision.HIGHEST)
    return inputs * cosine + turned * sine


def clip_of(clip_ends, token_index):
    return jnp.sum((token_index[:, None] >= clip_ends[None, :]).astype(jnp.int32), 1)


def local(hidden, modulation, in_projection, out_projection, lengths, positions, guidance):
    cfg = lax.axis_index("cfg")
    core = lax.axis_index("core")
    seq = lax.axis_index("x") * 2 + core
    blk = lax.axis_index("zhi") * lax.axis_size("y") + lax.axis_index("y")
    states = hidden[0]
    tok_count = states.shape[0]
    feat_width = states.shape[1]
    half_rows = tok_count // 2
    n_blk = lax.axis_size(BLK)
    inner_width = in_projection.shape[2]
    head_count = inner_width // HEAD_DIM

    sent_rows = lax.dynamic_slice_in_dim(states, (1 - cfg) * half_rows, half_rows, 0)
    other_rows = lax.ppermute(sent_rows, "cfg", SWAP)
    mine_rows = lax.dynamic_slice_in_dim(states, cfg * half_rows, half_rows, 0)
    is_cond = cfg == 0
    cond_rows = jnp.where(is_cond, mine_rows, other_rows).astype(jnp.float32)
    uncond_rows = jnp.where(is_cond, other_rows, mine_rows).astype(jnp.float32)
    scale = guidance[0]
    hidden_part = uncond_rows + scale * (cond_rows - uncond_rows)

    spread = jnp.broadcast_to(states[None], (n_blk,) + states.shape)
    full_states = lax.all_to_all(spread, BLK, 0, 0, tiled=False)
    full_states, hidden_part = lax.optimization_barrier((full_states, hidden_part))
    inputs = full_states.astype(jnp.float32)
    row_mean = jnp.mean(inputs, (0, 2), keepdims=True)
    centered = inputs - row_mean
    variance = jnp.mean(centered * centered, (0, 2), keepdims=True)
    normed = centered * lax.rsqrt(variance + 1e-06)
    mod_shift = modulation[0].reshape(n_blk, 1, feat_width)
    mod_scale = modulation[1].reshape(n_blk, 1, feat_width)
    modulated = (normed * (1.0 + mod_scale) + mod_shift).astype(jnp.bfloat16)

    shard_other = lax.ppermute(in_projection, "cfg", SWAP)
    stacked = jnp.stack(
        [
            jnp.where(is_cond, in_projection, shard_other),
            jnp.where(is_cond, shard_other, in_projection),
        ]
    )
    piece = lax.all_gather(stacked, SEQ, axis=0, tiled=False)
    n_seq = piece.shape[0]
    rows = in_projection.shape[0]
    per_blk = feat_width // rows
    mod_perm = modulated.reshape(2, n_blk // 2, tok_count, per_blk, rows).transpose(2, 1, 3, 0, 4)
    mod_perm = mod_perm.reshape(tok_count, n_seq, 2, rows)
    mixed = jnp.einsum(
        "tabi,abiqe->tqe",
        mod_perm,
        piece,
        preferred_element_type=jnp.float32,
    )
    mixed = with_layout_constraint(mixed, Layout((0, 1, 2)))
    mixed = mixed.reshape(tok_count, 3, head_count, HEAD_DIM)

    angle_table = jnp.asarray(rotary_angles(HEAD_DIM))
    turning = jnp.asarray(turn_matrix(HEAD_DIM))
    angles = jnp.einsum(
        "at,ae->te", positions.astype(jnp.float32), angle_table, precision=lax.Precision.HIGHEST
    )
    cosine = jnp.cos(angles)[:, None, :]
    sine = jnp.sin(angles)[:, None, :]
    queries = rotate(rms_norm(mixed[:, 0]), cosine, sine, turning).astype(jnp.bfloat16)
    key_rows = rotate(rms_norm(mixed[:, 1]), cosine, sine, turning).astype(jnp.bfloat16)
    value_rows = mixed[:, 2].astype(jnp.bfloat16)

    kv = jnp.stack([key_rows, value_rows], axis=1)
    n_x = lax.axis_size("x")
    x_index = lax.axis_index("x")
    clip_ends = jnp.cumsum(lengths)
    local_rows = jnp.arange(tok_count, dtype=jnp.int32)
    query_clip = clip_of(clip_ends, seq * tok_count + local_rows)

    blocks = []
    for j in range(n_x):
        if j == 0:
            kv_x = kv
        else:
            kv_x = lax.ppermute(kv, "x", [(i, (i + j) % n_x) for i in range(n_x)])
        x_src = (x_index - j + n_x) % n_x
        blocks.append((kv_x, x_src * 2 + core))
        blocks.append((lax.ppermute(kv_x, "core", SWAP), x_src * 2 + 1 - core))

    score_scale = HEAD_DIM ** (-0.5)

    def update(running, query_rows, clip_rows, block):
        numerator, denominator = running
        kv_block, source = block
        key_clip = clip_of(clip_ends, source * tok_count + local_rows)
        scores = (
            jnp.einsum("qhd,khd->hqk", query_rows, kv_block[:, 0], preferred_element_type=jnp.float32)
            * score_scale
        )
        same_clip = clip_rows[:, None] == key_clip[None, :]
        weights = jnp.where(same_clip[None], jnp.exp(scores), 0.0)
        numerator = numerator + jnp.einsum(
            "hqk,khd->qhd",
            weights.astype(jnp.bfloat16),
            kv_block[:, 1],
            preferred_element_type=jnp.float32,
        )
        denominator = denominator + jnp.sum(weights, -1)
        return (numerator, denominator)

    running = (
        jnp.zeros((tok_count, head_count, HEAD_DIM), jnp.float32),
        jnp.zeros((head_count, tok_count), jnp.float32),
    )
    for block in blocks[:-1]:
        running = update(running, queries, query_clip, block)

    def attend(first_query):
        part = (
            lax.dynamic_slice_in_dim(running[0], first_query, half_rows, 0),
            lax.dynamic_slice_in_dim(running[1], first_query, half_rows, 1),
        )
        numerator, denominator = update(
            part,
            lax.dynamic_slice_in_dim(queries, first_query, half_rows, 0),
            lax.dynamic_slice_in_dim(query_clip, first_query, half_rows, 0),
            blocks[-1],
        )
        return (
            (numerator / jnp.transpose(denominator)[:, :, None])
            .astype(jnp.bfloat16)
            .reshape(half_rows, inner_width)
        )

    sent_att = attend((1 - cfg) * half_rows)
    other_att = lax.ppermute(sent_att, "cfg", SWAP)
    mine_att = attend(cfg * half_rows)
    cond_att = jnp.where(is_cond, mine_att, other_att)
    uncond_att = jnp.where(is_cond, other_att, mine_att)
    out_piece = lax.all_gather(out_projection, ("cfg",) + SEQ, axis=1, tiled=True).reshape(
        inner_width, n_blk, feat_width
    )
    cond_part = jnp.einsum("te,ebn->btn", cond_att, out_piece, preferred_element_type=jnp.float32)
    uncond_part = jnp.einsum("te,ebn->btn", uncond_att, out_piece, preferred_element_type=jnp.float32)
    partial = (uncond_part + scale * (cond_part - uncond_part)).astype(jnp.bfloat16)
    arrived = lax.all_to_all(partial, BLK, 0, 0, tiled=False).astype(jnp.float32)
    gate = lax.dynamic_slice_in_dim(modulation[2], blk * feat_width, feat_width, 0)
    projected = gate * jnp.sum(arrived, 0)
    guided = hidden_part + projected
    return guided.reshape(1, 1, half_rows, feat_width)


def solution(mesh):
    devices = mesh.devices.reshape(2, 4, 2, 2, 4)
    own = Mesh(devices, ("cfg", "x", "core", "zhi", "y"))
    return jax.shard_map(
        local,
        mesh=own,
        in_specs=(
            P("cfg", SEQ, BLK),
            P(),
            P(("cfg",) + SEQ, None, BLK),
            P(BLK, ("cfg",) + SEQ),
            P(),
            P(None, SEQ),
            P(),
        ),
        out_specs=P(SEQ, "cfg", None, BLK),
        check_vma=False,
    )
```

```python
import jax
import jax.numpy as jnp
import numpy as np
from jax import lax
from jax.experimental.layout import Layout, with_layout_constraint
from jax.sharding import Mesh, PartitionSpec as P

HEAD_DIM = 128
SEQ = ("x", "core")
BLK = ("zhi", "y")
SWAP = [(0, 1), (1, 0)]


def rotary_angles(head_width):
    third = head_width // 6
    first_dim = head_width - 4 * third
    other_dim = 2 * third
    pair_index = np.arange(head_width) // 2
    first_pairs = first_dim // 2
    other_pairs = other_dim // 2
    in_first = pair_index < first_pairs
    in_second = (pair_index >= first_pairs) & (pair_index < first_pairs + other_pairs)
    in_third = pair_index >= first_pairs + other_pairs
    row_first = np.where(in_first, 10000.0 ** (-2.0 * pair_index / first_dim), 0.0)
    row_second = np.where(
        in_second, 10000.0 ** (-2.0 * (pair_index - first_pairs) / other_dim), 0.0
    )
    row_third = np.where(
        in_third, 10000.0 ** (-2.0 * (pair_index - first_pairs - other_pairs) / other_dim), 0.0
    )
    return np.stack([row_first, row_second, row_third]).astype(np.float32)


def turn_matrix(head_width):
    row_index = np.arange(head_width)[:, None]
    col_index = np.arange(head_width)[None, :]
    upper = np.where((col_index == row_index + 1) & (row_index % 2 == 0), 1.0, 0.0)
    lower = np.where((col_index == row_index - 1) & (row_index % 2 == 1), -1.0, 0.0)
    return (upper + lower).astype(np.float32)


def layer_norm(inputs):
    row_mean = jnp.mean(inputs, -1, keepdims=True)
    centered = inputs - row_mean
    variance = jnp.mean(centered * centered, -1, keepdims=True)
    return centered * lax.rsqrt(variance + 1e-06)


def rms_norm(inputs):
    return inputs * lax.rsqrt(jnp.mean(inputs * inputs, -1, keepdims=True) + 1e-06)


def rotate(inputs, cosine, sine, turning):
    turned = jnp.einsum("thd,de->the", inputs, turning, precision=lax.Precision.HIGHEST)
    return inputs * cosine + turned * sine


def clip_of(clip_ends, token_index):
    return jnp.sum((token_index[:, None] >= clip_ends[None, :]).astype(jnp.int32), 1)


def local(hidden, modulation, in_projection, out_projection, lengths, positions, guidance):
    cfg = lax.axis_index("cfg")
    core = lax.axis_index("core")
    seq = lax.axis_index("x") * 2 + core
    blk = lax.axis_index("zhi") * lax.axis_size("y") + lax.axis_index("y")
    states = hidden[0]
    tok_count = states.shape[0]
    feat_width = states.shape[1]
    half_rows = tok_count // 2
    n_blk = lax.axis_size(BLK)
    inner_width = in_projection.shape[2]
    head_count = inner_width // HEAD_DIM

    sent_rows = lax.dynamic_slice_in_dim(states, (1 - cfg) * half_rows, half_rows, 0)
    other_rows = lax.ppermute(sent_rows, "cfg", SWAP)
    mine_rows = lax.dynamic_slice_in_dim(states, cfg * half_rows, half_rows, 0)
    is_cond = cfg == 0
    cond_rows = jnp.where(is_cond, mine_rows, other_rows).astype(jnp.float32)
    uncond_rows = jnp.where(is_cond, other_rows, mine_rows).astype(jnp.float32)
    scale = guidance[0]
    hidden_part = uncond_rows + scale * (cond_rows - uncond_rows)

    spread = jnp.broadcast_to(states[None], (n_blk,) + states.shape)
    full_states = lax.all_to_all(spread, BLK, 0, 0, tiled=False)
    full_states, hidden_part = lax.optimization_barrier((full_states, hidden_part))
    inputs = full_states.astype(jnp.float32)
    row_mean = jnp.mean(inputs, (0, 2), keepdims=True)
    centered = inputs - row_mean
    variance = jnp.mean(centered * centered, (0, 2), keepdims=True)
    normed = centered * lax.rsqrt(variance + 1e-06)
    mod_shift = modulation[0].reshape(n_blk, 1, feat_width)
    mod_scale = modulation[1].reshape(n_blk, 1, feat_width)
    modulated = (normed * (1.0 + mod_scale) + mod_shift).astype(jnp.bfloat16)

    shard_other = lax.ppermute(in_projection, "cfg", SWAP)
    stacked = jnp.stack(
        [
            jnp.where(is_cond, in_projection, shard_other),
            jnp.where(is_cond, shard_other, in_projection),
        ]
    )
    piece = lax.all_gather(stacked, SEQ, axis=0, tiled=False)
    n_seq = piece.shape[0]
    rows = in_projection.shape[0]
    per_blk = feat_width // rows
    mod_perm = modulated.reshape(2, n_blk // 2, tok_count, per_blk, rows).transpose(2, 1, 3, 0, 4)
    mod_perm = mod_perm.reshape(tok_count, n_seq, 2, rows)
    mixed = jnp.einsum(
        "tabi,abiqe->tqe",
        mod_perm,
        piece,
        preferred_element_type=jnp.float32,
    )
    mixed = with_layout_constraint(mixed, Layout((0, 1, 2)))
    mixed = mixed.reshape(tok_count, 3, head_count, HEAD_DIM)

    angle_table = jnp.asarray(rotary_angles(HEAD_DIM))
    turning = jnp.asarray(turn_matrix(HEAD_DIM))
    angles = jnp.einsum(
        "at,ae->te", positions.astype(jnp.float32), angle_table, precision=lax.Precision.HIGHEST
    )
    cosine = jnp.cos(angles)[:, None, :]
    sine = jnp.sin(angles)[:, None, :]
    queries = rotate(rms_norm(mixed[:, 0]), cosine, sine, turning).astype(jnp.bfloat16)
    key_rows = rotate(rms_norm(mixed[:, 1]), cosine, sine, turning).astype(jnp.bfloat16)
    value_rows = mixed[:, 2].astype(jnp.bfloat16)

    kv = jnp.stack([key_rows, value_rows], axis=1)
    n_x = lax.axis_size("x")
    x_index = lax.axis_index("x")
    from_behind = lax.ppermute(kv, "x", [(i, (i + 1) % n_x) for i in range(n_x)])
    from_ahead = lax.ppermute(kv, "x", [(i, (i - 1) % n_x) for i in range(n_x)])
    relayed = jnp.where(core == 0, from_behind, from_ahead)
    relay_pairs = [(i * 2, ((i + 1) % n_x) * 2) for i in range(n_x)]
    relay_pairs += [(i * 2 + 1, ((i - 1) % n_x) * 2 + 1) for i in range(n_x)]
    from_far = lax.ppermute(relayed, SEQ, relay_pairs)
    kv_mine = jnp.concatenate([kv, from_behind, from_far, from_ahead], axis=0)
    kv_other = lax.ppermute(kv_mine, "core", SWAP)
    kv_all = jnp.concatenate([kv_mine, kv_other], axis=0)
    key_piece = kv_all[:, 0]
    value_piece = kv_all[:, 1]
    row_count = key_piece.shape[0]

    clip_ends = jnp.cumsum(lengths)
    query_clip = clip_of(clip_ends, seq * tok_count + jnp.arange(tok_count, dtype=jnp.int32))
    key_row = jnp.arange(row_count, dtype=jnp.int32)
    key_block = key_row // tok_count
    key_core = jnp.where(key_block < n_x, core, 1 - core)
    key_x = (x_index - key_block % n_x + n_x) % n_x
    key_token = (key_x * 2 + key_core) * tok_count + key_row % tok_count
    key_clip_all = clip_of(clip_ends, key_token)

    score_scale = HEAD_DIM ** (-0.5)
    key_block_size = 512 if row_count % 512 == 0 else row_count

    def attend(first_query):
        query_rows = lax.dynamic_slice_in_dim(queries, first_query, half_rows, 0)
        clip_rows = lax.dynamic_slice_in_dim(query_clip, first_query, half_rows, 0)
        numerator = jnp.zeros((half_rows, head_count, HEAD_DIM), jnp.float32)
        denominator = jnp.zeros((head_count, half_rows), jnp.float32)
        for start in range(0, row_count, key_block_size):
            key_slab = key_piece[start:start + key_block_size]
            value_slab = value_piece[start:start + key_block_size]
            key_clip = key_clip_all[start:start + key_block_size]
            scores = (
                jnp.einsum("qhd,khd->hqk", query_rows, key_slab, preferred_element_type=jnp.float32)
                * score_scale
            )
            same_clip = clip_rows[:, None] == key_clip[None, :]
            weights = jnp.where(same_clip[None], jnp.exp(scores), 0.0)
            numerator = numerator + jnp.einsum(
                "hqk,khd->qhd",
                weights.astype(jnp.bfloat16),
                value_slab,
                preferred_element_type=jnp.float32,
            )
            denominator = denominator + jnp.sum(weights, -1)
        return (
            (numerator / jnp.transpose(denominator)[:, :, None])
            .astype(jnp.bfloat16)
            .reshape(half_rows, inner_width)
        )

    sent_att = attend((1 - cfg) * half_rows)
    other_att = lax.ppermute(sent_att, "cfg", SWAP)
    mine_att = attend(cfg * half_rows)
    cond_att = jnp.where(is_cond, mine_att, other_att)
    uncond_att = jnp.where(is_cond, other_att, mine_att)
    out_piece = lax.all_gather(out_projection, ("cfg",) + SEQ, axis=1, tiled=True).reshape(
        inner_width, n_blk, feat_width
    )
    cond_part = jnp.einsum("te,ebn->btn", cond_att, out_piece, preferred_element_type=jnp.float32)
    uncond_part = jnp.einsum("te,ebn->btn", uncond_att, out_piece, preferred_element_type=jnp.float32)
    partial = (uncond_part + scale * (cond_part - uncond_part)).astype(jnp.bfloat16)
    arrived = lax.all_to_all(partial, BLK, 0, 0, tiled=False).astype(jnp.float32)
    gate = lax.dynamic_slice_in_dim(modulation[2], blk * feat_width, feat_width, 0)
    projected = gate * jnp.sum(arrived, 0)
    guided = hidden_part + projected
    return guided.reshape(1, 1, half_rows, feat_width)


def solution(mesh):
    devices = mesh.devices.reshape(2, 4, 2, 2, 4)
    own = Mesh(devices, ("cfg", "x", "core", "zhi", "y"))
    return jax.shard_map(
        local,
        mesh=own,
        in_specs=(
            P("cfg", SEQ, BLK),
            P(),
            P(("cfg",) + SEQ, None, BLK),
            P(BLK, ("cfg",) + SEQ),
            P(),
            P(None, SEQ),
            P(),
        ),
        out_specs=P(SEQ, "cfg", None, BLK),
        check_vma=False,
    )
```

```python
import jax
import jax.numpy as jnp
import numpy as np
from jax import lax
from jax.experimental.layout import Layout, with_layout_constraint
from jax.sharding import Mesh, PartitionSpec as P

HEAD_DIM = 128
SEQ = ("x", "core")
BLK = ("zhi", "y")
SWAP = [(0, 1), (1, 0)]


def rotary_angles(head_width):
    third = head_width // 6
    first_dim = head_width - 4 * third
    other_dim = 2 * third
    pair_index = np.arange(head_width) // 2
    first_pairs = first_dim // 2
    other_pairs = other_dim // 2
    in_first = pair_index < first_pairs
    in_second = (pair_index >= first_pairs) & (pair_index < first_pairs + other_pairs)
    in_third = pair_index >= first_pairs + other_pairs
    row_first = np.where(in_first, 10000.0 ** (-2.0 * pair_index / first_dim), 0.0)
    row_second = np.where(
        in_second, 10000.0 ** (-2.0 * (pair_index - first_pairs) / other_dim), 0.0
    )
    row_third = np.where(
        in_third, 10000.0 ** (-2.0 * (pair_index - first_pairs - other_pairs) / other_dim), 0.0
    )
    return np.stack([row_first, row_second, row_third]).astype(np.float32)


def turn_matrix(head_width):
    row_index = np.arange(head_width)[:, None]
    col_index = np.arange(head_width)[None, :]
    upper = np.where((col_index == row_index + 1) & (row_index % 2 == 0), 1.0, 0.0)
    lower = np.where((col_index == row_index - 1) & (row_index % 2 == 1), -1.0, 0.0)
    return (upper + lower).astype(np.float32)


def layer_norm(inputs):
    row_mean = jnp.mean(inputs, -1, keepdims=True)
    centered = inputs - row_mean
    variance = jnp.mean(centered * centered, -1, keepdims=True)
    return centered * lax.rsqrt(variance + 1e-06)


def rms_norm(inputs):
    return inputs * lax.rsqrt(jnp.mean(inputs * inputs, -1, keepdims=True) + 1e-06)


def rotate(inputs, cosine, sine, turning):
    turned = jnp.einsum("thd,de->the", inputs, turning, precision=lax.Precision.HIGHEST)
    return inputs * cosine + turned * sine


def clip_of(clip_ends, token_index):
    return jnp.sum((token_index[:, None] >= clip_ends[None, :]).astype(jnp.int32), 1)


def local(hidden, modulation, in_projection, out_projection, lengths, positions, guidance):
    cfg = lax.axis_index("cfg")
    core = lax.axis_index("core")
    seq = lax.axis_index("x") * 2 + core
    blk = lax.axis_index("zhi") * lax.axis_size("y") + lax.axis_index("y")
    states = hidden[0]
    tok_count = states.shape[0]
    feat_width = states.shape[1]
    half_rows = tok_count // 2
    n_blk = lax.axis_size(BLK)
    inner_width = in_projection.shape[2]
    head_count = inner_width // HEAD_DIM

    sent_rows = lax.dynamic_slice_in_dim(states, (1 - cfg) * half_rows, half_rows, 0)
    other_rows = lax.ppermute(sent_rows, "cfg", SWAP)
    mine_rows = lax.dynamic_slice_in_dim(states, cfg * half_rows, half_rows, 0)
    is_cond = cfg == 0
    cond_rows = jnp.where(is_cond, mine_rows, other_rows).astype(jnp.float32)
    uncond_rows = jnp.where(is_cond, other_rows, mine_rows).astype(jnp.float32)
    scale = guidance[0]
    hidden_part = uncond_rows + scale * (cond_rows - uncond_rows)

    spread = jnp.broadcast_to(states[None], (n_blk,) + states.shape)
    full_states = lax.all_to_all(spread, BLK, 0, 0, tiled=False)
    full_states, hidden_part = lax.optimization_barrier((full_states, hidden_part))
    inputs = full_states.astype(jnp.float32)
    row_mean = jnp.mean(inputs, (0, 2), keepdims=True)
    centered = inputs - row_mean
    variance = jnp.mean(centered * centered, (0, 2), keepdims=True)
    normed = centered * lax.rsqrt(variance + 1e-06)
    mod_shift = modulation[0].reshape(n_blk, 1, feat_width)
    mod_scale = modulation[1].reshape(n_blk, 1, feat_width)
    modulated = (normed * (1.0 + mod_scale) + mod_shift).astype(jnp.bfloat16)

    shard_other = lax.ppermute(in_projection, "cfg", SWAP)
    stacked = jnp.stack(
        [
            jnp.where(is_cond, in_projection, shard_other),
            jnp.where(is_cond, shard_other, in_projection),
        ]
    )
    piece = lax.all_gather(stacked, SEQ, axis=0, tiled=False)
    n_seq = piece.shape[0]
    rows = in_projection.shape[0]
    per_blk = feat_width // rows
    mod_perm = modulated.reshape(2, n_blk // 2, tok_count, per_blk, rows).transpose(2, 1, 3, 0, 4)
    mod_perm = mod_perm.reshape(tok_count, n_seq, 2, rows)
    mixed = jnp.einsum(
        "tabi,abiqe->tqe",
        mod_perm,
        piece,
        preferred_element_type=jnp.float32,
    )
    mixed = with_layout_constraint(mixed, Layout((0, 1, 2)))
    mixed = mixed.reshape(tok_count, 3, head_count, HEAD_DIM)

    angle_table = jnp.asarray(rotary_angles(HEAD_DIM))
    turning = jnp.asarray(turn_matrix(HEAD_DIM))
    angles = jnp.einsum(
        "at,ae->te", positions.astype(jnp.float32), angle_table, precision=lax.Precision.HIGHEST
    )
    cosine = jnp.cos(angles)[:, None, :]
    sine = jnp.sin(angles)[:, None, :]
    queries = rotate(rms_norm(mixed[:, 0]), cosine, sine, turning).astype(jnp.bfloat16)
    key_rows = rotate(rms_norm(mixed[:, 1]), cosine, sine, turning).astype(jnp.bfloat16)
    value_rows = mixed[:, 2].astype(jnp.bfloat16)

    kv = jnp.stack([key_rows, value_rows], axis=1)
    n_x = lax.axis_size("x")
    x_index = lax.axis_index("x")
    from_behind = lax.ppermute(kv, "x", [(i, (i + 1) % n_x) for i in range(n_x)])
    from_ahead = lax.ppermute(kv, "x", [(i, (i - 1) % n_x) for i in range(n_x)])
    relayed = jnp.where(core == 0, from_behind, from_ahead)
    relay_pairs = [(i * 2, ((i + 1) % n_x) * 2) for i in range(n_x)]
    relay_pairs += [(i * 2 + 1, ((i - 1) % n_x) * 2 + 1) for i in range(n_x)]
    from_far = lax.ppermute(relayed, SEQ, relay_pairs)
    kv_mine = jnp.concatenate([kv, from_behind, from_far, from_ahead], axis=0)
    kv_other = jnp.concatenate(
        [lax.ppermute(block, "core", SWAP) for block in (kv, from_behind, from_far, from_ahead)], axis=0
    )
    kv_all = jnp.concatenate([kv_mine, kv_other], axis=0)
    key_piece = kv_all[:, 0]
    value_piece = kv_all[:, 1]
    row_count = key_piece.shape[0]

    clip_ends = jnp.cumsum(lengths)
    query_clip = clip_of(clip_ends, seq * tok_count + jnp.arange(tok_count, dtype=jnp.int32))
    key_row = jnp.arange(row_count, dtype=jnp.int32)
    key_block = key_row // tok_count
    key_core = jnp.where(key_block < n_x, core, 1 - core)
    key_x = (x_index - key_block % n_x + n_x) % n_x
    key_token = (key_x * 2 + key_core) * tok_count + key_row % tok_count
    key_clip_all = clip_of(clip_ends, key_token)

    score_scale = HEAD_DIM ** (-0.5)
    key_block_size = 512 if row_count % 512 == 0 else row_count

    def attend(first_query):
        query_rows = lax.dynamic_slice_in_dim(queries, first_query, half_rows, 0)
        clip_rows = lax.dynamic_slice_in_dim(query_clip, first_query, half_rows, 0)
        numerator = jnp.zeros((half_rows, head_count, HEAD_DIM), jnp.float32)
        denominator = jnp.zeros((head_count, half_rows), jnp.float32)
        for start in range(0, row_count, key_block_size):
            key_slab = key_piece[start:start + key_block_size]
            value_slab = value_piece[start:start + key_block_size]
            key_clip = key_clip_all[start:start + key_block_size]
            scores = (
                jnp.einsum("qhd,khd->hqk", query_rows, key_slab, preferred_element_type=jnp.float32)
                * score_scale
            )
            same_clip = clip_rows[:, None] == key_clip[None, :]
            weights = jnp.where(same_clip[None], jnp.exp(scores), 0.0)
            numerator = numerator + jnp.einsum(
                "hqk,khd->qhd",
                weights.astype(jnp.bfloat16),
                value_slab,
                preferred_element_type=jnp.float32,
            )
            denominator = denominator + jnp.sum(weights, -1)
        return (
            (numerator / jnp.transpose(denominator)[:, :, None])
            .astype(jnp.bfloat16)
            .reshape(half_rows, inner_width)
        )

    sent_att = attend((1 - cfg) * half_rows)
    other_att = lax.ppermute(sent_att, "cfg", SWAP)
    mine_att = attend(cfg * half_rows)
    cond_att = jnp.where(is_cond, mine_att, other_att)
    uncond_att = jnp.where(is_cond, other_att, mine_att)
    out_piece = lax.all_gather(out_projection, ("cfg",) + SEQ, axis=1, tiled=True).reshape(
        inner_width, n_blk, feat_width
    )
    cond_part = jnp.einsum("te,ebn->btn", cond_att, out_piece, preferred_element_type=jnp.float32)
    uncond_part = jnp.einsum("te,ebn->btn", uncond_att, out_piece, preferred_element_type=jnp.float32)
    partial = (uncond_part + scale * (cond_part - uncond_part)).astype(jnp.bfloat16)
    arrived = lax.all_to_all(partial, BLK, 0, 0, tiled=False).astype(jnp.float32)
    gate = lax.dynamic_slice_in_dim(modulation[2], blk * feat_width, feat_width, 0)
    projected = gate * jnp.sum(arrived, 0)
    guided = hidden_part + projected
    return guided.reshape(1, 1, half_rows, feat_width)


def solution(mesh):
    devices = mesh.devices.reshape(2, 4, 2, 2, 4)
    own = Mesh(devices, ("cfg", "x", "core", "zhi", "y"))
    return jax.shard_map(
        local,
        mesh=own,
        in_specs=(
            P("cfg", SEQ, BLK),
            P(),
            P(("cfg",) + SEQ, None, BLK),
            P(BLK, ("cfg",) + SEQ),
            P(),
            P(None, SEQ),
            P(),
        ),
        out_specs=P(SEQ, "cfg", None, BLK),
        check_vma=False,
    )
```

```python
import jax
import jax.numpy as jnp
import numpy as np
from jax import lax
from jax.experimental.layout import Layout, with_layout_constraint
from jax.sharding import Mesh, PartitionSpec as P

HEAD_DIM = 128
SEQ = ("x", "core")
BLK = ("zhi", "y")
SWAP = [(0, 1), (1, 0)]


def rotary_angles(head_width):
    third = head_width // 6
    first_dim = head_width - 4 * third
    other_dim = 2 * third
    pair_index = np.arange(head_width) // 2
    first_pairs = first_dim // 2
    other_pairs = other_dim // 2
    in_first = pair_index < first_pairs
    in_second = (pair_index >= first_pairs) & (pair_index < first_pairs + other_pairs)
    in_third = pair_index >= first_pairs + other_pairs
    row_first = np.where(in_first, 10000.0 ** (-2.0 * pair_index / first_dim), 0.0)
    row_second = np.where(
        in_second, 10000.0 ** (-2.0 * (pair_index - first_pairs) / other_dim), 0.0
    )
    row_third = np.where(
        in_third, 10000.0 ** (-2.0 * (pair_index - first_pairs - other_pairs) / other_dim), 0.0
    )
    return np.stack([row_first, row_second, row_third]).astype(np.float32)


def turn_matrix(head_width):
    row_index = np.arange(head_width)[:, None]
    col_index = np.arange(head_width)[None, :]
    upper = np.where((col_index == row_index + 1) & (row_index % 2 == 0), 1.0, 0.0)
    lower = np.where((col_index == row_index - 1) & (row_index % 2 == 1), -1.0, 0.0)
    return (upper + lower).astype(np.float32)


def layer_norm(inputs):
    row_mean = jnp.mean(inputs, -1, keepdims=True)
    centered = inputs - row_mean
    variance = jnp.mean(centered * centered, -1, keepdims=True)
    return centered * lax.rsqrt(variance + 1e-06)


def rms_norm(inputs):
    return inputs * lax.rsqrt(jnp.mean(inputs * inputs, -1, keepdims=True) + 1e-06)


def rotate(inputs, cosine, sine, turning):
    turned = jnp.einsum("thd,de->the", inputs, turning, precision=lax.Precision.HIGHEST)
    return inputs * cosine + turned * sine


def clip_of(clip_ends, token_index):
    return jnp.sum((token_index[:, None] >= clip_ends[None, :]).astype(jnp.int32), 1)


def local(hidden, modulation, in_projection, out_projection, lengths, positions, guidance):
    cfg = lax.axis_index("cfg")
    core = lax.axis_index("core")
    seq = lax.axis_index("x") * 2 + core
    blk = lax.axis_index("zhi") * lax.axis_size("y") + lax.axis_index("y")
    states = hidden[0]
    tok_count = states.shape[0]
    feat_width = states.shape[1]
    half_rows = tok_count // 2
    n_blk = lax.axis_size(BLK)
    inner_width = in_projection.shape[2]
    head_count = inner_width // HEAD_DIM

    sent_rows = lax.dynamic_slice_in_dim(states, (1 - cfg) * half_rows, half_rows, 0)
    other_rows = lax.ppermute(sent_rows, "cfg", SWAP)
    mine_rows = lax.dynamic_slice_in_dim(states, cfg * half_rows, half_rows, 0)
    is_cond = cfg == 0
    cond_rows = jnp.where(is_cond, mine_rows, other_rows).astype(jnp.float32)
    uncond_rows = jnp.where(is_cond, other_rows, mine_rows).astype(jnp.float32)
    scale = guidance[0]
    hidden_part = uncond_rows + scale * (cond_rows - uncond_rows)

    spread = jnp.broadcast_to(states[None], (n_blk,) + states.shape)
    full_states = lax.all_to_all(spread, BLK, 0, 0, tiled=False)
    full_states, hidden_part = lax.optimization_barrier((full_states, hidden_part))
    inputs = full_states.astype(jnp.float32)
    row_mean = jnp.mean(inputs, (0, 2), keepdims=True)
    centered = inputs - row_mean
    variance = jnp.mean(centered * centered, (0, 2), keepdims=True)
    normed = centered * lax.rsqrt(variance + 1e-06)
    mod_shift = modulation[0].reshape(n_blk, 1, feat_width)
    mod_scale = modulation[1].reshape(n_blk, 1, feat_width)
    modulated = (normed * (1.0 + mod_scale) + mod_shift).astype(jnp.bfloat16)

    shard_other = lax.ppermute(in_projection, "cfg", SWAP)
    stacked = jnp.stack(
        [
            jnp.where(is_cond, in_projection, shard_other),
            jnp.where(is_cond, shard_other, in_projection),
        ]
    )
    piece = lax.all_gather(stacked, SEQ, axis=0, tiled=False)
    n_seq = piece.shape[0]
    rows = in_projection.shape[0]
    per_blk = feat_width // rows
    mod_perm = modulated.reshape(2, n_blk // 2, tok_count, per_blk, rows).transpose(2, 1, 3, 0, 4)
    mod_perm = mod_perm.reshape(tok_count, n_seq, 2, rows)
    mixed = jnp.einsum(
        "tabi,abiqe->tqe",
        mod_perm,
        piece,
        preferred_element_type=jnp.float32,
    )
    mixed = with_layout_constraint(mixed, Layout((0, 1, 2)))
    mixed = mixed.reshape(tok_count, 3, head_count, HEAD_DIM)

    angle_table = jnp.asarray(rotary_angles(HEAD_DIM))
    turning = jnp.asarray(turn_matrix(HEAD_DIM))
    angles = jnp.einsum(
        "at,ae->te", positions.astype(jnp.float32), angle_table, precision=lax.Precision.HIGHEST
    )
    cosine = jnp.cos(angles)[:, None, :]
    sine = jnp.sin(angles)[:, None, :]
    queries = rotate(rms_norm(mixed[:, 0]), cosine, sine, turning).astype(jnp.bfloat16)
    key_rows = rotate(rms_norm(mixed[:, 1]), cosine, sine, turning).astype(jnp.bfloat16)
    value_rows = mixed[:, 2].astype(jnp.bfloat16)

    kv = jnp.stack([key_rows, value_rows], axis=1)
    n_x = lax.axis_size("x")
    x_index = lax.axis_index("x")
    from_behind = lax.ppermute(kv, "x", [(i, (i + 1) % n_x) for i in range(n_x)])
    from_ahead = lax.ppermute(kv, "x", [(i, (i - 1) % n_x) for i in range(n_x)])
    relayed = jnp.where(core == 0, from_behind, from_ahead)
    relay_pairs = [(i * 2, ((i + 1) % n_x) * 2) for i in range(n_x)]
    relay_pairs += [(i * 2 + 1, ((i - 1) % n_x) * 2 + 1) for i in range(n_x)]
    from_far = lax.ppermute(relayed, SEQ, relay_pairs)
    kv_mine = jnp.concatenate([kv, from_behind, from_far, from_ahead], axis=0)
    kv_other = lax.ppermute(kv_mine, "core", SWAP)
    kv_all = jnp.concatenate([kv_mine, kv_other], axis=0)
    key_piece = kv_all[:, 0]
    value_piece = kv_all[:, 1]
    row_count = key_piece.shape[0]

    clip_ends = jnp.cumsum(lengths)
    query_clip = clip_of(clip_ends, seq * tok_count + jnp.arange(tok_count, dtype=jnp.int32))
    key_row = jnp.arange(row_count, dtype=jnp.int32)
    key_block = key_row // tok_count
    key_core = jnp.where(key_block < n_x, core, 1 - core)
    key_x = (x_index - key_block % n_x + n_x) % n_x
    key_token = (key_x * 2 + key_core) * tok_count + key_row % tok_count
    key_clip_all = clip_of(clip_ends, key_token)

    score_scale = HEAD_DIM ** (-0.5)
    key_block_size = 512 if row_count % 512 == 0 else row_count

    def attend(first_query):
        query_rows = lax.dynamic_slice_in_dim(queries, first_query, half_rows, 0)
        clip_rows = lax.dynamic_slice_in_dim(query_clip, first_query, half_rows, 0)
        numerator = jnp.zeros((half_rows, head_count, HEAD_DIM), jnp.float32)
        denominator = jnp.zeros((head_count, half_rows), jnp.float32)
        for start in range(0, row_count, key_block_size):
            key_slab = key_piece[start:start + key_block_size]
            value_slab = value_piece[start:start + key_block_size]
            key_clip = key_clip_all[start:start + key_block_size]
            scores = (
                jnp.einsum("qhd,khd->hqk", query_rows, key_slab, preferred_element_type=jnp.float32)
                * score_scale
            )
            same_clip = clip_rows[:, None] == key_clip[None, :]
            weights = jnp.where(same_clip[None], jnp.exp(scores), 0.0)
            numerator = numerator + jnp.einsum(
                "hqk,khd->qhd",
                weights.astype(jnp.bfloat16),
                value_slab,
                preferred_element_type=jnp.float32,
            )
            denominator = denominator + jnp.sum(weights, -1)
        return (
            (numerator / jnp.transpose(denominator)[:, :, None])
            .astype(jnp.bfloat16)
            .reshape(half_rows, inner_width)
        )

    sent_att = attend((1 - cfg) * half_rows)
    other_att = lax.ppermute(sent_att, "cfg", SWAP)
    mine_att = attend(cfg * half_rows)
    cond_att = jnp.where(is_cond, mine_att, other_att)
    uncond_att = jnp.where(is_cond, other_att, mine_att)
    out_piece = lax.all_gather(out_projection, ("cfg",) + SEQ, axis=1, tiled=True).reshape(
        inner_width, n_blk, feat_width
    )
    cond_part = jnp.einsum("te,ebn->btn", cond_att, out_piece, preferred_element_type=jnp.float32)
    uncond_part = jnp.einsum("te,ebn->btn", uncond_att, out_piece, preferred_element_type=jnp.float32)
    partial = (uncond_part + scale * (cond_part - uncond_part)).reshape(
        2, n_blk // 2, half_rows, feat_width
    )
    zhi = lax.axis_index("zhi")
    own_plane = lax.dynamic_index_in_dim(partial, zhi, axis=0, keepdims=False)
    sent_plane = lax.dynamic_index_in_dim(partial, 1 - zhi, axis=0, keepdims=False).astype(jnp.bfloat16)
    quarter = half_rows // 2
    flip_both = [(0, 3), (3, 0), (1, 2), (2, 1)]
    via_cfg = lax.ppermute(
        lax.ppermute(sent_plane[:, :quarter], "cfg", SWAP), ("cfg", "zhi"), flip_both
    )
    via_diagonal = lax.ppermute(
        lax.ppermute(sent_plane[:, quarter:], ("cfg", "zhi"), flip_both), "cfg", SWAP
    )
    plane_sum = own_plane + jnp.concatenate([via_cfg, via_diagonal], axis=1).astype(jnp.float32)
    arrived = lax.all_to_all(plane_sum.astype(jnp.bfloat16), "y", 0, 0, tiled=False).astype(jnp.float32)
    gate = lax.dynamic_slice_in_dim(modulation[2], blk * feat_width, feat_width, 0)
    projected = gate * jnp.sum(arrived, 0)
    guided = hidden_part + projected
    return guided.reshape(1, 1, half_rows, feat_width)


def solution(mesh):
    devices = mesh.devices.reshape(2, 4, 2, 2, 4)
    own = Mesh(devices, ("cfg", "x", "core", "zhi", "y"))
    return jax.shard_map(
        local,
        mesh=own,
        in_specs=(
            P("cfg", SEQ, BLK),
            P(),
            P(("cfg",) + SEQ, None, BLK),
            P(BLK, ("cfg",) + SEQ),
            P(),
            P(None, SEQ),
            P(),
        ),
        out_specs=P(SEQ, "cfg", None, BLK),
        check_vma=False,
    )
```

```python
import jax
import jax.numpy as jnp
import numpy as np
from jax import lax
from jax.experimental.layout import Layout, with_layout_constraint
from jax.sharding import Mesh, PartitionSpec as P

HEAD_DIM = 128
SEQ = ("x", "core")
BLK = ("zhi", "y")
SWAP = [(0, 1), (1, 0)]


def rotary_angles(head_width):
    third = head_width // 6
    first_dim = head_width - 4 * third
    other_dim = 2 * third
    pair_index = np.arange(head_width) // 2
    first_pairs = first_dim // 2
    other_pairs = other_dim // 2
    in_first = pair_index < first_pairs
    in_second = (pair_index >= first_pairs) & (pair_index < first_pairs + other_pairs)
    in_third = pair_index >= first_pairs + other_pairs
    row_first = np.where(in_first, 10000.0 ** (-2.0 * pair_index / first_dim), 0.0)
    row_second = np.where(
        in_second, 10000.0 ** (-2.0 * (pair_index - first_pairs) / other_dim), 0.0
    )
    row_third = np.where(
        in_third, 10000.0 ** (-2.0 * (pair_index - first_pairs - other_pairs) / other_dim), 0.0
    )
    return np.stack([row_first, row_second, row_third]).astype(np.float32)


def turn_matrix(head_width):
    row_index = np.arange(head_width)[:, None]
    col_index = np.arange(head_width)[None, :]
    upper = np.where((col_index == row_index + 1) & (row_index % 2 == 0), 1.0, 0.0)
    lower = np.where((col_index == row_index - 1) & (row_index % 2 == 1), -1.0, 0.0)
    return (upper + lower).astype(np.float32)


def layer_norm(inputs):
    row_mean = jnp.mean(inputs, -1, keepdims=True)
    centered = inputs - row_mean
    variance = jnp.mean(centered * centered, -1, keepdims=True)
    return centered * lax.rsqrt(variance + 1e-06)


def rms_norm(inputs):
    return inputs * lax.rsqrt(jnp.mean(inputs * inputs, -1, keepdims=True) + 1e-06)


def rotate(inputs, cosine, sine, turning):
    turned = jnp.einsum("thd,de->the", inputs, turning, precision=lax.Precision.HIGHEST)
    return inputs * cosine + turned * sine


def clip_of(clip_ends, token_index):
    return jnp.sum((token_index[:, None] >= clip_ends[None, :]).astype(jnp.int32), 1)


def local(hidden, modulation, in_projection, out_projection, lengths, positions, guidance):
    cfg = lax.axis_index("cfg")
    core = lax.axis_index("core")
    seq = lax.axis_index("x") * 2 + core
    blk = lax.axis_index("zhi") * lax.axis_size("y") + lax.axis_index("y")
    states = hidden[0]
    tok_count = states.shape[0]
    feat_width = states.shape[1]
    half_rows = tok_count // 2
    n_blk = lax.axis_size(BLK)
    inner_width = in_projection.shape[2]
    head_count = inner_width // HEAD_DIM

    sent_rows = lax.dynamic_slice_in_dim(states, (1 - cfg) * half_rows, half_rows, 0)
    other_rows = lax.ppermute(sent_rows, "cfg", SWAP)
    mine_rows = lax.dynamic_slice_in_dim(states, cfg * half_rows, half_rows, 0)
    is_cond = cfg == 0
    cond_rows = jnp.where(is_cond, mine_rows, other_rows).astype(jnp.float32)
    uncond_rows = jnp.where(is_cond, other_rows, mine_rows).astype(jnp.float32)
    scale = guidance[0]
    hidden_part = uncond_rows + scale * (cond_rows - uncond_rows)

    mod_shift = modulation[0].reshape(n_blk, 1, feat_width)
    mod_scale = modulation[1].reshape(n_blk, 1, feat_width)
    pieces = []
    for first in (0, half_rows):
        rows_here = states[first:first + half_rows]
        spread = jnp.broadcast_to(rows_here[None], (n_blk,) + rows_here.shape)
        pieces.append(lax.all_to_all(spread, BLK, 0, 0, tiled=False))
    pieces[1], hidden_part = lax.optimization_barrier((pieces[1], hidden_part))
    normed_pieces = []
    for full_states in pieces:
        inputs = full_states.astype(jnp.float32)
        row_mean = jnp.mean(inputs, (0, 2), keepdims=True)
        centered = inputs - row_mean
        variance = jnp.mean(centered * centered, (0, 2), keepdims=True)
        normed = centered * lax.rsqrt(variance + 1e-06)
        normed_pieces.append((normed * (1.0 + mod_scale) + mod_shift).astype(jnp.bfloat16))
    modulated = jnp.concatenate(normed_pieces, axis=1)

    shard_other = lax.ppermute(in_projection, "cfg", SWAP)
    stacked = jnp.stack(
        [
            jnp.where(is_cond, in_projection, shard_other),
            jnp.where(is_cond, shard_other, in_projection),
        ]
    )
    piece = lax.all_gather(stacked, SEQ, axis=0, tiled=False)
    n_seq = piece.shape[0]
    rows = in_projection.shape[0]
    per_blk = feat_width // rows
    mod_perm = modulated.reshape(2, n_blk // 2, tok_count, per_blk, rows).transpose(2, 1, 3, 0, 4)
    mod_perm = mod_perm.reshape(tok_count, n_seq, 2, rows)
    mixed = jnp.einsum(
        "tabi,abiqe->tqe",
        mod_perm,
        piece,
        preferred_element_type=jnp.float32,
    )
    mixed = with_layout_constraint(mixed, Layout((0, 1, 2)))
    mixed = mixed.reshape(tok_count, 3, head_count, HEAD_DIM)

    angle_table = jnp.asarray(rotary_angles(HEAD_DIM))
    turning = jnp.asarray(turn_matrix(HEAD_DIM))
    angles = jnp.einsum(
        "at,ae->te", positions.astype(jnp.float32), angle_table, precision=lax.Precision.HIGHEST
    )
    cosine = jnp.cos(angles)[:, None, :]
    sine = jnp.sin(angles)[:, None, :]
    queries = rotate(rms_norm(mixed[:, 0]), cosine, sine, turning).astype(jnp.bfloat16)
    key_rows = rotate(rms_norm(mixed[:, 1]), cosine, sine, turning).astype(jnp.bfloat16)
    value_rows = mixed[:, 2].astype(jnp.bfloat16)

    kv = jnp.stack([key_rows, value_rows], axis=1)
    n_x = lax.axis_size("x")
    x_index = lax.axis_index("x")
    from_behind = lax.ppermute(kv, "x", [(i, (i + 1) % n_x) for i in range(n_x)])
    from_ahead = lax.ppermute(kv, "x", [(i, (i - 1) % n_x) for i in range(n_x)])
    relayed = jnp.where(core == 0, from_behind, from_ahead)
    relay_pairs = [(i * 2, ((i + 1) % n_x) * 2) for i in range(n_x)]
    relay_pairs += [(i * 2 + 1, ((i - 1) % n_x) * 2 + 1) for i in range(n_x)]
    from_far = lax.ppermute(relayed, SEQ, relay_pairs)
    kv_mine = jnp.concatenate([kv, from_behind, from_far, from_ahead], axis=0)
    kv_other = lax.ppermute(kv_mine, "core", SWAP)
    kv_all = jnp.concatenate([kv_mine, kv_other], axis=0)
    key_piece = kv_all[:, 0]
    value_piece = kv_all[:, 1]
    row_count = key_piece.shape[0]

    clip_ends = jnp.cumsum(lengths)
    query_clip = clip_of(clip_ends, seq * tok_count + jnp.arange(tok_count, dtype=jnp.int32))
    key_row = jnp.arange(row_count, dtype=jnp.int32)
    key_block = key_row // tok_count
    key_core = jnp.where(key_block < n_x, core, 1 - core)
    key_x = (x_index - key_block % n_x + n_x) % n_x
    key_token = (key_x * 2 + key_core) * tok_count + key_row % tok_count
    key_clip_all = clip_of(clip_ends, key_token)

    score_scale = HEAD_DIM ** (-0.5)
    key_block_size = 512 if row_count % 512 == 0 else row_count

    def attend(first_query):
        query_rows = lax.dynamic_slice_in_dim(queries, first_query, half_rows, 0)
        clip_rows = lax.dynamic_slice_in_dim(query_clip, first_query, half_rows, 0)
        numerator = jnp.zeros((half_rows, head_count, HEAD_DIM), jnp.float32)
        denominator = jnp.zeros((head_count, half_rows), jnp.float32)
        for start in range(0, row_count, key_block_size):
            key_slab = key_piece[start:start + key_block_size]
            value_slab = value_piece[start:start + key_block_size]
            key_clip = key_clip_all[start:start + key_block_size]
            scores = (
                jnp.einsum("qhd,khd->hqk", query_rows, key_slab, preferred_element_type=jnp.float32)
                * score_scale
            )
            same_clip = clip_rows[:, None] == key_clip[None, :]
            weights = jnp.where(same_clip[None], jnp.exp(scores), 0.0)
            numerator = numerator + jnp.einsum(
                "hqk,khd->qhd",
                weights.astype(jnp.bfloat16),
                value_slab,
                preferred_element_type=jnp.float32,
            )
            denominator = denominator + jnp.sum(weights, -1)
        return (
            (numerator / jnp.transpose(denominator)[:, :, None])
            .astype(jnp.bfloat16)
            .reshape(half_rows, inner_width)
        )

    sent_att = attend((1 - cfg) * half_rows)
    other_att = lax.ppermute(sent_att, "cfg", SWAP)
    mine_att = attend(cfg * half_rows)
    cond_att = jnp.where(is_cond, mine_att, other_att)
    uncond_att = jnp.where(is_cond, other_att, mine_att)
    out_piece = lax.all_gather(out_projection, ("cfg",) + SEQ, axis=1, tiled=True).reshape(
        inner_width, n_blk, feat_width
    )
    cond_part = jnp.einsum("te,ebn->btn", cond_att, out_piece, preferred_element_type=jnp.float32)
    uncond_part = jnp.einsum("te,ebn->btn", uncond_att, out_piece, preferred_element_type=jnp.float32)
    partial = (uncond_part + scale * (cond_part - uncond_part)).astype(jnp.bfloat16)
    arrived = lax.all_to_all(partial, BLK, 0, 0, tiled=False).astype(jnp.float32)
    gate = lax.dynamic_slice_in_dim(modulation[2], blk * feat_width, feat_width, 0)
    projected = gate * jnp.sum(arrived, 0)
    guided = hidden_part + projected
    return guided.reshape(1, 1, half_rows, feat_width)


def solution(mesh):
    devices = mesh.devices.reshape(2, 4, 2, 2, 4)
    own = Mesh(devices, ("cfg", "x", "core", "zhi", "y"))
    return jax.shard_map(
        local,
        mesh=own,
        in_specs=(
            P("cfg", SEQ, BLK),
            P(),
            P(("cfg",) + SEQ, None, BLK),
            P(BLK, ("cfg",) + SEQ),
            P(),
            P(None, SEQ),
            P(),
        ),
        out_specs=P(SEQ, "cfg", None, BLK),
        check_vma=False,
    )
```

```python
import jax
import jax.numpy as jnp
import numpy as np
from jax import lax
from jax.experimental.layout import Layout, with_layout_constraint
from jax.sharding import Mesh, PartitionSpec as P

HEAD_DIM = 128
SEQ = ("x", "core")
BLK = ("zhi", "y")
SWAP = [(0, 1), (1, 0)]


def rotary_angles(head_width):
    third = head_width // 6
    first_dim = head_width - 4 * third
    other_dim = 2 * third
    pair_index = np.arange(head_width) // 2
    first_pairs = first_dim // 2
    other_pairs = other_dim // 2
    in_first = pair_index < first_pairs
    in_second = (pair_index >= first_pairs) & (pair_index < first_pairs + other_pairs)
    in_third = pair_index >= first_pairs + other_pairs
    row_first = np.where(in_first, 10000.0 ** (-2.0 * pair_index / first_dim), 0.0)
    row_second = np.where(
        in_second, 10000.0 ** (-2.0 * (pair_index - first_pairs) / other_dim), 0.0
    )
    row_third = np.where(
        in_third, 10000.0 ** (-2.0 * (pair_index - first_pairs - other_pairs) / other_dim), 0.0
    )
    return np.stack([row_first, row_second, row_third]).astype(np.float32)


def turn_matrix(head_width):
    row_index = np.arange(head_width)[:, None]
    col_index = np.arange(head_width)[None, :]
    upper = np.where((col_index == row_index + 1) & (row_index % 2 == 0), 1.0, 0.0)
    lower = np.where((col_index == row_index - 1) & (row_index % 2 == 1), -1.0, 0.0)
    return (upper + lower).astype(np.float32)


def layer_norm(inputs):
    row_mean = jnp.mean(inputs, -1, keepdims=True)
    centered = inputs - row_mean
    variance = jnp.mean(centered * centered, -1, keepdims=True)
    return centered * lax.rsqrt(variance + 1e-06)


def rms_norm(inputs):
    return inputs * lax.rsqrt(jnp.mean(inputs * inputs, -1, keepdims=True) + 1e-06)


def rotate(inputs, cosine, sine, turning):
    turned = jnp.einsum("thd,de->the", inputs, turning, precision=lax.Precision.HIGHEST)
    return inputs * cosine + turned * sine


def clip_of(clip_ends, token_index):
    return jnp.sum((token_index[:, None] >= clip_ends[None, :]).astype(jnp.int32), 1)


def local(hidden, modulation, in_projection, out_projection, lengths, positions, guidance):
    cfg = lax.axis_index("cfg")
    core = lax.axis_index("core")
    seq = lax.axis_index("x") * 2 + core
    blk = lax.axis_index("zhi") * lax.axis_size("y") + lax.axis_index("y")
    states = hidden[0]
    tok_count = states.shape[0]
    feat_width = states.shape[1]
    half_rows = tok_count // 2
    n_blk = lax.axis_size(BLK)
    inner_width = in_projection.shape[2]
    head_count = inner_width // HEAD_DIM

    sent_rows = lax.dynamic_slice_in_dim(states, (1 - cfg) * half_rows, half_rows, 0)
    other_rows = lax.ppermute(sent_rows, "cfg", SWAP)
    mine_rows = lax.dynamic_slice_in_dim(states, cfg * half_rows, half_rows, 0)
    is_cond = cfg == 0
    cond_rows = jnp.where(is_cond, mine_rows, other_rows).astype(jnp.float32)
    uncond_rows = jnp.where(is_cond, other_rows, mine_rows).astype(jnp.float32)
    scale = guidance[0]
    hidden_part = uncond_rows + scale * (cond_rows - uncond_rows)

    spread = jnp.broadcast_to(states[None], (n_blk,) + states.shape)
    full_states = lax.all_to_all(spread, BLK, 0, 0, tiled=False)
    full_states, hidden_part = lax.optimization_barrier((full_states, hidden_part))
    inputs = full_states.astype(jnp.float32)
    row_mean = jnp.mean(inputs, (0, 2), keepdims=True)
    centered = inputs - row_mean
    variance = jnp.mean(centered * centered, (0, 2), keepdims=True)
    normed = centered * lax.rsqrt(variance + 1e-06)
    mod_shift = modulation[0].reshape(n_blk, 1, feat_width)
    mod_scale = modulation[1].reshape(n_blk, 1, feat_width)
    modulated = (normed * (1.0 + mod_scale) + mod_shift).astype(jnp.bfloat16)

    shard_other = lax.ppermute(in_projection, "cfg", SWAP)
    stacked = jnp.stack(
        [
            jnp.where(is_cond, in_projection, shard_other),
            jnp.where(is_cond, shard_other, in_projection),
        ]
    )
    n_x = lax.axis_size("x")
    x_index = lax.axis_index("x")

    def around_x(block):
        from_behind = lax.ppermute(block, "x", [(i, (i + 1) % n_x) for i in range(n_x)])
        from_ahead = lax.ppermute(block, "x", [(i, (i - 1) % n_x) for i in range(n_x)])
        relayed = jnp.where(core == 0, from_behind, from_ahead)
        relay_pairs = [(i * 2, ((i + 1) % n_x) * 2) for i in range(n_x)]
        relay_pairs += [(i * 2 + 1, ((i - 1) % n_x) * 2 + 1) for i in range(n_x)]
        from_far = lax.ppermute(relayed, SEQ, relay_pairs)
        mine = jnp.stack([block, from_behind, from_far, from_ahead])
        return mine, lax.ppermute(mine, "core", SWAP)

    piece = lax.all_gather(stacked[:, :, :2], SEQ, axis=0, tiled=False)
    n_seq = piece.shape[0]
    rows = in_projection.shape[0]
    per_blk = feat_width // rows
    mod_perm = modulated.reshape(2, n_blk // 2, tok_count, per_blk, rows).transpose(2, 1, 3, 0, 4)
    mod_perm = mod_perm.reshape(tok_count, n_seq, 2, rows)
    mixed_qk = jnp.einsum(
        "tabi,abiqe->tqe",
        mod_perm,
        piece,
        preferred_element_type=jnp.float32,
    )
    value_mine, value_other = around_x(stacked[:, :, 2])
    value_piece = jnp.concatenate([value_mine, value_other], axis=0)
    back = jnp.arange(n_x, dtype=jnp.int32)
    source_x = (x_index - back + n_x) % n_x
    order = jnp.concatenate([source_x * 2 + core, source_x * 2 + 1 - core])
    mod_value = jnp.take(mod_perm, order, axis=1)
    mixed_v = jnp.einsum(
        "tabi,abie->te",
        mod_value,
        value_piece,
        preferred_element_type=jnp.float32,
    )
    mixed = jnp.concatenate([mixed_qk, mixed_v[:, None]], axis=1)
    mixed = with_layout_constraint(mixed, Layout((0, 1, 2)))
    mixed = mixed.reshape(tok_count, 3, head_count, HEAD_DIM)

    angle_table = jnp.asarray(rotary_angles(HEAD_DIM))
    turning = jnp.asarray(turn_matrix(HEAD_DIM))
    angles = jnp.einsum(
        "at,ae->te", positions.astype(jnp.float32), angle_table, precision=lax.Precision.HIGHEST
    )
    cosine = jnp.cos(angles)[:, None, :]
    sine = jnp.sin(angles)[:, None, :]
    queries = rotate(rms_norm(mixed[:, 0]), cosine, sine, turning).astype(jnp.bfloat16)
    key_rows = rotate(rms_norm(mixed[:, 1]), cosine, sine, turning).astype(jnp.bfloat16)
    value_rows = mixed[:, 2].astype(jnp.bfloat16)

    kv = jnp.stack([key_rows, value_rows], axis=1)
    kv_mine, kv_other = around_x(kv)
    kv_all = jnp.concatenate(
        [kv_mine.reshape((-1,) + kv.shape[1:]), kv_other.reshape((-1,) + kv.shape[1:])], axis=0
    )
    key_piece = kv_all[:, 0]
    value_piece = kv_all[:, 1]
    row_count = key_piece.shape[0]

    clip_ends = jnp.cumsum(lengths)
    query_clip = clip_of(clip_ends, seq * tok_count + jnp.arange(tok_count, dtype=jnp.int32))
    key_row = jnp.arange(row_count, dtype=jnp.int32)
    key_block = key_row // tok_count
    key_core = jnp.where(key_block < n_x, core, 1 - core)
    key_x = (x_index - key_block % n_x + n_x) % n_x
    key_token = (key_x * 2 + key_core) * tok_count + key_row % tok_count
    key_clip_all = clip_of(clip_ends, key_token)

    score_scale = HEAD_DIM ** (-0.5)
    key_block_size = 512 if row_count % 512 == 0 else row_count

    def attend(first_query):
        query_rows = lax.dynamic_slice_in_dim(queries, first_query, half_rows, 0)
        clip_rows = lax.dynamic_slice_in_dim(query_clip, first_query, half_rows, 0)
        numerator = jnp.zeros((half_rows, head_count, HEAD_DIM), jnp.float32)
        denominator = jnp.zeros((head_count, half_rows), jnp.float32)
        for start in range(0, row_count, key_block_size):
            key_slab = key_piece[start:start + key_block_size]
            value_slab = value_piece[start:start + key_block_size]
            key_clip = key_clip_all[start:start + key_block_size]
            scores = (
                jnp.einsum("qhd,khd->hqk", query_rows, key_slab, preferred_element_type=jnp.float32)
                * score_scale
            )
            same_clip = clip_rows[:, None] == key_clip[None, :]
            weights = jnp.where(same_clip[None], jnp.exp(scores), 0.0)
            numerator = numerator + jnp.einsum(
                "hqk,khd->qhd",
                weights.astype(jnp.bfloat16),
                value_slab,
                preferred_element_type=jnp.float32,
            )
            denominator = denominator + jnp.sum(weights, -1)
        return (
            (numerator / jnp.transpose(denominator)[:, :, None])
            .astype(jnp.bfloat16)
            .reshape(half_rows, inner_width)
        )

    sent_att = attend((1 - cfg) * half_rows)
    other_att = lax.ppermute(sent_att, "cfg", SWAP)
    mine_att = attend(cfg * half_rows)
    cond_att = jnp.where(is_cond, mine_att, other_att)
    uncond_att = jnp.where(is_cond, other_att, mine_att)
    out_piece = lax.all_gather(out_projection, ("cfg",) + SEQ, axis=1, tiled=True).reshape(
        inner_width, n_blk, feat_width
    )
    cond_part = jnp.einsum("te,ebn->btn", cond_att, out_piece, preferred_element_type=jnp.float32)
    uncond_part = jnp.einsum("te,ebn->btn", uncond_att, out_piece, preferred_element_type=jnp.float32)
    partial = (uncond_part + scale * (cond_part - uncond_part)).astype(jnp.bfloat16)
    arrived = lax.all_to_all(partial, BLK, 0, 0, tiled=False).astype(jnp.float32)
    gate = lax.dynamic_slice_in_dim(modulation[2], blk * feat_width, feat_width, 0)
    projected = gate * jnp.sum(arrived, 0)
    guided = hidden_part + projected
    return guided.reshape(1, 1, half_rows, feat_width)


def solution(mesh):
    devices = mesh.devices.reshape(2, 4, 2, 2, 4)
    own = Mesh(devices, ("cfg", "x", "core", "zhi", "y"))
    return jax.shard_map(
        local,
        mesh=own,
        in_specs=(
            P("cfg", SEQ, BLK),
            P(),
            P(("cfg",) + SEQ, None, BLK),
            P(BLK, ("cfg",) + SEQ),
            P(),
            P(None, SEQ),
            P(),
        ),
        out_specs=P(SEQ, "cfg", None, BLK),
        check_vma=False,
    )
```

```python
import jax
import jax.numpy as jnp
import numpy as np
from jax import lax
from jax.experimental.layout import Layout, with_layout_constraint
from jax.sharding import Mesh, PartitionSpec as P

HEAD_DIM = 128
SEQ = ("x", "core")
BLK = ("zhi", "y")
SWAP = [(0, 1), (1, 0)]


def rotary_angles(head_width):
    third = head_width // 6
    first_dim = head_width - 4 * third
    other_dim = 2 * third
    pair_index = np.arange(head_width) // 2
    first_pairs = first_dim // 2
    other_pairs = other_dim // 2
    in_first = pair_index < first_pairs
    in_second = (pair_index >= first_pairs) & (pair_index < first_pairs + other_pairs)
    in_third = pair_index >= first_pairs + other_pairs
    row_first = np.where(in_first, 10000.0 ** (-2.0 * pair_index / first_dim), 0.0)
    row_second = np.where(
        in_second, 10000.0 ** (-2.0 * (pair_index - first_pairs) / other_dim), 0.0
    )
    row_third = np.where(
        in_third, 10000.0 ** (-2.0 * (pair_index - first_pairs - other_pairs) / other_dim), 0.0
    )
    return np.stack([row_first, row_second, row_third]).astype(np.float32)


def turn_matrix(head_width):
    row_index = np.arange(head_width)[:, None]
    col_index = np.arange(head_width)[None, :]
    upper = np.where((col_index == row_index + 1) & (row_index % 2 == 0), 1.0, 0.0)
    lower = np.where((col_index == row_index - 1) & (row_index % 2 == 1), -1.0, 0.0)
    return (upper + lower).astype(np.float32)


def layer_norm(inputs):
    row_mean = jnp.mean(inputs, -1, keepdims=True)
    centered = inputs - row_mean
    variance = jnp.mean(centered * centered, -1, keepdims=True)
    return centered * lax.rsqrt(variance + 1e-06)


def rms_norm(inputs):
    return inputs * lax.rsqrt(jnp.mean(inputs * inputs, -1, keepdims=True) + 1e-06)


def rotate(inputs, cosine, sine, turning):
    turned = jnp.einsum("thd,de->the", inputs, turning, precision=lax.Precision.HIGHEST)
    return inputs * cosine + turned * sine


def clip_of(clip_ends, token_index):
    return jnp.sum((token_index[:, None] >= clip_ends[None, :]).astype(jnp.int32), 1)


def local(hidden, modulation, in_projection, out_projection, lengths, positions, guidance):
    cfg = lax.axis_index("cfg")
    core = lax.axis_index("core")
    seq = lax.axis_index("x") * 2 + core
    blk = lax.axis_index("zhi") * lax.axis_size("y") + lax.axis_index("y")
    states = hidden[0]
    tok_count = states.shape[0]
    feat_width = states.shape[1]
    half_rows = tok_count // 2
    n_blk = lax.axis_size(BLK)
    inner_width = in_projection.shape[2]
    head_count = inner_width // HEAD_DIM

    sent_rows = lax.dynamic_slice_in_dim(states, (1 - cfg) * half_rows, half_rows, 0)
    other_rows = lax.ppermute(sent_rows, "cfg", SWAP)
    mine_rows = lax.dynamic_slice_in_dim(states, cfg * half_rows, half_rows, 0)
    is_cond = cfg == 0
    cond_rows = jnp.where(is_cond, mine_rows, other_rows).astype(jnp.float32)
    uncond_rows = jnp.where(is_cond, other_rows, mine_rows).astype(jnp.float32)
    scale = guidance[0]
    hidden_part = uncond_rows + scale * (cond_rows - uncond_rows)

    spread = jnp.broadcast_to(states[None], (n_blk,) + states.shape)
    full_states = lax.all_to_all(spread, BLK, 0, 0, tiled=False)
    full_states, hidden_part = lax.optimization_barrier((full_states, hidden_part))
    inputs = full_states.astype(jnp.float32)
    row_mean = jnp.mean(inputs, (0, 2), keepdims=True)
    centered = inputs - row_mean
    variance = jnp.mean(centered * centered, (0, 2), keepdims=True)
    normed = centered * lax.rsqrt(variance + 1e-06)
    mod_shift = modulation[0].reshape(n_blk, 1, feat_width)
    mod_scale = modulation[1].reshape(n_blk, 1, feat_width)
    modulated = (normed * (1.0 + mod_scale) + mod_shift).astype(jnp.bfloat16)

    shard_other = lax.ppermute(in_projection, "cfg", SWAP)
    stacked = jnp.stack(
        [
            jnp.where(is_cond, in_projection, shard_other),
            jnp.where(is_cond, shard_other, in_projection),
        ]
    )
    piece = lax.all_gather(stacked, SEQ, axis=0, tiled=False)
    n_seq = piece.shape[0]
    rows = in_projection.shape[0]
    per_blk = feat_width // rows
    mod5 = modulated.reshape(2, n_blk // 2, tok_count, per_blk, rows)
    mixed = jnp.einsum(
        "zythi,yhzin->tn",
        mod5,
        piece.reshape(n_blk // 2, per_blk, 2, rows, 3 * inner_width),
        preferred_element_type=jnp.float32,
    ).reshape(tok_count, 3, inner_width)
    mixed = with_layout_constraint(mixed, Layout((0, 1, 2)))
    mixed = mixed.reshape(tok_count, 3, head_count, HEAD_DIM)

    angle_table = jnp.asarray(rotary_angles(HEAD_DIM))
    turning = jnp.asarray(turn_matrix(HEAD_DIM))
    angles = jnp.einsum(
        "at,ae->te", positions.astype(jnp.float32), angle_table, precision=lax.Precision.HIGHEST
    )
    cosine = jnp.cos(angles)[:, None, :]
    sine = jnp.sin(angles)[:, None, :]
    queries = rotate(rms_norm(mixed[:, 0]), cosine, sine, turning).astype(jnp.bfloat16)
    key_rows = rotate(rms_norm(mixed[:, 1]), cosine, sine, turning).astype(jnp.bfloat16)
    value_rows = mixed[:, 2].astype(jnp.bfloat16)

    kv = jnp.stack([key_rows, value_rows], axis=1)
    n_x = lax.axis_size("x")
    x_index = lax.axis_index("x")
    from_behind = lax.ppermute(kv, "x", [(i, (i + 1) % n_x) for i in range(n_x)])
    from_ahead = lax.ppermute(kv, "x", [(i, (i - 1) % n_x) for i in range(n_x)])
    relayed = jnp.where(core == 0, from_behind, from_ahead)
    relay_pairs = [(i * 2, ((i + 1) % n_x) * 2) for i in range(n_x)]
    relay_pairs += [(i * 2 + 1, ((i - 1) % n_x) * 2 + 1) for i in range(n_x)]
    from_far = lax.ppermute(relayed, SEQ, relay_pairs)
    kv_mine = jnp.concatenate([kv, from_behind, from_far, from_ahead], axis=0)
    kv_other = lax.ppermute(kv_mine, "core", SWAP)
    kv_all = jnp.concatenate([kv_mine, kv_other], axis=0)
    key_piece = kv_all[:, 0]
    value_piece = kv_all[:, 1]
    row_count = key_piece.shape[0]

    clip_ends = jnp.cumsum(lengths)
    query_clip = clip_of(clip_ends, seq * tok_count + jnp.arange(tok_count, dtype=jnp.int32))
    key_row = jnp.arange(row_count, dtype=jnp.int32)
    key_block = key_row // tok_count
    key_core = jnp.where(key_block < n_x, core, 1 - core)
    key_x = (x_index - key_block % n_x + n_x) % n_x
    key_token = (key_x * 2 + key_core) * tok_count + key_row % tok_count
    key_clip_all = clip_of(clip_ends, key_token)

    score_scale = HEAD_DIM ** (-0.5)
    key_block_size = 512 if row_count % 512 == 0 else row_count

    def attend(first_query):
        query_rows = lax.dynamic_slice_in_dim(queries, first_query, half_rows, 0)
        clip_rows = lax.dynamic_slice_in_dim(query_clip, first_query, half_rows, 0)
        numerator = jnp.zeros((half_rows, head_count, HEAD_DIM), jnp.float32)
        denominator = jnp.zeros((head_count, half_rows), jnp.float32)
        for start in range(0, row_count, key_block_size):
            key_slab = key_piece[start:start + key_block_size]
            value_slab = value_piece[start:start + key_block_size]
            key_clip = key_clip_all[start:start + key_block_size]
            scores = (
                jnp.einsum("qhd,khd->hqk", query_rows, key_slab, preferred_element_type=jnp.float32)
                * score_scale
            )
            same_clip = clip_rows[:, None] == key_clip[None, :]
            weights = jnp.where(same_clip[None], jnp.exp(scores), 0.0)
            numerator = numerator + jnp.einsum(
                "hqk,khd->qhd",
                weights.astype(jnp.bfloat16),
                value_slab,
                preferred_element_type=jnp.float32,
            )
            denominator = denominator + jnp.sum(weights, -1)
        return (
            (numerator / jnp.transpose(denominator)[:, :, None])
            .astype(jnp.bfloat16)
            .reshape(half_rows, inner_width)
        )

    sent_att = attend((1 - cfg) * half_rows)
    other_att = lax.ppermute(sent_att, "cfg", SWAP)
    mine_att = attend(cfg * half_rows)
    cond_att = jnp.where(is_cond, mine_att, other_att)
    uncond_att = jnp.where(is_cond, other_att, mine_att)
    out_piece = lax.all_gather(out_projection, ("cfg",) + SEQ, axis=1, tiled=True).reshape(
        inner_width, n_blk, feat_width
    )
    cond_part = jnp.einsum("te,ebn->btn", cond_att, out_piece, preferred_element_type=jnp.float32)
    uncond_part = jnp.einsum("te,ebn->btn", uncond_att, out_piece, preferred_element_type=jnp.float32)
    partial = (uncond_part + scale * (cond_part - uncond_part)).astype(jnp.bfloat16)
    arrived = lax.all_to_all(partial, BLK, 0, 0, tiled=False).astype(jnp.float32)
    gate = lax.dynamic_slice_in_dim(modulation[2], blk * feat_width, feat_width, 0)
    projected = gate * jnp.sum(arrived, 0)
    guided = hidden_part + projected
    return guided.reshape(1, 1, half_rows, feat_width)


def solution(mesh):
    devices = mesh.devices.reshape(2, 4, 2, 2, 4)
    own = Mesh(devices, ("cfg", "x", "core", "zhi", "y"))
    return jax.shard_map(
        local,
        mesh=own,
        in_specs=(
            P("cfg", SEQ, BLK),
            P(),
            P(("cfg",) + SEQ, None, BLK),
            P(BLK, ("cfg",) + SEQ),
            P(),
            P(None, SEQ),
            P(),
        ),
        out_specs=P(SEQ, "cfg", None, BLK),
        check_vma=False,
    )
```

```python
import jax
import jax.numpy as jnp
import numpy as np
from jax import lax
from jax.experimental.layout import Layout, with_layout_constraint
from jax.sharding import Mesh, PartitionSpec as P

HEAD_DIM = 128
SEQ = ("x", "core")
BLK = ("zhi", "y")
SWAP = [(0, 1), (1, 0)]


def rotary_angles(head_width):
    third = head_width // 6
    first_dim = head_width - 4 * third
    other_dim = 2 * third
    pair_index = np.arange(head_width) // 2
    first_pairs = first_dim // 2
    other_pairs = other_dim // 2
    in_first = pair_index < first_pairs
    in_second = (pair_index >= first_pairs) & (pair_index < first_pairs + other_pairs)
    in_third = pair_index >= first_pairs + other_pairs
    row_first = np.where(in_first, 10000.0 ** (-2.0 * pair_index / first_dim), 0.0)
    row_second = np.where(
        in_second, 10000.0 ** (-2.0 * (pair_index - first_pairs) / other_dim), 0.0
    )
    row_third = np.where(
        in_third, 10000.0 ** (-2.0 * (pair_index - first_pairs - other_pairs) / other_dim), 0.0
    )
    return np.stack([row_first, row_second, row_third]).astype(np.float32)


def turn_matrix(head_width):
    row_index = np.arange(head_width)[:, None]
    col_index = np.arange(head_width)[None, :]
    upper = np.where((col_index == row_index + 1) & (row_index % 2 == 0), 1.0, 0.0)
    lower = np.where((col_index == row_index - 1) & (row_index % 2 == 1), -1.0, 0.0)
    return (upper + lower).astype(np.float32)


def layer_norm(inputs):
    row_mean = jnp.mean(inputs, -1, keepdims=True)
    centered = inputs - row_mean
    variance = jnp.mean(centered * centered, -1, keepdims=True)
    return centered * lax.rsqrt(variance + 1e-06)


def rms_norm(inputs):
    return inputs * lax.rsqrt(jnp.mean(inputs * inputs, -1, keepdims=True) + 1e-06)


def rotate(inputs, cosine, sine, turning):
    turned = jnp.einsum("thd,de->the", inputs, turning, precision=lax.Precision.HIGHEST)
    return inputs * cosine + turned * sine


def clip_of(clip_ends, token_index):
    return jnp.sum((token_index[:, None] >= clip_ends[None, :]).astype(jnp.int32), 1)


def local(hidden, modulation, in_projection, out_projection, lengths, positions, guidance):
    cfg = lax.axis_index("cfg")
    core = lax.axis_index("core")
    seq = lax.axis_index("x") * 2 + core
    blk = lax.axis_index("zhi") * lax.axis_size("y") + lax.axis_index("y")
    states = hidden[0]
    tok_count = states.shape[0]
    feat_width = states.shape[1]
    half_rows = tok_count // 2
    n_blk = lax.axis_size(BLK)
    inner_width = in_projection.shape[2]
    head_count = inner_width // HEAD_DIM

    sent_rows = lax.dynamic_slice_in_dim(states, (1 - cfg) * half_rows, half_rows, 0)
    other_rows = lax.ppermute(sent_rows, "cfg", SWAP)
    mine_rows = lax.dynamic_slice_in_dim(states, cfg * half_rows, half_rows, 0)
    is_cond = cfg == 0
    cond_rows = jnp.where(is_cond, mine_rows, other_rows).astype(jnp.float32)
    uncond_rows = jnp.where(is_cond, other_rows, mine_rows).astype(jnp.float32)
    scale = guidance[0]
    hidden_part = uncond_rows + scale * (cond_rows - uncond_rows)

    spread = jnp.broadcast_to(states[None], (n_blk,) + states.shape)
    full_states = lax.all_to_all(spread, BLK, 0, 0, tiled=False)
    full_states, hidden_part = lax.optimization_barrier((full_states, hidden_part))
    inputs = full_states.astype(jnp.float32)
    row_mean = jnp.mean(inputs, (0, 2), keepdims=True)
    centered = inputs - row_mean
    variance = jnp.mean(centered * centered, (0, 2), keepdims=True)
    normed = centered * lax.rsqrt(variance + 1e-06)
    mod_shift = modulation[0].reshape(n_blk, 1, feat_width)
    mod_scale = modulation[1].reshape(n_blk, 1, feat_width)
    modulated = (normed * (1.0 + mod_scale) + mod_shift).astype(jnp.bfloat16)

    shard_other = lax.ppermute(in_projection, "cfg", SWAP)
    stacked = jnp.stack(
        [
            jnp.where(is_cond, in_projection, shard_other),
            jnp.where(is_cond, shard_other, in_projection),
        ]
    )
    n_x = lax.axis_size("x")
    x_index = lax.axis_index("x")

    def around_x(block):
        from_behind = lax.ppermute(block, "x", [(i, (i + 1) % n_x) for i in range(n_x)])
        from_ahead = lax.ppermute(block, "x", [(i, (i - 1) % n_x) for i in range(n_x)])
        relayed = jnp.where(core == 0, from_behind, from_ahead)
        relay_pairs = [(i * 2, ((i + 1) % n_x) * 2) for i in range(n_x)]
        relay_pairs += [(i * 2 + 1, ((i - 1) % n_x) * 2 + 1) for i in range(n_x)]
        from_far = lax.ppermute(relayed, SEQ, relay_pairs)
        mine = jnp.stack([block, from_behind, from_far, from_ahead])
        return mine, lax.ppermute(mine, "core", SWAP)

    w_mine, w_other = around_x(stacked)
    piece = jnp.concatenate([w_mine, w_other], axis=0)
    n_seq = piece.shape[0]
    rows = in_projection.shape[0]
    back = jnp.arange(n_x, dtype=jnp.int32)
    source_x = (x_index - back + n_x) % n_x
    order = jnp.concatenate([source_x * 2 + core, source_x * 2 + 1 - core])
    per_blk = feat_width // rows
    mod_perm = modulated.reshape(2, n_blk // 2, tok_count, per_blk, rows).transpose(2, 1, 3, 0, 4)
    mod_perm = mod_perm.reshape(tok_count, n_seq, 2, rows)
    mod_w = jnp.take(mod_perm, order, axis=1)
    mixed = jnp.einsum(
        "tabi,abiqe->tqe",
        mod_w,
        piece,
        preferred_element_type=jnp.float32,
    )
    mixed = with_layout_constraint(mixed, Layout((0, 1, 2)))
    mixed = mixed.reshape(tok_count, 3, head_count, HEAD_DIM)

    angle_table = jnp.asarray(rotary_angles(HEAD_DIM))
    turning = jnp.asarray(turn_matrix(HEAD_DIM))
    angles = jnp.einsum(
        "at,ae->te", positions.astype(jnp.float32), angle_table, precision=lax.Precision.HIGHEST
    )
    cosine = jnp.cos(angles)[:, None, :]
    sine = jnp.sin(angles)[:, None, :]
    queries = rotate(rms_norm(mixed[:, 0]), cosine, sine, turning).astype(jnp.bfloat16)
    key_rows = rotate(rms_norm(mixed[:, 1]), cosine, sine, turning).astype(jnp.bfloat16)
    value_rows = mixed[:, 2].astype(jnp.bfloat16)

    kv = jnp.stack([key_rows, value_rows], axis=1)
    kv_mine, kv_other = around_x(kv)
    kv_all = jnp.concatenate(
        [kv_mine.reshape((-1,) + kv.shape[1:]), kv_other.reshape((-1,) + kv.shape[1:])], axis=0
    )
    key_piece = kv_all[:, 0]
    value_piece = kv_all[:, 1]
    row_count = key_piece.shape[0]

    clip_ends = jnp.cumsum(lengths)
    query_clip = clip_of(clip_ends, seq * tok_count + jnp.arange(tok_count, dtype=jnp.int32))
    key_row = jnp.arange(row_count, dtype=jnp.int32)
    key_block = key_row // tok_count
    key_core = jnp.where(key_block < n_x, core, 1 - core)
    key_x = (x_index - key_block % n_x + n_x) % n_x
    key_token = (key_x * 2 + key_core) * tok_count + key_row % tok_count
    key_clip_all = clip_of(clip_ends, key_token)

    score_scale = HEAD_DIM ** (-0.5)
    key_block_size = 512 if row_count % 512 == 0 else row_count

    def attend(first_query):
        query_rows = lax.dynamic_slice_in_dim(queries, first_query, half_rows, 0)
        clip_rows = lax.dynamic_slice_in_dim(query_clip, first_query, half_rows, 0)
        numerator = jnp.zeros((half_rows, head_count, HEAD_DIM), jnp.float32)
        denominator = jnp.zeros((head_count, half_rows), jnp.float32)
        for start in range(0, row_count, key_block_size):
            key_slab = key_piece[start:start + key_block_size]
            value_slab = value_piece[start:start + key_block_size]
            key_clip = key_clip_all[start:start + key_block_size]
            scores = (
                jnp.einsum("qhd,khd->hqk", query_rows, key_slab, preferred_element_type=jnp.float32)
                * score_scale
            )
            same_clip = clip_rows[:, None] == key_clip[None, :]
            weights = jnp.where(same_clip[None], jnp.exp(scores), 0.0)
            numerator = numerator + jnp.einsum(
                "hqk,khd->qhd",
                weights.astype(jnp.bfloat16),
                value_slab,
                preferred_element_type=jnp.float32,
            )
            denominator = denominator + jnp.sum(weights, -1)
        return (
            (numerator / jnp.transpose(denominator)[:, :, None])
            .astype(jnp.bfloat16)
            .reshape(half_rows, inner_width)
        )

    sent_att = attend((1 - cfg) * half_rows)
    other_att = lax.ppermute(sent_att, "cfg", SWAP)
    mine_att = attend(cfg * half_rows)
    cond_att = jnp.where(is_cond, mine_att, other_att)
    uncond_att = jnp.where(is_cond, other_att, mine_att)
    out_other = lax.ppermute(out_projection, "cfg", SWAP)
    out_stacked = jnp.stack(
        [jnp.where(is_cond, out_projection, out_other), jnp.where(is_cond, out_other, out_projection)]
    )
    o_mine, o_other = around_x(out_stacked)
    o_all = jnp.concatenate([o_mine, o_other], axis=0)
    seq_ids = jnp.arange(n_seq, dtype=jnp.int32)
    x_of, core_of = seq_ids // 2, seq_ids % 2
    distance = (x_index - x_of + n_x) % n_x
    position = jnp.where(core_of == core, distance, n_x + distance)
    o_sorted = jnp.take(o_all, position, axis=0)
    out_piece = o_sorted.transpose(2, 1, 0, 3).reshape(inner_width, n_blk, feat_width)
    cond_part = jnp.einsum("te,ebn->btn", cond_att, out_piece, preferred_element_type=jnp.float32)
    uncond_part = jnp.einsum("te,ebn->btn", uncond_att, out_piece, preferred_element_type=jnp.float32)
    partial = (uncond_part + scale * (cond_part - uncond_part)).astype(jnp.bfloat16)
    arrived = lax.all_to_all(partial, BLK, 0, 0, tiled=False).astype(jnp.float32)
    gate = lax.dynamic_slice_in_dim(modulation[2], blk * feat_width, feat_width, 0)
    projected = gate * jnp.sum(arrived, 0)
    guided = hidden_part + projected
    return guided.reshape(1, 1, half_rows, feat_width)


def solution(mesh):
    devices = mesh.devices.reshape(2, 4, 2, 2, 4)
    own = Mesh(devices, ("cfg", "x", "core", "zhi", "y"))
    return jax.shard_map(
        local,
        mesh=own,
        in_specs=(
            P("cfg", SEQ, BLK),
            P(),
            P(("cfg",) + SEQ, None, BLK),
            P(BLK, ("cfg",) + SEQ),
            P(),
            P(None, SEQ),
            P(),
        ),
        out_specs=P(SEQ, "cfg", None, BLK),
        check_vma=False,
    )
```

```python
import jax
import jax.numpy as jnp
import numpy as np
from jax import lax
from jax.experimental.layout import Layout, with_layout_constraint
from jax.sharding import Mesh, PartitionSpec as P

HEAD_DIM = 128
SEQ = ("x", "core")
BLK = ("zhi", "y")
SWAP = [(0, 1), (1, 0)]


def rotary_angles(head_width):
    third = head_width // 6
    first_dim = head_width - 4 * third
    other_dim = 2 * third
    pair_index = np.arange(head_width) // 2
    first_pairs = first_dim // 2
    other_pairs = other_dim // 2
    in_first = pair_index < first_pairs
    in_second = (pair_index >= first_pairs) & (pair_index < first_pairs + other_pairs)
    in_third = pair_index >= first_pairs + other_pairs
    row_first = np.where(in_first, 10000.0 ** (-2.0 * pair_index / first_dim), 0.0)
    row_second = np.where(
        in_second, 10000.0 ** (-2.0 * (pair_index - first_pairs) / other_dim), 0.0
    )
    row_third = np.where(
        in_third, 10000.0 ** (-2.0 * (pair_index - first_pairs - other_pairs) / other_dim), 0.0
    )
    return np.stack([row_first, row_second, row_third]).astype(np.float32)


def turn_matrix(head_width):
    row_index = np.arange(head_width)[:, None]
    col_index = np.arange(head_width)[None, :]
    upper = np.where((col_index == row_index + 1) & (row_index % 2 == 0), 1.0, 0.0)
    lower = np.where((col_index == row_index - 1) & (row_index % 2 == 1), -1.0, 0.0)
    return (upper + lower).astype(np.float32)


def layer_norm(inputs):
    row_mean = jnp.mean(inputs, -1, keepdims=True)
    centered = inputs - row_mean
    variance = jnp.mean(centered * centered, -1, keepdims=True)
    return centered * lax.rsqrt(variance + 1e-06)


def rms_norm(inputs):
    return inputs * lax.rsqrt(jnp.mean(inputs * inputs, -1, keepdims=True) + 1e-06)


def rotate(inputs, cosine, sine, turning):
    turned = jnp.einsum("thd,de->the", inputs, turning, precision=lax.Precision.HIGHEST)
    return inputs * cosine + turned * sine


def clip_of(clip_ends, token_index):
    return jnp.sum((token_index[:, None] >= clip_ends[None, :]).astype(jnp.int32), 1)


def local(hidden, modulation, in_projection, out_projection, lengths, positions, guidance):
    cfg = lax.axis_index("cfg")
    core = lax.axis_index("core")
    seq = lax.axis_index("x") * 2 + core
    blk = lax.axis_index("zhi") * lax.axis_size("y") + lax.axis_index("y")
    states = hidden[0]
    tok_count = states.shape[0]
    feat_width = states.shape[1]
    half_rows = tok_count // 2
    n_blk = lax.axis_size(BLK)
    inner_width = in_projection.shape[2]
    head_count = inner_width // HEAD_DIM

    sent_rows = lax.dynamic_slice_in_dim(states, (1 - cfg) * half_rows, half_rows, 0)
    mine_rows = lax.dynamic_slice_in_dim(states, cfg * half_rows, half_rows, 0)
    is_cond = cfg == 0
    scale = guidance[0]

    spread = jnp.broadcast_to(states[None], (n_blk,) + states.shape)
    full_states = lax.all_to_all(spread, BLK, 0, 0, tiled=False)
    inputs = full_states.astype(jnp.float32)
    row_mean = jnp.mean(inputs, (0, 2), keepdims=True)
    centered = inputs - row_mean
    variance = jnp.mean(centered * centered, (0, 2), keepdims=True)
    normed = centered * lax.rsqrt(variance + 1e-06)
    mod_shift = modulation[0].reshape(n_blk, 1, feat_width)
    mod_scale = modulation[1].reshape(n_blk, 1, feat_width)
    modulated = (normed * (1.0 + mod_scale) + mod_shift).astype(jnp.bfloat16)

    shard_other = lax.ppermute(in_projection, "cfg", SWAP)
    stacked = jnp.stack(
        [
            jnp.where(is_cond, in_projection, shard_other),
            jnp.where(is_cond, shard_other, in_projection),
        ]
    )
    piece = lax.all_gather(stacked, SEQ, axis=0, tiled=False)
    n_seq = piece.shape[0]
    rows = in_projection.shape[0]
    per_blk = feat_width // rows
    mod_perm = modulated.reshape(2, n_blk // 2, tok_count, per_blk, rows).transpose(2, 1, 3, 0, 4)
    mod_perm = mod_perm.reshape(tok_count, n_seq, 2, rows)
    mixed = jnp.einsum(
        "tabi,abiqe->tqe",
        mod_perm,
        piece,
        preferred_element_type=jnp.float32,
    )
    mixed = with_layout_constraint(mixed, Layout((0, 1, 2)))
    mixed, sent_rows = lax.optimization_barrier((mixed, sent_rows))
    other_rows = lax.ppermute(sent_rows, "cfg", SWAP)
    cond_rows = jnp.where(is_cond, mine_rows, other_rows).astype(jnp.float32)
    uncond_rows = jnp.where(is_cond, other_rows, mine_rows).astype(jnp.float32)
    hidden_part = uncond_rows + scale * (cond_rows - uncond_rows)
    mixed = mixed.reshape(tok_count, 3, head_count, HEAD_DIM)

    angle_table = jnp.asarray(rotary_angles(HEAD_DIM))
    turning = jnp.asarray(turn_matrix(HEAD_DIM))
    angles = jnp.einsum(
        "at,ae->te", positions.astype(jnp.float32), angle_table, precision=lax.Precision.HIGHEST
    )
    cosine = jnp.cos(angles)[:, None, :]
    sine = jnp.sin(angles)[:, None, :]
    queries = rotate(rms_norm(mixed[:, 0]), cosine, sine, turning).astype(jnp.bfloat16)
    key_rows = rotate(rms_norm(mixed[:, 1]), cosine, sine, turning).astype(jnp.bfloat16)
    value_rows = mixed[:, 2].astype(jnp.bfloat16)

    kv = jnp.stack([key_rows, value_rows], axis=1)
    n_x = lax.axis_size("x")
    x_index = lax.axis_index("x")
    from_behind = lax.ppermute(kv, "x", [(i, (i + 1) % n_x) for i in range(n_x)])
    from_ahead = lax.ppermute(kv, "x", [(i, (i - 1) % n_x) for i in range(n_x)])
    relayed = jnp.where(core == 0, from_behind, from_ahead)
    relay_pairs = [(i * 2, ((i + 1) % n_x) * 2) for i in range(n_x)]
    relay_pairs += [(i * 2 + 1, ((i - 1) % n_x) * 2 + 1) for i in range(n_x)]
    from_far = lax.ppermute(relayed, SEQ, relay_pairs)
    kv_mine = jnp.concatenate([kv, from_behind, from_far, from_ahead], axis=0)
    kv_other = lax.ppermute(kv_mine, "core", SWAP)
    kv_all = jnp.concatenate([kv_mine, kv_other], axis=0)
    kv_all, hidden_part = lax.optimization_barrier((kv_all, hidden_part))
    key_piece = kv_all[:, 0]
    value_piece = kv_all[:, 1]
    row_count = key_piece.shape[0]

    clip_ends = jnp.cumsum(lengths)
    query_clip = clip_of(clip_ends, seq * tok_count + jnp.arange(tok_count, dtype=jnp.int32))
    key_row = jnp.arange(row_count, dtype=jnp.int32)
    key_block = key_row // tok_count
    key_core = jnp.where(key_block < n_x, core, 1 - core)
    key_x = (x_index - key_block % n_x + n_x) % n_x
    key_token = (key_x * 2 + key_core) * tok_count + key_row % tok_count
    key_clip_all = clip_of(clip_ends, key_token)

    score_scale = HEAD_DIM ** (-0.5)
    key_block_size = 512 if row_count % 512 == 0 else row_count

    def attend(first_query):
        query_rows = lax.dynamic_slice_in_dim(queries, first_query, half_rows, 0)
        clip_rows = lax.dynamic_slice_in_dim(query_clip, first_query, half_rows, 0)
        numerator = jnp.zeros((half_rows, head_count, HEAD_DIM), jnp.float32)
        denominator = jnp.zeros((head_count, half_rows), jnp.float32)
        for start in range(0, row_count, key_block_size):
            key_slab = key_piece[start:start + key_block_size]
            value_slab = value_piece[start:start + key_block_size]
            key_clip = key_clip_all[start:start + key_block_size]
            scores = (
                jnp.einsum("qhd,khd->hqk", query_rows, key_slab, preferred_element_type=jnp.float32)
                * score_scale
            )
            same_clip = clip_rows[:, None] == key_clip[None, :]
            weights = jnp.where(same_clip[None], jnp.exp(scores), 0.0)
            numerator = numerator + jnp.einsum(
                "hqk,khd->qhd",
                weights.astype(jnp.bfloat16),
                value_slab,
                preferred_element_type=jnp.float32,
            )
            denominator = denominator + jnp.sum(weights, -1)
        return (
            (numerator / jnp.transpose(denominator)[:, :, None])
            .astype(jnp.bfloat16)
            .reshape(half_rows, inner_width)
        )

    sent_att = attend((1 - cfg) * half_rows)
    other_att = lax.ppermute(sent_att, "cfg", SWAP)
    mine_att = attend(cfg * half_rows)
    cond_att = jnp.where(is_cond, mine_att, other_att)
    uncond_att = jnp.where(is_cond, other_att, mine_att)
    out_piece = lax.all_gather(out_projection, ("cfg",) + SEQ, axis=1, tiled=True).reshape(
        inner_width, n_blk, feat_width
    )
    cond_part = jnp.einsum("te,ebn->btn", cond_att, out_piece, preferred_element_type=jnp.float32)
    uncond_part = jnp.einsum("te,ebn->btn", uncond_att, out_piece, preferred_element_type=jnp.float32)
    partial = (uncond_part + scale * (cond_part - uncond_part)).astype(jnp.bfloat16)
    arrived = lax.all_to_all(partial, BLK, 0, 0, tiled=False).astype(jnp.float32)
    gate = lax.dynamic_slice_in_dim(modulation[2], blk * feat_width, feat_width, 0)
    projected = gate * jnp.sum(arrived, 0)
    guided = hidden_part + projected
    return guided.reshape(1, 1, half_rows, feat_width)


def solution(mesh):
    devices = mesh.devices.reshape(2, 4, 2, 2, 4)
    own = Mesh(devices, ("cfg", "x", "core", "zhi", "y"))
    return jax.shard_map(
        local,
        mesh=own,
        in_specs=(
            P("cfg", SEQ, BLK),
            P(),
            P(("cfg",) + SEQ, None, BLK),
            P(BLK, ("cfg",) + SEQ),
            P(),
            P(None, SEQ),
            P(),
        ),
        out_specs=P(SEQ, "cfg", None, BLK),
        check_vma=False,
    )
```

```python
import jax
import jax.numpy as jnp
import numpy as np
from jax import lax
from jax.experimental.layout import Layout, with_layout_constraint
from jax.sharding import Mesh, PartitionSpec as P

HEAD_DIM = 128
SEQ = ("x", "core")
BLK = ("zhi", "y")
SWAP = [(0, 1), (1, 0)]


def rotary_angles(head_width):
    third = head_width // 6
    first_dim = head_width - 4 * third
    other_dim = 2 * third
    pair_index = np.arange(head_width) // 2
    first_pairs = first_dim // 2
    other_pairs = other_dim // 2
    in_first = pair_index < first_pairs
    in_second = (pair_index >= first_pairs) & (pair_index < first_pairs + other_pairs)
    in_third = pair_index >= first_pairs + other_pairs
    row_first = np.where(in_first, 10000.0 ** (-2.0 * pair_index / first_dim), 0.0)
    row_second = np.where(
        in_second, 10000.0 ** (-2.0 * (pair_index - first_pairs) / other_dim), 0.0
    )
    row_third = np.where(
        in_third, 10000.0 ** (-2.0 * (pair_index - first_pairs - other_pairs) / other_dim), 0.0
    )
    return np.stack([row_first, row_second, row_third]).astype(np.float32)


def turn_matrix(head_width):
    row_index = np.arange(head_width)[:, None]
    col_index = np.arange(head_width)[None, :]
    upper = np.where((col_index == row_index + 1) & (row_index % 2 == 0), 1.0, 0.0)
    lower = np.where((col_index == row_index - 1) & (row_index % 2 == 1), -1.0, 0.0)
    return (upper + lower).astype(np.float32)


def layer_norm(inputs):
    row_mean = jnp.mean(inputs, -1, keepdims=True)
    centered = inputs - row_mean
    variance = jnp.mean(centered * centered, -1, keepdims=True)
    return centered * lax.rsqrt(variance + 1e-06)


def rms_norm(inputs):
    return inputs * lax.rsqrt(jnp.mean(inputs * inputs, -1, keepdims=True) + 1e-06)


def rotate(inputs, cosine, sine, turning):
    turned = jnp.einsum("thd,de->the", inputs, turning, precision=lax.Precision.HIGHEST)
    return inputs * cosine + turned * sine


def clip_of(clip_ends, token_index):
    return jnp.sum((token_index[:, None] >= clip_ends[None, :]).astype(jnp.int32), 1)


def local(hidden, modulation, in_projection, out_projection, lengths, positions, guidance):
    cfg = lax.axis_index("cfg")
    core = lax.axis_index("core")
    seq = lax.axis_index("x") * 2 + core
    blk = lax.axis_index("zhi") * lax.axis_size("y") + lax.axis_index("y")
    states = hidden[0]
    tok_count = states.shape[0]
    feat_width = states.shape[1]
    half_rows = tok_count // 2
    n_blk = lax.axis_size(BLK)
    inner_width = in_projection.shape[2]
    head_count = inner_width // HEAD_DIM

    sent_rows = lax.dynamic_slice_in_dim(states, (1 - cfg) * half_rows, half_rows, 0)
    other_rows = lax.ppermute(sent_rows, "cfg", SWAP)
    mine_rows = lax.dynamic_slice_in_dim(states, cfg * half_rows, half_rows, 0)
    is_cond = cfg == 0
    cond_rows = jnp.where(is_cond, mine_rows, other_rows).astype(jnp.float32)
    uncond_rows = jnp.where(is_cond, other_rows, mine_rows).astype(jnp.float32)
    scale = guidance[0]
    hidden_part = uncond_rows + scale * (cond_rows - uncond_rows)

    spread = jnp.broadcast_to(states[None], (n_blk,) + states.shape)
    full_states = lax.all_to_all(spread, BLK, 0, 0, tiled=False)
    full_states, hidden_part = lax.optimization_barrier((full_states, hidden_part))
    inputs = full_states.astype(jnp.float32)
    block_mean = jnp.mean(inputs, 2, keepdims=True)
    block_dev = inputs - block_mean
    block_m2 = jnp.sum(block_dev * block_dev, 2, keepdims=True)
    row_mean = jnp.mean(block_mean, 0, keepdims=True)
    shift = block_mean - row_mean
    total_m2 = jnp.sum(block_m2, 0, keepdims=True) + feat_width * jnp.sum(shift * shift, 0, keepdims=True)
    variance = total_m2 / (n_blk * feat_width)
    normed = (inputs - row_mean) * lax.rsqrt(variance + 1e-06)
    mod_shift = modulation[0].reshape(n_blk, 1, feat_width)
    mod_scale = modulation[1].reshape(n_blk, 1, feat_width)
    modulated = (normed * (1.0 + mod_scale) + mod_shift).astype(jnp.bfloat16)

    shard_other = lax.ppermute(in_projection, "cfg", SWAP)
    stacked = jnp.stack(
        [
            jnp.where(is_cond, in_projection, shard_other),
            jnp.where(is_cond, shard_other, in_projection),
        ]
    )
    piece = lax.all_gather(stacked, SEQ, axis=0, tiled=False)
    n_seq = piece.shape[0]
    rows = in_projection.shape[0]
    per_blk = feat_width // rows
    mod_perm = modulated.reshape(2, n_blk // 2, tok_count, per_blk, rows).transpose(2, 1, 3, 0, 4)
    mod_perm = mod_perm.reshape(tok_count, n_seq, 2, rows)
    mixed = jnp.einsum(
        "tabi,abiqe->tqe",
        mod_perm,
        piece,
        preferred_element_type=jnp.float32,
    )
    mixed = with_layout_constraint(mixed, Layout((0, 1, 2)))
    mixed = mixed.reshape(tok_count, 3, head_count, HEAD_DIM)

    angle_table = jnp.asarray(rotary_angles(HEAD_DIM))
    turning = jnp.asarray(turn_matrix(HEAD_DIM))
    angles = jnp.einsum(
        "at,ae->te", positions.astype(jnp.float32), angle_table, precision=lax.Precision.HIGHEST
    )
    cosine = jnp.cos(angles)[:, None, :]
    sine = jnp.sin(angles)[:, None, :]
    queries = rotate(rms_norm(mixed[:, 0]), cosine, sine, turning).astype(jnp.bfloat16)
    key_rows = rotate(rms_norm(mixed[:, 1]), cosine, sine, turning).astype(jnp.bfloat16)
    value_rows = mixed[:, 2].astype(jnp.bfloat16)

    kv = jnp.stack([key_rows, value_rows], axis=1)
    n_x = lax.axis_size("x")
    x_index = lax.axis_index("x")
    from_behind = lax.ppermute(kv, "x", [(i, (i + 1) % n_x) for i in range(n_x)])
    from_ahead = lax.ppermute(kv, "x", [(i, (i - 1) % n_x) for i in range(n_x)])
    relayed = jnp.where(core == 0, from_behind, from_ahead)
    relay_pairs = [(i * 2, ((i + 1) % n_x) * 2) for i in range(n_x)]
    relay_pairs += [(i * 2 + 1, ((i - 1) % n_x) * 2 + 1) for i in range(n_x)]
    from_far = lax.ppermute(relayed, SEQ, relay_pairs)
    kv_mine = jnp.concatenate([kv, from_behind, from_far, from_ahead], axis=0)
    kv_other = lax.ppermute(kv_mine, "core", SWAP)
    kv_all = jnp.concatenate([kv_mine, kv_other], axis=0)
    key_piece = kv_all[:, 0]
    value_piece = kv_all[:, 1]
    row_count = key_piece.shape[0]

    clip_ends = jnp.cumsum(lengths)
    query_clip = clip_of(clip_ends, seq * tok_count + jnp.arange(tok_count, dtype=jnp.int32))
    key_row = jnp.arange(row_count, dtype=jnp.int32)
    key_block = key_row // tok_count
    key_core = jnp.where(key_block < n_x, core, 1 - core)
    key_x = (x_index - key_block % n_x + n_x) % n_x
    key_token = (key_x * 2 + key_core) * tok_count + key_row % tok_count
    key_clip_all = clip_of(clip_ends, key_token)

    score_scale = HEAD_DIM ** (-0.5)
    key_block_size = 512 if row_count % 512 == 0 else row_count

    def attend(first_query):
        query_rows = lax.dynamic_slice_in_dim(queries, first_query, half_rows, 0)
        clip_rows = lax.dynamic_slice_in_dim(query_clip, first_query, half_rows, 0)
        numerator = jnp.zeros((half_rows, head_count, HEAD_DIM), jnp.float32)
        denominator = jnp.zeros((head_count, half_rows), jnp.float32)
        for start in range(0, row_count, key_block_size):
            key_slab = key_piece[start:start + key_block_size]
            value_slab = value_piece[start:start + key_block_size]
            key_clip = key_clip_all[start:start + key_block_size]
            scores = (
                jnp.einsum("qhd,khd->hqk", query_rows, key_slab, preferred_element_type=jnp.float32)
                * score_scale
            )
            same_clip = clip_rows[:, None] == key_clip[None, :]
            weights = jnp.where(same_clip[None], jnp.exp(scores), 0.0)
            numerator = numerator + jnp.einsum(
                "hqk,khd->qhd",
                weights.astype(jnp.bfloat16),
                value_slab,
                preferred_element_type=jnp.float32,
            )
            denominator = denominator + jnp.sum(weights, -1)
        return (
            (numerator / jnp.transpose(denominator)[:, :, None])
            .astype(jnp.bfloat16)
            .reshape(half_rows, inner_width)
        )

    sent_att = attend((1 - cfg) * half_rows)
    other_att = lax.ppermute(sent_att, "cfg", SWAP)
    mine_att = attend(cfg * half_rows)
    cond_att = jnp.where(is_cond, mine_att, other_att)
    uncond_att = jnp.where(is_cond, other_att, mine_att)
    out_piece = lax.all_gather(out_projection, ("cfg",) + SEQ, axis=1, tiled=True).reshape(
        inner_width, n_blk, feat_width
    )
    cond_part = jnp.einsum("te,ebn->btn", cond_att, out_piece, preferred_element_type=jnp.float32)
    uncond_part = jnp.einsum("te,ebn->btn", uncond_att, out_piece, preferred_element_type=jnp.float32)
    partial = (uncond_part + scale * (cond_part - uncond_part)).astype(jnp.bfloat16)
    arrived = lax.all_to_all(partial, BLK, 0, 0, tiled=False).astype(jnp.float32)
    gate = lax.dynamic_slice_in_dim(modulation[2], blk * feat_width, feat_width, 0)
    projected = gate * jnp.sum(arrived, 0)
    guided = hidden_part + projected
    return guided.reshape(1, 1, half_rows, feat_width)


def solution(mesh):
    devices = mesh.devices.reshape(2, 4, 2, 2, 4)
    own = Mesh(devices, ("cfg", "x", "core", "zhi", "y"))
    return jax.shard_map(
        local,
        mesh=own,
        in_specs=(
            P("cfg", SEQ, BLK),
            P(),
            P(("cfg",) + SEQ, None, BLK),
            P(BLK, ("cfg",) + SEQ),
            P(),
            P(None, SEQ),
            P(),
        ),
        out_specs=P(SEQ, "cfg", None, BLK),
        check_vma=False,
    )
```

```python
import jax
import jax.numpy as jnp
import numpy as np
from jax import lax
from jax.experimental.layout import Layout, with_layout_constraint
from jax.sharding import Mesh, PartitionSpec as P

HEAD_DIM = 128
SEQ = ("x", "core")
BLK = ("zhi", "y")
SWAP = [(0, 1), (1, 0)]


def rotary_angles(head_width):
    third = head_width // 6
    first_dim = head_width - 4 * third
    other_dim = 2 * third
    pair_index = np.arange(head_width) // 2
    first_pairs = first_dim // 2
    other_pairs = other_dim // 2
    in_first = pair_index < first_pairs
    in_second = (pair_index >= first_pairs) & (pair_index < first_pairs + other_pairs)
    in_third = pair_index >= first_pairs + other_pairs
    row_first = np.where(in_first, 10000.0 ** (-2.0 * pair_index / first_dim), 0.0)
    row_second = np.where(
        in_second, 10000.0 ** (-2.0 * (pair_index - first_pairs) / other_dim), 0.0
    )
    row_third = np.where(
        in_third, 10000.0 ** (-2.0 * (pair_index - first_pairs - other_pairs) / other_dim), 0.0
    )
    return np.stack([row_first, row_second, row_third]).astype(np.float32)


def turn_matrix(head_width):
    row_index = np.arange(head_width)[:, None]
    col_index = np.arange(head_width)[None, :]
    upper = np.where((col_index == row_index + 1) & (row_index % 2 == 0), 1.0, 0.0)
    lower = np.where((col_index == row_index - 1) & (row_index % 2 == 1), -1.0, 0.0)
    return (upper + lower).astype(np.float32)


def layer_norm(inputs):
    row_mean = jnp.mean(inputs, -1, keepdims=True)
    centered = inputs - row_mean
    variance = jnp.mean(centered * centered, -1, keepdims=True)
    return centered * lax.rsqrt(variance + 1e-06)


def rms_norm(inputs):
    return inputs * lax.rsqrt(jnp.mean(inputs * inputs, -1, keepdims=True) + 1e-06)


def rotate(inputs, cosine, sine, turning):
    turned = jnp.einsum("thd,de->the", inputs, turning, precision=lax.Precision.HIGHEST)
    return inputs * cosine + turned * sine


def clip_of(clip_ends, token_index):
    return jnp.sum((token_index[:, None] >= clip_ends[None, :]).astype(jnp.int32), 1)


def local(hidden, modulation, in_projection, out_projection, lengths, positions, guidance):
    cfg = lax.axis_index("cfg")
    core = lax.axis_index("core")
    seq = lax.axis_index("x") * 2 + core
    blk = lax.axis_index("zhi") * lax.axis_size("y") + lax.axis_index("y")
    states = hidden[0]
    tok_count = states.shape[0]
    feat_width = states.shape[1]
    half_rows = tok_count // 2
    n_blk = lax.axis_size(BLK)
    inner_width = in_projection.shape[2]
    head_count = inner_width // HEAD_DIM

    sent_rows = lax.dynamic_slice_in_dim(states, (1 - cfg) * half_rows, half_rows, 0)
    other_rows = lax.ppermute(sent_rows, "cfg", SWAP)
    mine_rows = lax.dynamic_slice_in_dim(states, cfg * half_rows, half_rows, 0)
    is_cond = cfg == 0
    cond_rows = jnp.where(is_cond, mine_rows, other_rows).astype(jnp.float32)
    uncond_rows = jnp.where(is_cond, other_rows, mine_rows).astype(jnp.float32)
    scale = guidance[0]
    hidden_part = uncond_rows + scale * (cond_rows - uncond_rows)

    spread = jnp.broadcast_to(states[None], (n_blk,) + states.shape)
    full_states = lax.all_to_all(spread, BLK, 0, 0, tiled=False)
    full_states, hidden_part = lax.optimization_barrier((full_states, hidden_part))
    inputs = full_states.astype(jnp.float32)
    row_mean = jnp.mean(inputs, (0, 2), keepdims=True)
    centered = inputs - row_mean
    variance = jnp.mean(centered * centered, (0, 2), keepdims=True)
    normed = centered * lax.rsqrt(variance + 1e-06)
    mod_shift = modulation[0].reshape(n_blk, 1, feat_width)
    mod_scale = modulation[1].reshape(n_blk, 1, feat_width)
    modulated = (normed * (1.0 + mod_scale) + mod_shift).astype(jnp.bfloat16)

    shard_other = lax.ppermute(in_projection, "cfg", SWAP)
    stacked = jnp.stack(
        [
            jnp.where(is_cond, in_projection, shard_other),
            jnp.where(is_cond, shard_other, in_projection),
        ]
    )
    piece = lax.all_gather(stacked, SEQ, axis=0, tiled=False)
    n_seq = piece.shape[0]
    rows = in_projection.shape[0]
    per_blk = feat_width // rows
    mod_perm = modulated.reshape(2, n_blk // 2, tok_count, per_blk, rows).transpose(2, 1, 3, 0, 4)
    mod_perm = mod_perm.reshape(tok_count, n_seq, 2, rows)
    mixed = jnp.einsum(
        "tabi,abiqe->tqe",
        mod_perm,
        piece,
        preferred_element_type=jnp.float32,
    )
    mixed = with_layout_constraint(mixed, Layout((0, 1, 2)))
    mixed = mixed.reshape(tok_count, 3, head_count, HEAD_DIM)

    angle_table = jnp.asarray(rotary_angles(HEAD_DIM))
    turning = jnp.asarray(turn_matrix(HEAD_DIM))
    angles = jnp.einsum(
        "at,ae->te", positions.astype(jnp.float32), angle_table, precision=lax.Precision.HIGHEST
    )
    cosine = jnp.cos(angles)[:, None, :]
    sine = jnp.sin(angles)[:, None, :]
    queries = rotate(rms_norm(mixed[:, 0]), cosine, sine, turning).astype(jnp.bfloat16)
    key_rows = rotate(rms_norm(mixed[:, 1]), cosine, sine, turning).astype(jnp.bfloat16)
    value_rows = mixed[:, 2].astype(jnp.bfloat16)

    kv = jnp.stack([key_rows, value_rows], axis=1)
    n_x = lax.axis_size("x")
    x_index = lax.axis_index("x")
    from_behind = lax.ppermute(kv, "x", [(i, (i + 1) % n_x) for i in range(n_x)])
    from_ahead = lax.ppermute(kv, "x", [(i, (i - 1) % n_x) for i in range(n_x)])
    relayed = jnp.where(core == 0, from_behind, from_ahead)
    relay_pairs = [(i * 2, ((i + 1) % n_x) * 2) for i in range(n_x)]
    relay_pairs += [(i * 2 + 1, ((i - 1) % n_x) * 2 + 1) for i in range(n_x)]
    from_far = lax.ppermute(relayed, SEQ, relay_pairs)
    kv_mine = jnp.concatenate([kv, from_behind, from_far, from_ahead], axis=0)
    kv_other = lax.ppermute(kv_mine, "core", SWAP)
    kv_all = jnp.concatenate([kv_mine, kv_other], axis=0)
    key_piece = kv_all[:, 0]
    value_piece = kv_all[:, 1]
    row_count = key_piece.shape[0]

    clip_ends = jnp.cumsum(lengths)
    query_clip = clip_of(clip_ends, seq * tok_count + jnp.arange(tok_count, dtype=jnp.int32))
    key_row = jnp.arange(row_count, dtype=jnp.int32)
    key_block = key_row // tok_count
    key_core = jnp.where(key_block < n_x, core, 1 - core)
    key_x = (x_index - key_block % n_x + n_x) % n_x
    key_token = (key_x * 2 + key_core) * tok_count + key_row % tok_count
    key_clip_all = clip_of(clip_ends, key_token)

    score_scale = HEAD_DIM ** (-0.5)
    key_block_size = 512 if row_count % 512 == 0 else row_count

    def attend(first_query):
        query_rows = lax.dynamic_slice_in_dim(queries, first_query, half_rows, 0)
        clip_rows = lax.dynamic_slice_in_dim(query_clip, first_query, half_rows, 0)
        numerator = jnp.zeros((half_rows, head_count, HEAD_DIM), jnp.float32)
        denominator = jnp.zeros((head_count, half_rows), jnp.float32)
        for start in range(0, row_count, key_block_size):
            key_slab = key_piece[start:start + key_block_size]
            value_slab = value_piece[start:start + key_block_size]
            key_clip = key_clip_all[start:start + key_block_size]
            scores = (
                jnp.einsum("qhd,khd->hqk", query_rows, key_slab, preferred_element_type=jnp.float32)
                * score_scale
            )
            same_clip = clip_rows[:, None] == key_clip[None, :]
            weights = jnp.where(same_clip[None], jnp.exp(scores), 0.0)
            numerator = numerator + jnp.einsum(
                "hqk,khd->qhd",
                weights.astype(jnp.bfloat16),
                value_slab,
                preferred_element_type=jnp.float32,
            )
            denominator = denominator + jnp.sum(weights, -1)
        return (
            (numerator / jnp.transpose(denominator)[:, :, None])
            .astype(jnp.bfloat16)
            .reshape(half_rows, inner_width)
        )

    sent_att = attend((1 - cfg) * half_rows)
    other_att = lax.ppermute(sent_att, "cfg", SWAP)
    mine_att = attend(cfg * half_rows)
    cond_att = jnp.where(is_cond, mine_att, other_att)
    uncond_att = jnp.where(is_cond, other_att, mine_att)
    out_piece = lax.all_gather(out_projection, ("cfg",) + SEQ, axis=1, tiled=True).reshape(
        inner_width, n_blk, feat_width
    )
    both_part = jnp.einsum(
        "cte,ebn->cbtn", jnp.stack([cond_att, uncond_att]), out_piece, preferred_element_type=jnp.float32
    )
    cond_part, uncond_part = both_part[0], both_part[1]
    partial = (uncond_part + scale * (cond_part - uncond_part)).astype(jnp.bfloat16)
    arrived = lax.all_to_all(partial, BLK, 0, 0, tiled=False).astype(jnp.float32)
    gate = lax.dynamic_slice_in_dim(modulation[2], blk * feat_width, feat_width, 0)
    projected = gate * jnp.sum(arrived, 0)
    guided = hidden_part + projected
    return guided.reshape(1, 1, half_rows, feat_width)


def solution(mesh):
    devices = mesh.devices.reshape(2, 4, 2, 2, 4)
    own = Mesh(devices, ("cfg", "x", "core", "zhi", "y"))
    return jax.shard_map(
        local,
        mesh=own,
        in_specs=(
            P("cfg", SEQ, BLK),
            P(),
            P(("cfg",) + SEQ, None, BLK),
            P(BLK, ("cfg",) + SEQ),
            P(),
            P(None, SEQ),
            P(),
        ),
        out_specs=P(SEQ, "cfg", None, BLK),
        check_vma=False,
    )
```

```python
import jax
import jax.numpy as jnp
import numpy as np
from jax import lax
from jax.experimental.layout import Layout, with_layout_constraint
from jax.sharding import Mesh, PartitionSpec as P

HEAD_DIM = 128
SEQ = ("x", "core")
BLK = ("zhi", "y")
SWAP = [(0, 1), (1, 0)]


def rotary_angles(head_width):
    third = head_width // 6
    first_dim = head_width - 4 * third
    other_dim = 2 * third
    pair_index = np.arange(head_width) // 2
    first_pairs = first_dim // 2
    other_pairs = other_dim // 2
    in_first = pair_index < first_pairs
    in_second = (pair_index >= first_pairs) & (pair_index < first_pairs + other_pairs)
    in_third = pair_index >= first_pairs + other_pairs
    row_first = np.where(in_first, 10000.0 ** (-2.0 * pair_index / first_dim), 0.0)
    row_second = np.where(
        in_second, 10000.0 ** (-2.0 * (pair_index - first_pairs) / other_dim), 0.0
    )
    row_third = np.where(
        in_third, 10000.0 ** (-2.0 * (pair_index - first_pairs - other_pairs) / other_dim), 0.0
    )
    return np.stack([row_first, row_second, row_third]).astype(np.float32)


def turn_matrix(head_width):
    row_index = np.arange(head_width)[:, None]
    col_index = np.arange(head_width)[None, :]
    upper = np.where((col_index == row_index + 1) & (row_index % 2 == 0), 1.0, 0.0)
    lower = np.where((col_index == row_index - 1) & (row_index % 2 == 1), -1.0, 0.0)
    return (upper + lower).astype(np.float32)


def layer_norm(inputs):
    row_mean = jnp.mean(inputs, -1, keepdims=True)
    centered = inputs - row_mean
    variance = jnp.mean(centered * centered, -1, keepdims=True)
    return centered * lax.rsqrt(variance + 1e-06)


def rms_norm(inputs):
    return inputs * lax.rsqrt(jnp.mean(inputs * inputs, -1, keepdims=True) + 1e-06)


def rotate(inputs, cosine, sine, turning):
    turned = jnp.einsum("thd,de->the", inputs, turning, precision=lax.Precision.HIGHEST)
    return inputs * cosine + turned * sine


def clip_of(clip_ends, token_index):
    return jnp.sum((token_index[:, None] >= clip_ends[None, :]).astype(jnp.int32), 1)


def local(hidden, modulation, in_projection, out_projection, lengths, positions, guidance):
    cfg = lax.axis_index("cfg")
    core = lax.axis_index("core")
    seq = lax.axis_index("x") * 2 + core
    blk = lax.axis_index("zhi") * lax.axis_size("y") + lax.axis_index("y")
    states = hidden[0]
    tok_count = states.shape[0]
    feat_width = states.shape[1]
    half_rows = tok_count // 2
    n_blk = lax.axis_size(BLK)
    inner_width = in_projection.shape[2]
    head_count = inner_width // HEAD_DIM

    sent_rows = lax.dynamic_slice_in_dim(states, (1 - cfg) * half_rows, half_rows, 0)
    other_rows = lax.ppermute(sent_rows, "cfg", SWAP)
    mine_rows = lax.dynamic_slice_in_dim(states, cfg * half_rows, half_rows, 0)
    is_cond = cfg == 0
    cond_rows = jnp.where(is_cond, mine_rows, other_rows).astype(jnp.float32)
    uncond_rows = jnp.where(is_cond, other_rows, mine_rows).astype(jnp.float32)
    scale = guidance[0]
    hidden_part = uncond_rows + scale * (cond_rows - uncond_rows)

    spread = jnp.broadcast_to(states[None], (n_blk,) + states.shape)
    full_states = lax.all_to_all(spread, BLK, 0, 0, tiled=False)
    full_states, hidden_part = lax.optimization_barrier((full_states, hidden_part))
    inputs = full_states.astype(jnp.float32)
    row_mean = jnp.mean(inputs, (0, 2), keepdims=True)
    centered = inputs - row_mean
    variance = jnp.mean(centered * centered, (0, 2), keepdims=True)
    normed = centered * lax.rsqrt(variance + 1e-06)
    mod_shift = modulation[0].reshape(n_blk, 1, feat_width)
    mod_scale = modulation[1].reshape(n_blk, 1, feat_width)
    modulated = (normed * (1.0 + mod_scale) + mod_shift).astype(jnp.bfloat16)

    shard_other = lax.ppermute(in_projection, "cfg", SWAP)
    stacked = jnp.stack(
        [
            jnp.where(is_cond, in_projection, shard_other),
            jnp.where(is_cond, shard_other, in_projection),
        ]
    )
    piece = lax.all_gather(stacked, SEQ, axis=0, tiled=False)
    n_seq = piece.shape[0]
    rows = in_projection.shape[0]
    per_blk = feat_width // rows
    mod_perm = modulated.reshape(2, n_blk // 2, tok_count, per_blk, rows).transpose(2, 1, 3, 0, 4)
    mod_perm = mod_perm.reshape(tok_count, n_seq, 2, rows)
    mixed = jnp.einsum(
        "tabi,abiqe->tqe",
        mod_perm,
        piece,
        preferred_element_type=jnp.float32,
    )
    mixed = with_layout_constraint(mixed, Layout((0, 1, 2)))
    mixed = mixed.reshape(tok_count, 3, head_count, HEAD_DIM)

    angle_table = jnp.asarray(rotary_angles(HEAD_DIM))
    turning = jnp.asarray(turn_matrix(HEAD_DIM))
    angles = jnp.einsum(
        "at,ae->te", positions.astype(jnp.float32), angle_table, precision=lax.Precision.HIGHEST
    )
    cosine = jnp.cos(angles)[:, None, :]
    sine = jnp.sin(angles)[:, None, :]
    queries = rotate(rms_norm(mixed[:, 0]), cosine, sine, turning).astype(jnp.bfloat16)
    key_rows = rotate(rms_norm(mixed[:, 1]), cosine, sine, turning).astype(jnp.bfloat16)
    value_rows = mixed[:, 2].astype(jnp.bfloat16)

    kv = jnp.stack([key_rows, value_rows], axis=1)
    n_x = lax.axis_size("x")
    x_index = lax.axis_index("x")
    from_behind = lax.ppermute(kv, "x", [(i, (i + 1) % n_x) for i in range(n_x)])
    from_ahead = lax.ppermute(kv, "x", [(i, (i - 1) % n_x) for i in range(n_x)])
    direct = lax.ppermute(kv, SEQ, [(i * 2, ((i + 2) % n_x) * 2) for i in range(n_x)])
    relay = lax.ppermute(from_ahead, SEQ, [(i * 2 + 1, ((i - 1) % n_x) * 2 + 1) for i in range(n_x)])
    from_far = jnp.where(core == 0, direct, relay)
    kv_mine = jnp.concatenate([kv, from_behind, from_far, from_ahead], axis=0)
    kv_other = lax.ppermute(kv_mine, "core", SWAP)
    kv_all = jnp.concatenate([kv_mine, kv_other], axis=0)
    key_piece = kv_all[:, 0]
    value_piece = kv_all[:, 1]
    row_count = key_piece.shape[0]

    clip_ends = jnp.cumsum(lengths)
    query_clip = clip_of(clip_ends, seq * tok_count + jnp.arange(tok_count, dtype=jnp.int32))
    key_row = jnp.arange(row_count, dtype=jnp.int32)
    key_block = key_row // tok_count
    key_core = jnp.where(key_block < n_x, core, 1 - core)
    key_x = (x_index - key_block % n_x + n_x) % n_x
    key_token = (key_x * 2 + key_core) * tok_count + key_row % tok_count
    key_clip_all = clip_of(clip_ends, key_token)

    score_scale = HEAD_DIM ** (-0.5)
    key_block_size = 512 if row_count % 512 == 0 else row_count

    def attend(first_query):
        query_rows = lax.dynamic_slice_in_dim(queries, first_query, half_rows, 0)
        clip_rows = lax.dynamic_slice_in_dim(query_clip, first_query, half_rows, 0)
        numerator = jnp.zeros((half_rows, head_count, HEAD_DIM), jnp.float32)
        denominator = jnp.zeros((head_count, half_rows), jnp.float32)
        for start in range(0, row_count, key_block_size):
            key_slab = key_piece[start:start + key_block_size]
            value_slab = value_piece[start:start + key_block_size]
            key_clip = key_clip_all[start:start + key_block_size]
            scores = (
                jnp.einsum("qhd,khd->hqk", query_rows, key_slab, preferred_element_type=jnp.float32)
                * score_scale
            )
            same_clip = clip_rows[:, None] == key_clip[None, :]
            weights = jnp.where(same_clip[None], jnp.exp(scores), 0.0)
            numerator = numerator + jnp.einsum(
                "hqk,khd->qhd",
                weights.astype(jnp.bfloat16),
                value_slab,
                preferred_element_type=jnp.float32,
            )
            denominator = denominator + jnp.sum(weights, -1)
        return (
            (numerator / jnp.transpose(denominator)[:, :, None])
            .astype(jnp.bfloat16)
            .reshape(half_rows, inner_width)
        )

    sent_att = attend((1 - cfg) * half_rows)
    other_att = lax.ppermute(sent_att, "cfg", SWAP)
    mine_att = attend(cfg * half_rows)
    cond_att = jnp.where(is_cond, mine_att, other_att)
    uncond_att = jnp.where(is_cond, other_att, mine_att)
    out_piece = lax.all_gather(out_projection, ("cfg",) + SEQ, axis=1, tiled=True).reshape(
        inner_width, n_blk, feat_width
    )
    both_part = jnp.einsum(
        "cte,ebn->cbtn", jnp.stack([cond_att, uncond_att]), out_piece, preferred_element_type=jnp.float32
    )
    cond_part, uncond_part = both_part[0], both_part[1]
    partial = (uncond_part + scale * (cond_part - uncond_part)).astype(jnp.bfloat16)
    arrived = lax.all_to_all(partial, BLK, 0, 0, tiled=False).astype(jnp.float32)
    gate = lax.dynamic_slice_in_dim(modulation[2], blk * feat_width, feat_width, 0)
    projected = gate * jnp.sum(arrived, 0)
    guided = hidden_part + projected
    return guided.reshape(1, 1, half_rows, feat_width)


def solution(mesh):
    devices = mesh.devices.reshape(2, 4, 2, 2, 4)
    own = Mesh(devices, ("cfg", "x", "core", "zhi", "y"))
    return jax.shard_map(
        local,
        mesh=own,
        in_specs=(
            P("cfg", SEQ, BLK),
            P(),
            P(("cfg",) + SEQ, None, BLK),
            P(BLK, ("cfg",) + SEQ),
            P(),
            P(None, SEQ),
            P(),
        ),
        out_specs=P(SEQ, "cfg", None, BLK),
        check_vma=False,
    )
```
